32 devices in a mesh: seq: 16 (over z, x, core), batch: 2 (over y).
Axes of the slice: x: 2, y: 2, z: 4, core: 2. Of those that a mesh axis runs over, the one named last changes fastest.
Arguments:
- inputs: bfloat16 [2, 2, 1024, 1024], P(None, 'batch', 'seq'), may hold values from -6 to 6
- cotangent: bfloat16 [2, 2, 1024, 1024], P(None, 'batch', 'seq'), may hold values from -6 to 6
- document_ids: int32 [2, 2, 1024], P(None, 'batch'), may hold values from 0 to 3, never falling along the last dimension, each value on 1 to 512 neighbouring positions
- query_weight: bfloat16 [1024, 1024], P(('seq', 'batch')), may hold values from -0.1875 to 0.1875
- key_weight: bfloat16 [1024, 1024], P(('seq', 'batch')), may hold values from -0.1875 to 0.1875
- value_weight: bfloat16 [1024, 1024], P(('seq', 'batch')), may hold values from -0.1875 to 0.1875
- beta_weight: bfloat16 [1024, 8], P(('seq', 'batch')), may hold values from -0.75 to 0.75
- outgate_weight: bfloat16 [1024, 1024], P(('seq', 'batch')), may hold values from -0.1875 to 0.1875
- output_weight: bfloat16 [1024, 1024], P(('seq', 'batch')), may hold values from -0.375 to 0.375
- gate_weight: bfloat16 [1024, 2816], P(('seq', 'batch')), may hold values from -0.1875 to 0.1875
- up_weight: bfloat16 [1024, 2816], P(('seq', 'batch')), may hold values from -0.1875 to 0.1875
- down_weight: bfloat16 [2816, 1024], P(('seq', 'batch')), may hold values from -0.21875 to 0.21875
- mixer_gain: bfloat16 [1024], P(('seq', 'batch')), may hold values from 0.5 to 1.5
- swiglu_gain: bfloat16 [1024], P(('seq', 'batch')), may hold values from 0.5 to 1.5
- head_gain: bfloat16 [128], replicated, may hold values from 0.5 to 1.5
- conv_weight: bfloat16 [12, 1024], P(None, ('seq', 'batch')), may hold values from -3 to 3
Outputs:
- block_output: bfloat16 [2, 2, 1024, 1024], P(None, 'batch', 'seq')
- input_grad: bfloat16 [2, 2, 1024, 1024], P(None, 'batch', 'seq')
- query_grad: float32 [1024, 1024], P(('seq', 'batch'))
- key_grad: float32 [1024, 1024], P(('seq', 'batch'))
- value_grad: float32 [1024, 1024], P(('seq', 'batch'))
- beta_grad: float32 [1024, 8], P(('seq', 'batch'))
- outgate_grad: float32 [1024, 1024], P(('seq', 'batch'))
- outproj_grad: float32 [1024, 1024], P(('seq', 'batch'))
- gate_grad: float32 [1024, 2816], P(('seq', 'batch'))
- up_grad: float32 [1024, 2816], P(('seq', 'batch'))
- down_grad: float32 [2816, 1024], P(('seq', 'batch'))
- mixer_gain_grad: float32 [1024], P(('seq', 'batch'))
- swiglu_gain_grad: float32 [1024], P(('seq', 'batch'))
- head_gain_grad: float32 [128], replicated
- conv_grad: float32 [12, 1024], P(None, ('seq', 'batch'))
The draws below stay inside these ranges and needn't reach their ends.
Inputs may be any that keep to these rules, and one draw needn't show every extreme that they name: `document_ids`: along each packed row the ids never fall; each id holds 1 to 512 consecutive tokens, and one holds exactly 512.
All inputs are finite; a program needn't handle non-finite values.
Results may differ from the reference program's by a relative error of at most 0.017.
Values may be sent and summed in bfloat16 or wider, within the bound.
No kernel may reach another device: no remote copies, remote signals or barrier semaphores. Data moves between devices by JAX's collectives and lax.ppermute only.
A program may use at most 320 MiB of HBM per device.

```python
import math
import jax
import jax.numpy as jnp
import numpy as np
from jax import lax

D = 1024
HEADS = 8
HEAD = 128
FF = 2816
CONV = 4
BLOCK = 64
MB = 2
SEGS = 4
LEN = 1024
ROWS = 2


def shard_levels(key, shape, cuts, low, largest):
    def one(dim, parts):
        heights = jax.random.uniform(jax.random.fold_in(jax.random.fold_in(key, 6), dim), (parts,), jnp.float32, low / len(cuts), largest / len(cuts))
        return jnp.repeat(jnp.exp(heights), shape[dim] // parts).reshape((-1,) + (1,) * (len(shape) - dim - 1))

    loudness = one(*cuts[0])
    for cut in cuts[1:]:
        loudness = loudness * one(*cut)
    return loudness


def profile(number_of, total, most, slope):
    weights = [(1 << 20) // math.isqrt(grade ** slope) + 1 for grade in range(2, number_of + 1)]
    rest, counts = total - most - (number_of - 1), [1] * (number_of - 1)
    while rest > 0:
        candidates = [i for i in range(number_of - 1) if counts[i] < most]
        pool, remaining = sum([weights[i] for i in candidates]), rest
        for i in candidates:
            extra = min(most - counts[i], max(1, remaining * weights[i] // pool), rest)
            counts[i] = counts[i] + extra
            rest = rest - extra
    return np.array([most] + counts)


def ragged(rng, amount, total, most, skew):
    if amount == 2:
        one = jax.random.randint(rng, (), max(1, total - most), min(most, total - 1) + 1)
        return jnp.stack([one, total - one])
    tallies = jnp.asarray(profile(amount, total, most, skew), jnp.int32)
    twos = (amount - 1) // 2
    donor, taker = tallies[1:1 + 2 * twos:2], tallies[2:2 + 2 * twos:2]
    slack = jnp.minimum(donor - 1, most - taker)
    shifted = jax.random.randint(jax.random.fold_in(rng, 1), (twos,), 0, 1 << 20) % (slack + 1)
    tallies = tallies.at[1:1 + 2 * twos:2].set(donor - shifted).at[2:2 + 2 * twos:2].set(taker + shifted)
    return tallies[jax.random.permutation(jax.random.fold_in(rng, 2), amount)]


def bell_draw(rng, extent, spread, bound, shards=(), dtype=jnp.bfloat16):
    drawn = spread * jax.random.normal(rng, extent, jnp.float32)
    if shards:
        drawn = drawn * shard_levels(rng, extent, shards, -0.22, 0.18)
    return jnp.clip(drawn, -bound, bound).astype(dtype)


def setup_inputs(seed: int = 0) -> dict:
    key_of = jax.random.split(jax.random.key(seed), 17)
    inputs = bell_draw(key_of[0], (MB, ROWS, LEN, D), 1.0, 6.0, ((1, 2), (2, 16)))
    cotangent = bell_draw(key_of[1], (MB, ROWS, LEN, D), 1.0, 6.0, ((1, 2), (2, 16)))
    document_ids = jax.vmap(lambda own: jnp.searchsorted(jnp.cumsum(ragged(own, SEGS, LEN, LEN // 2, 0)), jnp.arange(LEN), side="right"))(jax.random.split(key_of[2], MB * ROWS)).reshape((MB, ROWS, LEN)).astype(jnp.int32)
    query_weight = bell_draw(key_of[3], (D, D), D ** -0.5, 0.1875, ((0, 32),))
    key_weight = bell_draw(key_of[4], (D, D), D ** -0.5, 0.1875, ((0, 32),))
    value_weight = bell_draw(key_of[5], (D, D), D ** -0.5, 0.1875, ((0, 32),))
    beta_weight = bell_draw(key_of[6], (D, HEADS), (D // 16) ** -0.5, 0.75, ((0, 32),))
    outgate_weight = bell_draw(key_of[7], (D, D), D ** -0.5, 0.1875, ((0, 32),))
    output_weight = bell_draw(key_of[8], (D, D), (D // 4) ** -0.5, 0.375, ((0, 32),))
    gate_weight = bell_draw(key_of[9], (D, FF), D ** -0.5, 0.1875, ((0, 32),))
    up_weight = bell_draw(key_of[10], (D, FF), D ** -0.5, 0.1875, ((0, 32),))
    down_weight = bell_draw(key_of[11], (FF, D), (FF // 4) ** -0.5, 0.21875, ((0, 32),))
    mixer_gain = jnp.clip(1.0 + 0.1 * jax.random.normal(key_of[12], (D,), jnp.float32), 0.5, 1.5).astype(jnp.bfloat16)
    swiglu_gain = jnp.clip(1.0 + 0.1 * jax.random.normal(key_of[13], (D,), jnp.float32), 0.5, 1.5).astype(jnp.bfloat16)
    head_gain = jnp.clip(1.0 + 0.1 * jax.random.normal(key_of[14], (HEAD,), jnp.float32), 0.5, 1.5).astype(jnp.bfloat16)
    conv_weight = bell_draw(key_of[15], (3 * CONV, D), 0.5, 3.0, ((1, 32),))
    return dict(inputs=inputs, cotangent=cotangent, document_ids=document_ids, query_weight=query_weight, key_weight=key_weight, value_weight=value_weight, beta_weight=beta_weight, outgate_weight=outgate_weight, output_weight=output_weight, gate_weight=gate_weight, up_weight=up_weight, down_weight=down_weight, mixer_gain=mixer_gain, swiglu_gain=swiglu_gain, head_gain=head_gain, conv_weight=conv_weight)


HIGH = lax.Precision.HIGHEST
EPSILON = 1e-05
UNIT_EPSILON = 1e-06

@jax.custom_vjp
def low(v):
    return lax.optimization_barrier(v.astype(jnp.bfloat16)).astype(jnp.float32)

@jax.custom_vjp
def low_back(v):
    return v

def low_keep(v):
    return (low(v), None)

def low_pass(kept, grad):
    return (grad,)

def back_keep(v):
    return (v, None)

def back_low(kept, grad):
    return (low(grad),)
low.defvjp(low_keep, low_pass)
low_back.defvjp(back_keep, back_low)

def matmul(left, right):
    return jnp.dot(left, right, precision=HIGH)

def rms_norm(values_in, gain_vec):
    return values_in * lax.rsqrt(lax.optimization_barrier(jnp.mean(values_in * values_in, axis=-1, keepdims=True)) + EPSILON) * gain_vec

def unit_norm(values_in):
    return values_in * lax.rsqrt(lax.optimization_barrier(jnp.sum(values_in * values_in, axis=-1, keepdims=True)) + UNIT_EPSILON)

def delta_rule(queries, key_vectors, value_vectors, beta_vals, carried):
    length = queries.shape[0]
    block_count = length // BLOCK

    def to_blocks(array):
        return array.reshape((block_count, BLOCK) + array.shape[1:])

    def token_step(memory, pieces):
        query_row, key_row, value_row, beta_row, keep_row = pieces
        memory = memory * keep_row
        predicted = jnp.einsum('hvk,hk->hv', memory, key_row, precision=HIGH)
        update = beta_row[:, None] * (value_row - predicted)
        memory = memory + jnp.einsum('hv,hk->hvk', update, key_row, precision=HIGH)
        return (memory, jnp.einsum('hvk,hk->hv', memory, query_row, precision=HIGH))

    def block_step(memory, pieces):
        return lax.scan(token_step, memory, pieces)
    initial = jnp.zeros((queries.shape[1], value_vectors.shape[2], key_vectors.shape[2]), jnp.float32)
    _, produced = lax.scan(jax.checkpoint(block_step), initial, (to_blocks(queries), to_blocks(key_vectors), to_blocks(value_vectors), to_blocks(beta_vals), to_blocks(carried)))
    return produced.reshape(value_vectors.shape)

def block_row(row_input, row_ids, weights):
    query_w, key_w, value_w, beta_w, outgate_w, output_w, gate_w, up_w, down_w, mixer_g, swiglu_g, head_g, conv_w = weights
    length = row_input.shape[0]
    normed = low(rms_norm(row_input, mixer_g))
    activations = []
    for channel, proj_w in enumerate((query_w, key_w, value_w)):
        projected = low_back(low(matmul(normed, proj_w)))
        padded = jnp.concatenate([jnp.zeros((CONV - 1, D), jnp.float32), projected], axis=0)
        summed = conv_w[CONV * channel][None, :] * projected
        for offset in range(1, CONV):
            same_doc = jnp.concatenate([jnp.zeros((offset,), jnp.float32), (row_ids[offset:] == row_ids[:-offset]).astype(jnp.float32)])
            window = padded[CONV - 1 - offset:CONV - 1 - offset + length]
            summed = summed + conv_w[CONV * channel + offset][None, :] * window * same_doc[:, None]
        activations.append(jax.nn.silu(summed))
    head_shape = (length, HEADS, HEAD)
    queries = unit_norm(activations[0].reshape(head_shape)) * HEAD ** (-0.5)
    key_vectors = unit_norm(activations[1].reshape(head_shape))
    value_vectors = activations[2].reshape(head_shape)
    beta_vals = jax.nn.sigmoid(matmul(normed, beta_w))
    carried = jnp.concatenate([jnp.zeros((1,), jnp.float32), (row_ids[1:] == row_ids[:-1]).astype(jnp.float32)])
    mixer_out = delta_rule(queries, key_vectors, value_vectors, beta_vals, carried)
    gate_lin = low_back(matmul(normed, outgate_w)).reshape(head_shape)
    heads_out = low((rms_norm(mixer_out, head_g) * jax.nn.silu(gate_lin)).reshape(length, D))
    residual = row_input + low_back(matmul(heads_out, output_w))
    normed_two = low(rms_norm(residual, swiglu_g))
    gate_pre = low_back(matmul(normed_two, gate_w))
    upward = low_back(matmul(normed_two, up_w))
    hidden = low(jax.nn.silu(gate_pre) * upward)
    return residual + low_back(matmul(hidden, down_w))

def reference(inputs, cotangent, document_ids, query_weight, key_weight, value_weight, beta_weight, outgate_weight, output_weight, gate_weight, up_weight, down_weight, mixer_gain, swiglu_gain, head_gain, conv_weight):
    weights = tuple((tensor.astype(jnp.float32) for tensor in (query_weight, key_weight, value_weight, beta_weight, outgate_weight, output_weight, gate_weight, up_weight, down_weight, mixer_gain, swiglu_gain, head_gain, conv_weight)))
    rows_input = inputs.astype(jnp.float32).reshape(-1, LEN, D)
    rows_ids = document_ids.reshape(-1, LEN).astype(jnp.int32)
    rows_grad = cotangent.astype(jnp.float32).reshape(-1, LEN, D)

    def forward(all_input, all_weights):

        def one_row(carry_in, pieces):
            return (carry_in, block_row(pieces[0], pieces[1], all_weights))
        _, produced = lax.scan(jax.checkpoint(one_row), jnp.zeros((), jnp.float32), (all_input, rows_ids))
        return produced
    produced, pullback = jax.vjp(forward, rows_input, weights)
    input_grad, weight_grads = pullback(rows_grad)
    return (produced.reshape(inputs.shape).astype(jnp.bfloat16), input_grad.reshape(inputs.shape).astype(jnp.bfloat16), weight_grads[0], weight_grads[1], weight_grads[2], weight_grads[3], weight_grads[4], weight_grads[5], weight_grads[6], weight_grads[7], weight_grads[8], weight_grads[9], weight_grads[10], weight_grads[11], weight_grads[12])
```

```python
from functools import partial

import jax
import jax.numpy as jnp
from jax import lax
from jax.experimental import pallas as pl
from jax.experimental.pallas import tpu as pltpu
from jax.sharding import PartitionSpec as P

HEADS = 8
HEAD = 128
CONV = 4
EPSILON = 1e-05
UNIT_EPSILON = 1e-06
CHUNK = 128
GROUP = 4
F32 = jnp.float32
BF16 = jnp.bfloat16
NN = (((1,), (0,)), ((), ()))
NT = (((1,), (1,)), ((), ()))
TN = (((0,), (0,)), ((), ()))


def split(value):
    high = value.astype(BF16)
    return (high, (value - high.astype(F32)).astype(BF16))


def mm(left, right, dims):
    def dot(a, b):
        return lax.dot_general(a, b, dims, preferred_element_type=F32)

    return dot(left[0], right[0]) + (dot(left[0], right[1]) + dot(left[1], right[0]))


def block_mask(size, width):
    row = lax.broadcasted_iota(jnp.int32, (size, size), 0)
    col = lax.broadcasted_iota(jnp.int32, (size, size), 1)
    return (row // width) == (col // width)


def tri_masks(size):
    row = lax.broadcasted_iota(jnp.int32, (size, size), 0)
    col = lax.broadcasted_iota(jnp.int32, (size, size), 1)
    return (row > col, row >= col, row == col)


def unit_lower_inverses(mats):
    size = mats[0].shape[0]
    eye = tri_masks(size)[2].astype(F32)
    near = block_mask(size, 8)
    base = [split(jnp.where(near, m, 0.0)) for m in mats]
    square = [split(mm(b, b, NN)) for b in base]
    first = [eye - jnp.where(near, m, 0.0) for m in mats]
    second = [f + mm(split(f), s, NN) for f, s in zip(first, square)]
    fourth = [split(mm(s, s, NN)) for s in square]
    inverse = [f + mm(split(f), s, NN) for f, s in zip(second, fourth)]
    width = 8
    while width < size:
        inside, wider = block_mask(size, width), block_mask(size, 2 * width)
        cut = jnp.logical_and(wider, jnp.logical_not(inside))
        off = [split(jnp.where(cut, m, 0.0)) for m in mats]
        halves = [split(t) for t in inverse]
        step = [split(mm(t, o, NN)) for t, o in zip(halves, off)]
        inverse = [t - mm(s, h, NN) for t, s, h in zip(inverse, step, halves)]
        width *= 2
    return inverse


def mixer_forward(
    y_ref,
    flag_ref,
    idc_ref,
    idr_ref,
    pick_ref,
    tap_ref,
    gain_ref,
    heads_ref,
    p_ref,
    qh_ref,
    k_ref,
    sq_ref,
    sk_ref,
    sv_ref,
    beta_ref,
    t_ref,
    sc_ref,
    map_ref,
    state_ref,
    ps_ref,
    er_ref,
    oh_ref,
    ro_ref,
    v_ref,
    pb_ref,
    w_ref,
    add_ref,
):
    length = y_ref.shape[0]
    count = length // CHUNK
    strict, incl, _ = tri_masks(CHUNK)
    pick = pick_ref[...]
    p_ref[0:8, :] = jnp.zeros((8, 3 * HEAD), F32)
    p_ref[8 : 8 + length, :] = y_ref[:, 0 : 3 * HEAD].astype(BF16).astype(F32)
    for n in range(count):
        r0 = n * CHUNK
        rows = slice(r0, r0 + CHUNK)
        keep = [None] + [flag_ref[rows, j : j + 1] for j in range(CONV - 1)]
        for c in range(3):
            cols = slice(c * HEAD, (c + 1) * HEAD)
            pre = tap_ref[4 * c : 4 * c + 1, :] * p_ref[8 + r0 : 8 + r0 + CHUNK, cols]
            for j in range(1, CONV):
                moved = p_ref[8 + r0 - j : 8 + r0 - j + CHUNK, cols]
                pre = pre + tap_ref[4 * c + j : 4 * c + j + 1, :] * moved * keep[j]
            sig = jax.nn.sigmoid(pre)
            act = pre * sig
            slope = sig * (1.0 + pre * (1.0 - sig))
            if c == 2:
                v_ref[rows, :] = act
                sv_ref[rows, :] = slope
            else:
                scale = lax.rsqrt(jnp.sum(act * act, axis=-1, keepdims=True) + UNIT_EPSILON)
                (qh_ref if c == 0 else k_ref)[rows, :] = act * scale
                (sq_ref if c == 0 else sk_ref)[rows, :] = slope * scale
        logit = jnp.sum(y_ref[rows, 4 * HEAD : 5 * HEAD] * pick, axis=-1, keepdims=True)
        beta_ref[rows, :] = jax.nn.sigmoid(logit)

    def prepare(group, carry):
        spots = [pl.multiple_of((group * GROUP + i) * CHUNK, CHUNK) for i in range(GROUP)]
        rows = [pl.ds(s, CHUNK) for s in spots]
        key = [split(k_ref[r, :]) for r in rows]
        same = [
            idc_ref[r, :] == idr_ref[group * GROUP + i, :, :] for i, r in enumerate(rows)
        ]
        beta = [beta_ref[r, :] for r in rows]
        mats = [
            jnp.where(jnp.logical_and(s, strict), b * mm(k, k, NT), 0.0)
            for s, b, k in zip(same, beta, key)
        ]
        inverse = unit_lower_inverses(mats)
        for i, r in enumerate(rows):
            t_ref[r, :] = inverse[i]
            inv = split(inverse[i])
            pseudo = mm(inv, split(beta[i] * v_ref[r, :]), NN)
            weighed = split(
                mm(inv, split(beta[i] * flag_ref[r, 3:4] * k_ref[r, :]), NN)
            )
            ends = split(flag_ref[r, 4:5] * k_ref[r, :])
            query = split(qh_ref[r, :] * HEAD ** (-0.5))
            sc_ref[r, :] = jnp.where(
                jnp.logical_and(same[i], incl), mm(query, key[i], NT), 0.0
            )
            pb_ref[r, :] = pseudo
            w_ref[r, :] = weighed[0].astype(F32) + weighed[1].astype(F32)
            map_ref[r, :] = mm(weighed, ends, TN)
            add_ref[r, :] = mm(split(pseudo), ends, TN)
        return carry

    lax.fori_loop(0, count // GROUP, prepare, 0)
    state = jnp.zeros((HEAD, HEAD), F32)
    for n in range(count):
        rows = slice(n * CHUNK, (n + 1) * CHUNK)
        state_ref[rows, :] = state
        last = flag_ref[(n + 1) * CHUNK - 1 : (n + 1) * CHUNK, 3:4]
        state = last * state - mm(split(state), split(map_ref[rows, :]), NN) + add_ref[rows, :]

    def produce(group, carry):
        for i in range(GROUP):
            r = pl.ds(pl.multiple_of((group * GROUP + i) * CHUNK, CHUNK), CHUNK)
            same = idc_ref[r, :] == idr_ref[group * GROUP + i, :, :]
            key = split(k_ref[r, :])
            state_i = split(state_ref[r, :])
            flag = flag_ref[r, 3:4]
            pseudo = pb_ref[r, :] - mm(split(w_ref[r, :]), state_i, NT)
            ps_ref[r, :] = pseudo
            halves = split(pseudo)
            gram = jnp.where(jnp.logical_and(same, strict), mm(key, key, NT), 0.0)
            er_ref[r, :] = (
                v_ref[r, :] - flag * mm(key, state_i, NT) - mm(split(gram), halves, NN)
            )
            query = split(qh_ref[r, :] * HEAD ** (-0.5))
            out = flag * mm(query, state_i, NT) + mm(split(sc_ref[r, :]), halves, NN)
            scale = lax.rsqrt(jnp.mean(out * out, axis=-1, keepdims=True) + EPSILON)
            hat = out * scale
            oh_ref[r, :] = hat
            ro_ref[r, :] = scale
            lin = y_ref[r, 3 * HEAD : 4 * HEAD]
            heads_ref[r, :] = (
                hat * gain_ref[...] * (lin * jax.nn.sigmoid(lin))
            ).astype(BF16)
        return carry

    lax.fori_loop(0, count // GROUP, produce, 0)


def mixer_backward(
    dh_ref,
    y_ref,
    flag_ref,
    idc_ref,
    idr_ref,
    pick_ref,
    tap_ref,
    gain_ref,
    p_ref,
    qh_ref,
    k_ref,
    sq_ref,
    sk_ref,
    sv_ref,
    beta_ref,
    t_ref,
    sc_ref,
    map_ref,
    state_ref,
    ps_ref,
    er_ref,
    oh_ref,
    ro_ref,
    dcat_ref,
    tapgrad_ref,
    headgrad_ref,
    do_ref,
    dpre_ref,
    back_ref,
    dstate_ref,
    du_ref,
):
    length = y_ref.shape[0]
    count = length // CHUNK
    strict, incl, _ = tri_masks(CHUNK)
    scale_q = HEAD ** (-0.5)
    headgrad_ref[...] = jnp.zeros(headgrad_ref.shape, F32)

    def first(group, carry):
        for i in range(GROUP):
            r = pl.ds(pl.multiple_of((group * GROUP + i) * CHUNK, CHUNK), CHUNK)
            grad = dh_ref[r, :].astype(F32)
            lin = y_ref[r, 3 * HEAD : 4 * HEAD]
            sig = jax.nn.sigmoid(lin)
            swish = lin * sig
            hat = oh_ref[r, :]
            gain = gain_ref[...]
            both = grad * hat
            headgrad_ref[0:1, :] += jnp.sum(both * swish, axis=0, keepdims=True)
            dcat_ref[r, 3 * HEAD : 4 * HEAD] = (
                both * gain * (sig * (1.0 + lin * (1.0 - sig)))
            ).astype(BF16)
            lead = grad * gain * swish
            grad_out = ro_ref[r, :] * (
                lead - hat * jnp.mean(lead * hat, axis=-1, keepdims=True)
            )
            do_ref[r, :] = grad_out
            flag = flag_ref[r, 3:4]
            direct = mm(split(sc_ref[r, :]), split(grad_out), TN)
            dpre_ref[r, :] = direct
            zed = mm(split(t_ref[r, :]), split(direct), TN)
            back_ref[r, :] = mm(
                split(flag * grad_out), split(qh_ref[r, :] * scale_q), TN
            ) - mm(split(beta_ref[r, :] * flag * zed), split(k_ref[r, :]), TN)
        return carry

    lax.fori_loop(0, count // GROUP, first, 0)
    grad_state = jnp.zeros((HEAD, HEAD), F32)
    for n in reversed(range(count)):
        rows = slice(n * CHUNK, (n + 1) * CHUNK)
        dstate_ref[rows, :] = grad_state
        last = flag_ref[(n + 1) * CHUNK - 1 : (n + 1) * CHUNK, 3:4]
        grad_state = (
            last * grad_state
            - mm(split(grad_state), split(map_ref[rows, :]), NT)
            + back_ref[rows, :]
        )
    du_ref[length : length + 8, :] = jnp.zeros((8, 3 * HEAD), F32)

    def second(group, carry):
        for i in range(GROUP):
            r = pl.ds(pl.multiple_of((group * GROUP + i) * CHUNK, CHUNK), CHUNK)
            same = idc_ref[r, :] == idr_ref[group * GROUP + i, :, :]
            low = jnp.logical_and(same, strict)
            full = jnp.logical_and(same, incl)
            flag = flag_ref[r, 3:4]
            ends = flag_ref[r, 4:5]
            beta = beta_ref[r, :]
            key_f = k_ref[r, :]
            key = split(key_f)
            q_hat = qh_ref[r, :]
            query = split(q_hat * scale_q)
            state_i = split(state_ref[r, :])
            dstate = split(dstate_ref[r, :])
            grad_out = split(do_ref[r, :])
            pseudo = split(ps_ref[r, :])
            dpre = dpre_ref[r, :] + ends * mm(key, dstate, NT)
            zed = mm(split(t_ref[r, :]), split(dpre), TN)
            zeds = split(zed)
            dscore = split(jnp.where(full, mm(grad_out, pseudo, NT), 0.0))
            grad_q = flag * mm(grad_out, state_i, NN) + mm(dscore, key, NN)
            dgram = split(jnp.where(low, -beta * mm(zeds, pseudo, NT), 0.0))
            grad_v = beta * zed
            grad_k = (
                mm(dscore, query, TN)
                + ends * mm(pseudo, dstate, NN)
                + mm(dgram, key, NN)
                + mm(dgram, key, TN)
                - flag * mm(split(grad_v), state_i, NN)
            )
            grad_b = jnp.sum(zed * er_ref[r, :], axis=-1, keepdims=True)
            dz = grad_b * beta * (1.0 - beta)
            dcat_ref[r, 4 * HEAD : 5 * HEAD] = (dz * pick_ref[...]).astype(BF16)
            lead = scale_q * grad_q
            du_ref[r, 0:HEAD] = sq_ref[r, :] * (
                lead - q_hat * jnp.sum(lead * q_hat, axis=-1, keepdims=True)
            )
            du_ref[r, HEAD : 2 * HEAD] = sk_ref[r, :] * (
                grad_k - key_f * jnp.sum(grad_k * key_f, axis=-1, keepdims=True)
            )
            du_ref[r, 2 * HEAD : 3 * HEAD] = sv_ref[r, :] * grad_v
        return carry

    lax.fori_loop(0, count // GROUP, second, 0)
    sums = [[jnp.zeros((1, HEAD), F32) for _ in range(CONV)] for _ in range(3)]
    for n in range(count):
        r0 = n * CHUNK
        rows = slice(r0, r0 + CHUNK)
        for c in range(3):
            cols = slice(c * HEAD, (c + 1) * HEAD)
            here = du_ref[rows, cols]
            grad = tap_ref[4 * c : 4 * c + 1, :] * here
            sums[c][0] += jnp.sum(
                here * p_ref[8 + r0 : 8 + r0 + CHUNK, cols], axis=0, keepdims=True
            )
            for j in range(1, CONV):
                after = slice(r0 + j, r0 + j + CHUNK)
                grad = grad + tap_ref[4 * c + j : 4 * c + j + 1, :] * (
                    du_ref[after, cols] * flag_ref[after, j - 1 : j]
                )
                moved = p_ref[8 + r0 - j : 8 + r0 - j + CHUNK, cols]
                sums[c][j] += jnp.sum(
                    here * flag_ref[rows, j - 1 : j] * moved, axis=0, keepdims=True
                )
            dcat_ref[rows, cols] = grad.astype(BF16)
    tapgrad_ref[...] = jnp.concatenate(
        [sums[c][j] for c in range(3) for j in range(CONV)]
        + [jnp.zeros((4, HEAD), F32)],
        axis=0,
    )


VMEM_SPEC = pl.BlockSpec(memory_space=pltpu.VMEM)


def run_kernel(body, name, operands, out_shapes, scratch, flops):
    return pl.pallas_call(
        body,
        name=name,
        out_shape=[jax.ShapeDtypeStruct(*s) for s in out_shapes],
        in_specs=[VMEM_SPEC] * len(operands),
        out_specs=[VMEM_SPEC] * len(out_shapes),
        scratch_shapes=[pltpu.VMEM(*s) for s in scratch],
        compiler_params=pltpu.CompilerParams(vmem_limit_bytes=56 * 1024 * 1024),
        cost_estimate=pl.CostEstimate(flops=flops, bytes_accessed=1 << 20, transcendentals=0),
    )(*operands)


def silu_slope(values_in):
    sigmoid_vals = jax.nn.sigmoid(values_in)
    return sigmoid_vals * (1.0 + values_in * (1.0 - sigmoid_vals))


def rms_scale(values_in):
    return lax.rsqrt(jnp.mean(values_in * values_in, axis=-1, keepdims=True) + EPSILON)


def rms_back(grad_hat, normal, scaling):
    return scaling * (grad_hat - normal * jnp.mean(grad_hat * normal, axis=-1, keepdims=True))


def on_device(
    inputs,
    cotangent,
    document_ids,
    query_weight,
    key_weight,
    value_weight,
    beta_weight,
    outgate_weight,
    output_weight,
    gate_weight,
    up_weight,
    down_weight,
    mixer_gain,
    swiglu_gain,
    head_gain,
    conv_weight,
):
    micro, _, span, width = inputs.shape
    n_seq, n_batch = lax.axis_size("seq"), lax.axis_size("batch")
    group = n_seq // micro
    chips = group // 2
    half_heads = HEADS // 2
    repeat = chips // half_heads
    length = n_seq * span
    rows_w = query_weight.shape[0]
    rows_f = down_weight.shape[0]
    ff_here = rows_f * micro * 2 * n_batch
    place = lax.axis_index("seq")
    batch = lax.axis_index("batch")
    row = place // group
    chip = (place % group) // 2
    core = place % 2
    head = core * half_heads + chip // repeat
    share = chip % repeat

    def swap(value, axis, mask):
        return lax.ppermute(value, axis, [(i, i ^ mask) for i in range(lax.axis_size(axis))])

    def ordered(bit, mine, other):
        flag = bit == 1
        return (jnp.where(flag, other, mine), jnp.where(flag, mine, other))

    def cross(values, index):
        values, step = list(values), 1
        while step < len(values):
            flag = (index // step) % 2 == 1
            values = [jnp.where(flag, values[j ^ step], values[j]) for j in range(len(values))]
            step *= 2
        return values

    def chip_exchange(blocks):
        mine = cross(blocks, chip)
        got = [mine[0]] + [swap(mine[d], "seq", 2 * d) for d in range(1, chips)]
        return cross(got, chip)

    def chip_sum(blocks):
        mine = cross(blocks, chip)
        total = mine[0].astype(F32)
        for d in range(1, chips):
            total = total + swap(mine[d].astype(BF16), "seq", 2 * d).astype(F32)
        return total

    def gather_batch(value, axis):
        step = 1
        while step < n_batch:
            got = swap(value, "batch", step)
            value = jnp.stack(ordered((batch // step) % 2, value, got), axis=axis)
            step *= 2
        return value

    def scatter_bit(value, axis, bit, mesh_axis, mask):
        low, high = (lax.index_in_dim(value, i, axis, keepdims=False) for i in (0, 1))
        flag = bit == 1
        keep, send = jnp.where(flag, high, low), jnp.where(flag, low, high)
        return keep + swap(send.astype(BF16), mesh_axis, mask).astype(F32)

    def scatter_batch(value, axis):
        step = n_batch // 2
        while step >= 1:
            shape = value.shape
            value = value.reshape(shape[:axis] + (2, shape[axis] // 2) + shape[axis + 1 :])
            value = scatter_bit(value, axis, (batch // step) % 2, "batch", step)
            step //= 2
        return lax.squeeze(value, (axis,))

    both = jnp.stack([inputs[:, 0], cotangent[:, 0]], axis=1)
    flag_row = row == 1
    own = jnp.where(flag_row, both[1], both[0])
    away = jnp.where(flag_row, both[0], both[1])
    slabs = jnp.stack(ordered(row, own, swap(away, "seq", group)), axis=1)
    x_own, cot_own = slabs[0], slabs[1]
    x_half = jnp.stack(chip_exchange([x_own] * chips), axis=1)
    x_all = jnp.stack(ordered(core, x_half, swap(x_half, "seq", 1)), axis=2)
    x_all = x_all.reshape(length, width)
    x_half = x_half.reshape(length // 2, width)
    cot_half = jnp.stack(chip_exchange([cot_own] * chips), axis=1).reshape(length // 2, width)

    small = jnp.concatenate(
        [
            beta_weight,
            mixer_gain[:, None],
            swiglu_gain[:, None],
            jnp.swapaxes(conv_weight, 0, 1),
            jnp.zeros((rows_w, HEAD - HEADS - 2 - 3 * CONV), BF16),
        ],
        axis=1,
    )
    mats = jnp.stack([query_weight, key_weight, value_weight, outgate_weight], axis=1)
    mats = mats.reshape(rows_w, 4, 2, half_heads, HEAD)
    blocks = []
    for j in range(chips):
        block = jnp.swapaxes(mats[:, :, :, j // repeat], 1, 2).reshape(rows_w, 8 * HEAD)
        blocks.append(jnp.concatenate([block, small], axis=1))
    pieces = jnp.stack(chip_exchange(blocks), axis=0)
    pieces = jnp.stack(ordered(row, pieces, swap(pieces, "seq", group)), axis=0)
    pieces = gather_batch(pieces.reshape(micro * chips, rows_w, 9 * HEAD), 1)
    pieces = pieces.reshape(micro * chips, n_batch * rows_w, 9 * HEAD)
    low, high, rest = pieces[..., : 4 * HEAD], pieces[..., 4 * HEAD : 8 * HEAD], pieces[..., 8 * HEAD :]
    flag_core = core == 1
    keep = jnp.concatenate([jnp.where(flag_core, high, low), rest], axis=-1)
    send = jnp.concatenate([jnp.where(flag_core, low, high), rest], axis=-1)
    w_cat = jnp.stack(ordered(core, keep, swap(send, "seq", 1)), axis=1).reshape(width, 5 * HEAD)
    w_small = w_cat[:, 4 * HEAD :]
    mixer_vec = w_small[:, HEADS].astype(F32)[None, :]
    swiglu_vec = w_small[:, HEADS + 1].astype(F32)[None, :]
    taps = lax.dynamic_slice_in_dim(w_small, head * HEAD, HEAD, 0)
    taps = jnp.swapaxes(taps[:, HEADS + 2 : HEADS + 2 + 16], 0, 1).astype(F32)
    gain_vec = head_gain.astype(F32)[None, :]

    wo_full = lax.all_gather(output_weight, ("seq", "batch"), axis=0, tiled=True)
    pair = jnp.stack([gate_weight, up_weight], axis=1).reshape(
        rows_w, 2, micro, chips, 2 * n_batch * rows_f
    )
    blocks = [pair[:, :, :, j].reshape(rows_w, 2 * ff_here) for j in range(chips)]
    pieces = jnp.stack(chip_exchange(blocks), axis=0)
    pieces = jnp.stack(ordered(row, pieces, swap(pieces, "seq", group)), axis=0)
    pieces = gather_batch(pieces.reshape(micro * chips, rows_w, 2 * ff_here), 1)
    pieces = pieces.reshape(micro * chips, n_batch * rows_w, 2 * ff_here)
    w_gu = jnp.stack(ordered(core, pieces, swap(pieces, "seq", 1)), axis=1)
    w_gu = w_gu.reshape(width, 2 * ff_here)
    w_gate, w_up = w_gu[:, :ff_here], w_gu[:, ff_here:]
    pieces = jnp.stack(ordered(row, down_weight, swap(down_weight, "seq", group)), axis=0)
    pieces = gather_batch(pieces, 1).reshape(micro, n_batch * rows_f, width)
    w_down = jnp.stack(ordered(core, pieces, swap(pieces, "seq", 1)), axis=1)
    w_down = w_down.reshape(ff_here, width)

    ids = jnp.where(flag_row, document_ids[1, 0], document_ids[0, 0])
    padded = jnp.concatenate([jnp.full((CONV - 1,), -1, jnp.int32), ids])
    count = length // CHUNK
    by_chunk = ids.reshape(count, CHUNK)
    before = jnp.concatenate([jnp.full((1,), -1, jnp.int32), by_chunk[:-1, -1]])
    columns = [padded[CONV - 1 - j : CONV - 1 - j + length] == ids for j in range(1, CONV)]
    columns.append((by_chunk == before[:, None]).reshape(length))
    columns.append((by_chunk == by_chunk[:, -1:]).reshape(length))
    flags = jnp.stack(columns, axis=1).astype(F32)
    flags = jnp.pad(flags, ((0, 8), (0, 3)))
    pick = (lax.broadcasted_iota(jnp.int32, (1, HEAD), 1) == head).astype(F32)

    x_f = x_all.astype(F32)
    scale_zero = rms_scale(x_f)
    hat_zero = x_f * scale_zero
    normed = (hat_zero * mixer_vec).astype(BF16)
    y = jnp.dot(normed, w_cat, preferred_element_type=F32)
    common = (flags, ids[:, None], by_chunk[:, None, :], pick, taps, gain_vec)
    tall = ((length, HEAD), F32)
    square = ((length, CHUNK), F32)
    states = ((count * HEAD, HEAD), F32)
    thin = ((length, 1), F32)
    heads_here, *saved = run_kernel(
        mixer_forward,
        "mixer_forward",
        (y,) + common,
        [((length, HEAD), BF16), ((length + 8, 3 * HEAD), F32)]
        + [tall] * 5
        + [thin, square, square, states, states, tall, tall, tall, thin],
        [tall, tall, tall, states],
        length * CHUNK * HEAD * 2 * 60,
    )

    parted = heads_here.reshape(micro * chips, 2, span, HEAD)
    keep = jnp.where(flag_core, parted[:, 1], parted[:, 0])
    send = jnp.where(flag_core, parted[:, 0], parted[:, 1])
    duo = jnp.concatenate(ordered(core, keep, swap(send, "seq", 1)), axis=-1)
    duo = duo.reshape(length // 2, 2 * HEAD)
    spread = [duo] + [swap(duo, "seq", 2 * repeat * d) for d in range(1, half_heads)]
    spread = cross(spread, chip // repeat)
    heads_half = jnp.concatenate(
        [s[:, :HEAD] for s in spread] + [s[:, HEAD:] for s in spread], axis=1
    )
    residual = x_half.astype(F32) + jnp.dot(heads_half, wo_full, preferred_element_type=F32)
    scale_one = rms_scale(residual)
    hat_one = residual * scale_one
    normed_two = (hat_one * swiglu_vec).astype(BF16)

    gate_pre = jnp.dot(normed_two, w_gate, preferred_element_type=F32)
    upward = jnp.dot(normed_two, w_up, preferred_element_type=F32)
    gate_act = jax.nn.silu(gate_pre)
    hidden = (gate_act * upward).astype(BF16)
    out_part = jnp.dot(hidden, w_down, preferred_element_type=F32)
    grad_hidden = jnp.einsum("td,fd->tf", cot_half, w_down, preferred_element_type=F32)
    grad_gate_pre = (grad_hidden * upward * silu_slope(gate_pre)).astype(BF16)
    grad_upward = (grad_hidden * gate_act).astype(BF16)
    norm_part = jnp.einsum(
        "tf,df->td", grad_gate_pre, w_gate, preferred_element_type=F32
    ) + jnp.einsum("tf,df->td", grad_upward, w_up, preferred_element_type=F32)
    swiglu_part = jnp.sum(norm_part * hat_one, axis=0)

    def own_tokens(value):
        parts = value.reshape(micro, chips, span, width)
        return lax.dynamic_index_in_dim(parts, chip, 1, keepdims=False)

    def token_sum(value):
        parts = value.astype(BF16).reshape(micro, chips, span, width)
        return chip_sum([parts[:, j] for j in range(chips)])

    norm_own = token_sum(norm_part)
    hat_own, scale_own, res_own = own_tokens(hat_one), None, own_tokens(residual)
    scale_own = rms_scale(res_own)
    grad_resid = cot_own.astype(F32) + rms_back(norm_own * swiglu_vec, hat_own, scale_own)
    grad_branch = grad_resid.astype(BF16)
    grad_heads = jnp.einsum(
        "mte,de->mtd", grad_branch, wo_full, preferred_element_type=F32
    ).astype(BF16)
    parted = grad_heads.reshape(micro, span, 2, half_heads, HEAD)
    got = chip_exchange([parted[:, :, :, j // repeat] for j in range(chips)])
    got = jnp.stack(got, axis=1)
    keep = jnp.where(flag_core, got[:, :, :, 1], got[:, :, :, 0])
    send = jnp.where(flag_core, got[:, :, :, 0], got[:, :, :, 1])
    dheads = jnp.stack(ordered(core, keep, swap(send, "seq", 1)), axis=2)
    dheads = dheads.reshape(length, HEAD)

    dcat, tap_grads, head_part = run_kernel(
        mixer_backward,
        "mixer_backward",
        (dheads, y) + common + tuple(saved),
        [((length, 5 * HEAD), BF16), ((16, HEAD), F32), ((8, HEAD), F32)],
        [tall, tall, states, states, ((length + 8, 3 * HEAD), F32)],
        length * CHUNK * HEAD * 2 * 60,
    )
    counts = share == 0
    if repeat > 1:
        mine = (jnp.arange(length) // (2 * span)) % chips % repeat == share
        dcat = jnp.where(mine[:, None], dcat, jnp.zeros_like(dcat))
        tap_grads = jnp.where(counts, tap_grads, 0.0)
        head_part = jnp.where(counts, head_part, 0.0)

    grad_pair = jnp.concatenate(
        [
            jnp.einsum("td,tf->df", normed_two, grad_gate_pre, preferred_element_type=F32),
            jnp.einsum("td,tf->df", normed_two, grad_upward, preferred_element_type=F32),
        ],
        axis=1,
    )

    def scatter_rows(value, lead):
        rows = value.shape[0] // (micro * lead * 2 * n_batch)
        value = value.reshape(micro * lead, 2, n_batch * rows, value.shape[1])
        value = scatter_bit(value, 1, core, "seq", 1)
        value = value.reshape(micro * lead, n_batch, rows, value.shape[-1])
        value = scatter_batch(value, 1)
        value = value.reshape(micro, lead, rows, value.shape[-1])
        return scatter_bit(value, 0, row, "seq", group)

    down_grad = scatter_rows(
        jnp.einsum("tf,td->fd", hidden, cot_half, preferred_element_type=F32), 1
    )[0]
    pair_rows = scatter_rows(grad_pair, chips).astype(BF16)
    got = chip_exchange([pair_rows[j] for j in range(chips)])
    got = jnp.stack([g.reshape(rows_w, 2, micro, ff_here // micro) for g in got], axis=3)
    got = got.astype(F32).reshape(rows_w, 2, micro * chips * (ff_here // micro))
    gate_grad, up_grad = got[:, 0], got[:, 1]

    branch_half = jnp.stack(chip_exchange([grad_branch] * chips), axis=1)
    duo_here = duo
    if repeat > 1:
        mine = (jnp.arange(length // 2) // span) % chips % repeat == share
        duo_here = jnp.where(mine[:, None], duo, jnp.zeros_like(duo))
    out_rows = jnp.einsum(
        "td,te->de",
        duo_here,
        branch_half.reshape(length // 2, width),
        preferred_element_type=F32,
    )
    step = repeat // 2
    out_rows = out_rows.reshape(micro, HEAD, width)
    while step >= 1:
        shape = out_rows.shape
        out_rows = out_rows.reshape(micro, 2, shape[1] // 2, width)
        out_rows = scatter_bit(out_rows, 1, (share // step) % 2, "seq", 2 * step)
        step //= 2
    outproj_grad = scatter_rows(out_rows.reshape(-1, width), 1)[0]

    norm_part = jnp.einsum("te,de->td", dcat, w_cat, preferred_element_type=F32)
    mixer_part = jnp.sum(norm_part * hat_zero, axis=0)
    parted = norm_part.astype(BF16).reshape(micro * chips, 2, span, width)
    summed = scatter_bit(parted.astype(F32), 1, core, "seq", 1)
    norm_own = token_sum(summed)
    x_here = x_own.astype(F32)
    scale_here = rms_scale(x_here)
    grad_own = (
        grad_resid + rms_back(norm_own * mixer_vec, x_here * scale_here, scale_here)
    ).astype(BF16)
    out_own = (res_own + token_sum(out_part)).astype(BF16)
    pair_own = jnp.stack([out_own, grad_own], axis=1)
    keep = jnp.where(flag_row, pair_own[1], pair_own[0])
    send = jnp.where(flag_row, pair_own[0], pair_own[1])
    final = jnp.stack(ordered(row, keep, swap(send, "seq", group)), axis=0)

    w_grad = jnp.einsum("td,te->de", normed, dcat, preferred_element_type=F32)
    tap_cols = jnp.pad(jnp.swapaxes(tap_grads, 0, 1), ((0, 0), (HEADS + 2, HEAD - HEADS - 18)))
    tap_cols = lax.dynamic_update_slice_in_dim(
        jnp.zeros((width, HEAD), F32), tap_cols, head * HEAD, 0
    )
    lane = lax.broadcasted_iota(jnp.int32, (1, HEAD), 1)
    small_grad = jnp.where(lane < HEADS, w_grad[:, 4 * HEAD :], tap_cols)
    small_grad = small_grad + (lane == HEADS) * mixer_part[:, None]
    small_grad = small_grad + (lane == HEADS + 1) * swiglu_part[:, None]
    w_grad = jnp.concatenate([w_grad[:, : 4 * HEAD], small_grad], axis=1)
    parted = w_grad.reshape(micro * chips, 2, n_batch * rows_w, 5 * HEAD)
    keep = jnp.where(flag_core, parted[:, 1], parted[:, 0])
    send = jnp.where(flag_core, parted[:, 0], parted[:, 1]).astype(BF16)
    got = swap(send, "seq", 1).astype(F32)
    first, second = ordered(core, keep, got)
    value = jnp.concatenate(
        [first[..., : 4 * HEAD], second[..., : 4 * HEAD], first[..., 4 * HEAD :] + second[..., 4 * HEAD :]],
        axis=-1,
    )
    value = value.reshape(micro * chips, n_batch, rows_w, 9 * HEAD)
    value = scatter_batch(value, 1).reshape(micro, chips, rows_w, 9 * HEAD)
    value = scatter_bit(value, 0, row, "seq", group).astype(BF16)
    got = [g.astype(F32) for g in chip_exchange([value[j] for j in range(chips)])]
    small_sum = sum(g[:, 8 * HEAD :] for g in got)
    by_head = [
        sum(got[j * repeat + i] for i in range(repeat))[:, : 8 * HEAD].reshape(rows_w, 2, 4, HEAD)
        for j in range(half_heads)
    ]
    merged = jnp.stack(by_head, axis=2)
    merged = [merged[:, :, :, i].reshape(rows_w, width) for i in range(4)]
    head_sum = lax.psum(head_part[0], ("seq", "batch"))
    return (
        final[:, 0][:, None],
        final[:, 1][:, None],
        merged[0],
        merged[1],
        merged[2],
        small_sum[:, :HEADS],
        merged[3],
        outproj_grad,
        gate_grad,
        up_grad,
        down_grad,
        small_sum[:, HEADS],
        small_sum[:, HEADS + 1],
        head_sum,
        jnp.swapaxes(small_sum[:, HEADS + 2 : HEADS + 2 + 3 * CONV], 0, 1),
    )


def solution(mesh):
    tokens, rows = P(None, "batch", "seq", None), P(("seq", "batch"), None)
    vector = P(("seq", "batch"))
    taps = P(None, ("seq", "batch"))
    return jax.shard_map(
        on_device,
        mesh=mesh,
        in_specs=(tokens, tokens, P(None, "batch", None))
        + (rows,) * 9
        + (vector, vector, P(), taps),
        out_specs=(tokens, tokens) + (rows,) * 9 + (vector, vector, P(), taps),
        check_vma=False,
    )
```

```python
from functools import partial

import jax
import jax.numpy as jnp
from jax import lax
from jax.experimental import pallas as pl
from jax.experimental.pallas import tpu as pltpu
from jax.sharding import Mesh, PartitionSpec as P

HEADS = 8
HEAD = 128
CONV = 4
EPSILON = 1e-05
UNIT_EPSILON = 1e-06
CHUNK = 128
GROUP = 4
COST = 10**6
F32 = jnp.float32
BF16 = jnp.bfloat16
NN = (((1,), (0,)), ((), ()))
NT = (((1,), (1,)), ((), ()))
TN = (((0,), (0,)), ((), ()))


def split(value):
    high = value.astype(BF16)
    return (high, (value - high.astype(F32)).astype(BF16))


def mm(left, right, dims):
    def dot(a, b):
        return lax.dot_general(a, b, dims, preferred_element_type=F32)

    return dot(left[0], right[0]) + (dot(left[0], right[1]) + dot(left[1], right[0]))


def block_mask(size, width):
    row = lax.broadcasted_iota(jnp.int32, (size, size), 0)
    col = lax.broadcasted_iota(jnp.int32, (size, size), 1)
    return (row // width) == (col // width)


def tri_masks(size):
    row = lax.broadcasted_iota(jnp.int32, (size, size), 0)
    col = lax.broadcasted_iota(jnp.int32, (size, size), 1)
    return (row > col, row >= col, row == col)


def unit_lower_inverses(mats):
    size = mats[0].shape[0]
    eye = tri_masks(size)[2].astype(F32)
    near = block_mask(size, 8)
    base = [split(jnp.where(near, m, 0.0)) for m in mats]
    square = [split(mm(b, b, NN)) for b in base]
    first = [eye - jnp.where(near, m, 0.0) for m in mats]
    second = [f + mm(split(f), s, NN) for f, s in zip(first, square)]
    fourth = [split(mm(s, s, NN)) for s in square]
    inverse = [f + mm(split(f), s, NN) for f, s in zip(second, fourth)]
    width = 8
    while width < size:
        inside, wider = block_mask(size, width), block_mask(size, 2 * width)
        cut = jnp.logical_and(wider, jnp.logical_not(inside))
        off = [split(jnp.where(cut, m, 0.0)) for m in mats]
        halves = [split(t) for t in inverse]
        step = [split(mm(t, o, NN)) for t, o in zip(halves, off)]
        inverse = [t - mm(s, h, NN) for t, s, h in zip(inverse, step, halves)]
        width *= 2
    return inverse


def place_of(pos_ref):
    return (pos_ref[0], pos_ref[1], pos_ref[2], pos_ref[3])


def head_of(pos_ref, chips):
    return pos_ref[2] * (HEADS // 2) + pos_ref[1] // (chips // (HEADS // 2))


def pack_heads(pos_ref, wq_ref, wk_ref, wv_ref, wg_ref, small_ref, *out_refs):
    chips = len(out_refs)
    repeat = chips // (HEADS // 2)
    for d, out_ref in enumerate(out_refs):
        slot = (pos_ref[1] ^ d) // repeat
        for i in range(2):
            cols = pl.ds(pl.multiple_of((i * (HEADS // 2) + slot) * HEAD, HEAD), HEAD)
            for t, w_ref in enumerate((wq_ref, wk_ref, wv_ref, wg_ref)):
                spot = (4 * i + t) * HEAD
                out_ref[:, spot : spot + HEAD] = w_ref[:, cols]
        out_ref[:, 8 * HEAD :] = small_ref[...]


def mixer_prepare(
    pos_ref,
    xown_ref,
    xsib_ref,
    wown_ref,
    wsib_ref,
    flag_ref,
    idc_ref,
    idr_ref,
    normed_ref,
    wcat_ref,
    lin_ref,
    tap_ref,
    gains_ref,
    p_ref,
    qh_ref,
    k_ref,
    v_ref,
    sq_ref,
    sk_ref,
    sv_ref,
    beta_ref,
    t_ref,
    sc_ref,
    pb_ref,
    w_ref,
    map_ref,
    add_ref,
    across_ref,
):
    chips, _, span, width = xown_ref.shape
    length = normed_ref.shape[0]
    count = length // CHUNK
    strict, incl, _ = tri_masks(CHUNK)
    m, q, c, _ = place_of(pos_ref)
    head = head_of(pos_ref, chips)
    rows_here = wown_ref.shape[1]
    for i in range(wown_ref.shape[0]):
        block = (m ^ (i // chips)) * chips + (q ^ (i % chips))
        mine = pl.ds(pl.multiple_of((2 * block + c) * rows_here, rows_here), rows_here)
        theirs = pl.ds(pl.multiple_of((2 * block + 1 - c) * rows_here, rows_here), rows_here)
        cols = pl.ds(pl.multiple_of(c * 4 * HEAD, 4 * HEAD), 4 * HEAD)
        wcat_ref[mine, 0 : 4 * HEAD] = wown_ref[i, :, cols]
        wcat_ref[mine, 4 * HEAD :] = wown_ref[i, :, 8 * HEAD :]
        wcat_ref[theirs, :] = wsib_ref[i, :, :]
    for i in range(width // HEAD):
        rows = slice(i * HEAD, (i + 1) * HEAD)
        across_ref[:, rows] = jnp.transpose(wcat_ref[rows, 4 * HEAD :].astype(F32))
    gain = across_ref[HEADS : HEADS + 1, :]
    gains_ref[...] = across_ref[HEADS : HEADS + 8, :]
    mine = pl.ds(pl.multiple_of(head * HEAD, HEAD), HEAD)
    tap_ref[...] = across_ref[HEADS + 2 : HEADS + 18, mine]
    for i in range(2 * chips):
        block = (m ^ (i % 2)) * chips + (q ^ (i // 2))
        for which, ref in ((c, xown_ref), (1 - c, xsib_ref)):
            x = ref[i // 2, i % 2, :, :].astype(F32)
            scale = lax.rsqrt(jnp.mean(x * x, axis=-1, keepdims=True) + EPSILON)
            spot = pl.ds(pl.multiple_of((2 * block + which) * span, span), span)
            normed_ref[spot, :] = (x * scale * gain).astype(BF16)
    lane = lax.broadcasted_iota(jnp.int32, (1, HEAD), 1)
    pick = (lane == head).astype(F32)
    p_ref[0:8, :] = jnp.zeros((8, 3 * HEAD), F32)

    tall = 4 * CHUNK
    for n in range(length // tall):
        rows = slice(n * tall, (n + 1) * tall)
        y = lax.dot_general(normed_ref[rows, :], wcat_ref[...], NN, preferred_element_type=F32)
        p_ref[8 + n * tall : 8 + (n + 1) * tall, :] = y[:, 0 : 3 * HEAD].astype(BF16).astype(F32)
        lin_ref[rows, :] = y[:, 3 * HEAD : 4 * HEAD]
        logit = jnp.sum(y[:, 4 * HEAD :] * pick, axis=-1, keepdims=True)
        beta_ref[rows, :] = jax.nn.sigmoid(logit)
    for n in range(count):
        r0 = n * CHUNK
        rows = slice(r0, r0 + CHUNK)
        keep = [None] + [flag_ref[rows, j : j + 1] for j in range(CONV - 1)]
        for c in range(3):
            cols = slice(c * HEAD, (c + 1) * HEAD)
            pre = tap_ref[4 * c : 4 * c + 1, :] * p_ref[8 + r0 : 8 + r0 + CHUNK, cols]
            for j in range(1, CONV):
                moved = p_ref[8 + r0 - j : 8 + r0 - j + CHUNK, cols]
                pre = pre + tap_ref[4 * c + j : 4 * c + j + 1, :] * moved * keep[j]
            sig = jax.nn.sigmoid(pre)
            act = pre * sig
            slope = sig * (1.0 + pre * (1.0 - sig))
            if c == 2:
                v_ref[rows, :] = act
                sv_ref[rows, :] = slope
            else:
                scale = lax.rsqrt(jnp.sum(act * act, axis=-1, keepdims=True) + UNIT_EPSILON)
                (qh_ref if c == 0 else k_ref)[rows, :] = act * scale
                (sq_ref if c == 0 else sk_ref)[rows, :] = slope * scale
    def prepare(group, carry):
        spots = [pl.multiple_of((group * GROUP + i) * CHUNK, CHUNK) for i in range(GROUP)]
        rows = [pl.ds(s, CHUNK) for s in spots]
        key = [split(k_ref[r, :]) for r in rows]
        same = [
            idc_ref[r, :] == idr_ref[group * GROUP + i, :, :] for i, r in enumerate(rows)
        ]
        beta = [beta_ref[r, :] for r in rows]
        mats = [
            jnp.where(jnp.logical_and(s, strict), b * mm(k, k, NT), 0.0)
            for s, b, k in zip(same, beta, key)
        ]
        inverse = unit_lower_inverses(mats)
        for i, r in enumerate(rows):
            t_ref[r, :] = inverse[i]
            inv = split(inverse[i])
            pseudo = mm(inv, split(beta[i] * v_ref[r, :]), NN)
            weighed = split(
                mm(inv, split(beta[i] * flag_ref[r, 3:4] * k_ref[r, :]), NN)
            )
            ends = split(flag_ref[r, 4:5] * k_ref[r, :])
            query = split(qh_ref[r, :] * HEAD ** (-0.5))
            sc_ref[r, :] = jnp.where(
                jnp.logical_and(same[i], incl), mm(query, key[i], NT), 0.0
            )
            pb_ref[r, :] = pseudo
            w_ref[r, :] = weighed[0].astype(F32) + weighed[1].astype(F32)
            map_ref[r, :] = mm(weighed, ends, TN)
            add_ref[r, :] = mm(split(pseudo), ends, TN)
        return carry

    lax.fori_loop(0, count // GROUP, prepare, 0)


def mixer_produce(
    lin_ref,
    flag_ref,
    idc_ref,
    idr_ref,
    gain_ref,
    qh_ref,
    k_ref,
    v_ref,
    sc_ref,
    pb_ref,
    w_ref,
    map_ref,
    add_ref,
    heads_ref,
    state_ref,
    ps_ref,
    er_ref,
    oh_ref,
    ro_ref,
):
    length = lin_ref.shape[0]
    count = length // CHUNK
    strict, _, _ = tri_masks(CHUNK)
    state = jnp.zeros((HEAD, HEAD), F32)
    for n in range(count):
        rows = slice(n * CHUNK, (n + 1) * CHUNK)
        state_ref[rows, :] = state
        last = flag_ref[(n + 1) * CHUNK - 1 : (n + 1) * CHUNK, 3:4]
        state = last * state - mm(split(state), split(map_ref[rows, :]), NN) + add_ref[rows, :]

    def produce(group, carry):
        for i in range(GROUP):
            r = pl.ds(pl.multiple_of((group * GROUP + i) * CHUNK, CHUNK), CHUNK)
            same = idc_ref[r, :] == idr_ref[group * GROUP + i, :, :]
            key = split(k_ref[r, :])
            state_i = split(state_ref[r, :])
            flag = flag_ref[r, 3:4]
            pseudo = pb_ref[r, :] - mm(split(w_ref[r, :]), state_i, NT)
            ps_ref[r, :] = pseudo
            halves = split(pseudo)
            gram = jnp.where(jnp.logical_and(same, strict), mm(key, key, NT), 0.0)
            er_ref[r, :] = (
                v_ref[r, :] - flag * mm(key, state_i, NT) - mm(split(gram), halves, NN)
            )
            query = split(qh_ref[r, :] * HEAD ** (-0.5))
            out = flag * mm(query, state_i, NT) + mm(split(sc_ref[r, :]), halves, NN)
            scale = lax.rsqrt(jnp.mean(out * out, axis=-1, keepdims=True) + EPSILON)
            hat = out * scale
            oh_ref[r, :] = hat
            ro_ref[r, :] = scale
            lin = lin_ref[r, :]
            made = (hat * gain_ref[...] * (lin * jax.nn.sigmoid(lin))).astype(BF16)
            half = CHUNK // 2
            spot = pl.ds(pl.multiple_of((group * GROUP + i) * half, half), half)
            for chip in range(heads_ref.shape[0]):
                heads_ref[chip, 0, spot, :] = made[:half]
                heads_ref[chip, 1, spot, :] = made[half:]
        return carry

    lax.fori_loop(0, count // GROUP, produce, 0)


def mixer_backward_states(
    dh_ref,
    lin_ref,
    flag_ref,
    gain_ref,
    qh_ref,
    k_ref,
    beta_ref,
    t_ref,
    sc_ref,
    map_ref,
    oh_ref,
    ro_ref,
    dg_ref,
    headgrad_ref,
    do_ref,
    dpre_ref,
    dstate_ref,
    back_ref,
):
    length = lin_ref.shape[0]
    count = length // CHUNK
    chips = dh_ref.shape[0] // 2
    scale_q = HEAD ** (-0.5)
    headgrad_ref[...] = jnp.zeros(headgrad_ref.shape, F32)

    def first(group, carry):
        for i in range(GROUP):
            r = pl.ds(pl.multiple_of((group * GROUP + i) * CHUNK, CHUNK), CHUNK)
            block = group * GROUP + i
            pair = [dh_ref[2 * (block % chips) + j, block // chips, :, :] for j in range(2)]
            grad = jnp.concatenate(pair, axis=0).astype(F32)
            lin = lin_ref[r, :]
            sig = jax.nn.sigmoid(lin)
            swish = lin * sig
            hat = oh_ref[r, :]
            gain = gain_ref[...]
            both = grad * hat
            headgrad_ref[0:1, :] += jnp.sum(both * swish, axis=0, keepdims=True)
            dg_ref[r, :] = (
                both * gain * (sig * (1.0 + lin * (1.0 - sig)))
            ).astype(BF16)
            lead = grad * gain * swish
            grad_out = ro_ref[r, :] * (
                lead - hat * jnp.mean(lead * hat, axis=-1, keepdims=True)
            )
            do_ref[r, :] = grad_out
            flag = flag_ref[r, 3:4]
            direct = mm(split(sc_ref[r, :]), split(grad_out), TN)
            dpre_ref[r, :] = direct
            zed = mm(split(t_ref[r, :]), split(direct), TN)
            back_ref[r, :] = mm(
                split(flag * grad_out), split(qh_ref[r, :] * scale_q), TN
            ) - mm(split(beta_ref[r, :] * flag * zed), split(k_ref[r, :]), TN)
        return carry

    lax.fori_loop(0, count // GROUP, first, 0)
    grad_state = jnp.zeros((HEAD, HEAD), F32)
    for n in reversed(range(count)):
        rows = slice(n * CHUNK, (n + 1) * CHUNK)
        dstate_ref[rows, :] = grad_state
        last = flag_ref[(n + 1) * CHUNK - 1 : (n + 1) * CHUNK, 3:4]
        grad_state = (
            last * grad_state
            - mm(split(grad_state), split(map_ref[rows, :]), NT)
            + back_ref[rows, :]
        )


def mixer_backward_tokens(
    do_ref,
    dpre_ref,
    dstate_ref,
    flag_ref,
    idc_ref,
    idr_ref,
    pick_ref,
    qh_ref,
    k_ref,
    sq_ref,
    sk_ref,
    sv_ref,
    beta_ref,
    t_ref,
    state_ref,
    ps_ref,
    er_ref,
    du_ref,
    dz_ref,
):
    length = do_ref.shape[0]
    count = length // CHUNK
    strict, incl, _ = tri_masks(CHUNK)
    scale_q = HEAD ** (-0.5)
    du_ref[length : length + 8, :] = jnp.zeros((8, 3 * HEAD), F32)

    def second(group, carry):
        for i in range(GROUP):
            r = pl.ds(pl.multiple_of((group * GROUP + i) * CHUNK, CHUNK), CHUNK)
            same = idc_ref[r, :] == idr_ref[group * GROUP + i, :, :]
            low = jnp.logical_and(same, strict)
            full = jnp.logical_and(same, incl)
            flag = flag_ref[r, 3:4]
            ends = flag_ref[r, 4:5]
            beta = beta_ref[r, :]
            key_f = k_ref[r, :]
            key = split(key_f)
            q_hat = qh_ref[r, :]
            query = split(q_hat * scale_q)
            state_i = split(state_ref[r, :])
            dstate = split(dstate_ref[r, :])
            grad_out = split(do_ref[r, :])
            pseudo = split(ps_ref[r, :])
            dpre = dpre_ref[r, :] + ends * mm(key, dstate, NT)
            zed = mm(split(t_ref[r, :]), split(dpre), TN)
            zeds = split(zed)
            dscore = split(jnp.where(full, mm(grad_out, pseudo, NT), 0.0))
            grad_q = flag * mm(grad_out, state_i, NN) + mm(dscore, key, NN)
            dgram = split(jnp.where(low, -beta * mm(zeds, pseudo, NT), 0.0))
            grad_v = beta * zed
            grad_k = (
                mm(dscore, query, TN)
                + ends * mm(pseudo, dstate, NN)
                + mm(dgram, key, NN)
                + mm(dgram, key, TN)
                - flag * mm(split(grad_v), state_i, NN)
            )
            grad_b = jnp.sum(zed * er_ref[r, :], axis=-1, keepdims=True)
            dz = grad_b * beta * (1.0 - beta)
            dz_ref[r, :] = (dz * pick_ref[...]).astype(BF16)
            lead = scale_q * grad_q
            du_ref[r, 0:HEAD] = sq_ref[r, :] * (
                lead - q_hat * jnp.sum(lead * q_hat, axis=-1, keepdims=True)
            )
            du_ref[r, HEAD : 2 * HEAD] = sk_ref[r, :] * (
                grad_k - key_f * jnp.sum(grad_k * key_f, axis=-1, keepdims=True)
            )
            du_ref[r, 2 * HEAD : 3 * HEAD] = sv_ref[r, :] * grad_v
        return carry

    lax.fori_loop(0, count // GROUP, second, 0)


def mixer_backward_taps(
    du_ref,
    dg_ref,
    dz_ref,
    flag_ref,
    tap_ref,
    p_ref,
    pos_ref,
    normed_ref,
    wcat_ref,
    swiglu_ref,
    dnkeep_ref,
    dnsend_ref,
    dwkeep_ref,
    dwsend_ref,
    dcat_ref,
    tapgrad_ref,
):
    length = dg_ref.shape[0]
    count = length // CHUNK
    blocks, rows_here, _ = dwkeep_ref.shape
    chips = blocks // 2
    repeat = chips // (HEADS // 2)
    span = length // (2 * blocks)
    core, share = pos_ref[2], pos_ref[1] % repeat
    head = head_of(pos_ref, chips)
    dcat_ref[:, 3 * HEAD : 4 * HEAD] = dg_ref[...]
    dcat_ref[:, 4 * HEAD : 5 * HEAD] = dz_ref[...]
    sums = [[jnp.zeros((1, HEAD), F32) for _ in range(CONV)] for _ in range(3)]
    for n in range(count):
        r0 = n * CHUNK
        rows = slice(r0, r0 + CHUNK)
        for c in range(3):
            cols = slice(c * HEAD, (c + 1) * HEAD)
            here = du_ref[rows, cols]
            grad = tap_ref[4 * c : 4 * c + 1, :] * here
            sums[c][0] += jnp.sum(
                here * p_ref[8 + r0 : 8 + r0 + CHUNK, cols], axis=0, keepdims=True
            )
            for j in range(1, CONV):
                after = slice(r0 + j, r0 + j + CHUNK)
                grad = grad + tap_ref[4 * c + j : 4 * c + j + 1, :] * (
                    du_ref[after, cols] * flag_ref[after, j - 1 : j]
                )
                moved = p_ref[8 + r0 - j : 8 + r0 - j + CHUNK, cols]
                sums[c][j] += jnp.sum(
                    here * flag_ref[rows, j - 1 : j] * moved, axis=0, keepdims=True
                )
            dcat_ref[rows, cols] = grad.astype(BF16)
    tapgrad_ref[...] = jnp.concatenate(
        [sums[c][j] for c in range(3) for j in range(CONV)]
        + [jnp.zeros((4, HEAD), F32)],
        axis=0,
    )
    if repeat > 1:
        for n in range(count):
            counts = (n % chips % repeat == share).astype(F32)
            rows = slice(n * CHUNK, (n + 1) * CHUNK)
            dcat_ref[rows, :] = (dcat_ref[rows, :].astype(F32) * counts).astype(BF16)
        tapgrad_ref[...] = tapgrad_ref[...] * (share == 0).astype(F32)
    width = normed_ref.shape[1]

    tall = 4 * CHUNK
    for n in range(length // tall):
        rows = slice(n * tall, (n + 1) * tall)
        part = lax.dot_general(dcat_ref[rows, :], wcat_ref[...], NT, preferred_element_type=F32)
        for j in range(4):
            low = part[2 * j * span : (2 * j + 1) * span]
            high = part[(2 * j + 1) * span : (2 * j + 2) * span]
            dnkeep_ref[4 * n + j, :, :] = jnp.where(core == 1, high, low).astype(BF16)
            dnsend_ref[4 * n + j, :, :] = jnp.where(core == 1, low, high).astype(BF16)
    for i in range(width // HEAD):
        cols = slice(i * HEAD, (i + 1) * HEAD)
        if i % 4 == 0:
            wide = slice(i * HEAD, (i + 4) * HEAD)
            four = lax.dot_general(
                normed_ref[:, wide], dcat_ref[...], TN, preferred_element_type=F32
            )
        grad = four[i % 4 * HEAD : (i % 4 + 1) * HEAD]
        mats = wcat_ref[cols, :].astype(F32)
        gain = mats[:, 4 * HEAD + HEADS : 4 * HEAD + HEADS + 1]
        gain_grad = jnp.sum(grad * mats, axis=-1, keepdims=True) / gain
        here = (head == i).astype(F32)
        lines = jnp.concatenate(
            [
                jnp.zeros((HEADS, HEAD), F32),
                jnp.zeros((1, HEAD), F32),
                swiglu_ref[0:1, cols],
                tapgrad_ref[0 : 3 * CONV, :] * here,
                jnp.zeros((HEAD - HEADS - 2 - 3 * CONV, HEAD), F32),
            ],
            axis=0,
        )
        lane = lax.broadcasted_iota(jnp.int32, (1, HEAD), 1)
        small = grad[:, 4 * HEAD :] + jnp.transpose(lines) + gain_grad * (lane == HEADS)
        grad = jnp.concatenate([grad[:, : 4 * HEAD], small], axis=1)
        per = HEAD // (2 * rows_here)
        for j in range(per):
            low = grad[2 * j * rows_here : (2 * j + 1) * rows_here]
            high = grad[(2 * j + 1) * rows_here : (2 * j + 2) * rows_here]
            dwkeep_ref[i * per + j, :, :] = jnp.where(core == 1, high, low).astype(BF16)
            dwsend_ref[i * per + j, :, :] = jnp.where(core == 1, low, high).astype(BF16)


def feed_forward(
    pos_ref,
    got_ref,
    xown_ref,
    cot_ref,
    oown_ref,
    osib_ref,
    pown_ref,
    psib_ref,
    down_ref,
    gains_ref,
    wo_ref,
    normed_ref,
    grads_ref,
    hidden_ref,
    cots_ref,
    swiglu_ref,
    res_ref,
    norm_ref,
    *rest,
):
    chips, _, span, width = xown_ref.shape
    send_refs, (wp_ref, heads_ref, total_ref, hat_ref, part_ref) = rest[: chips - 1], rest[chips - 1 :]
    repeat = chips // (HEADS // 2)
    tokens = 2 * chips * span
    ff = down_ref.shape[0]
    m, q, c, _ = place_of(pos_ref)
    rows_here = oown_ref.shape[2]
    for i in range(2 * chips):
        d, e = i // 2, i % 2
        block = (m ^ e) * chips + (q ^ d)
        for which, o_ref, p_ref in ((c, oown_ref, pown_ref), (1 - c, osib_ref, psib_ref)):
            spot = pl.ds(pl.multiple_of((2 * block + which) * rows_here, rows_here), rows_here)
            wo_ref[spot, :] = o_ref[d, e, :, :]
            other = (m ^ e) * chips + d
            spot = pl.ds(pl.multiple_of((2 * other + which) * rows_here, rows_here), rows_here)
            wp_ref[spot, :] = p_ref[e, d, :, :]
        spot = pl.ds(pl.multiple_of(block * span, span), span)
        total_ref[spot, :] = xown_ref[d, e, :, :].astype(F32)
        cots_ref[spot, :] = cot_ref[d, e, :, :]
    for i in range(2):
        for j in range(HEADS // 2):
            h = i * (HEADS // 2) + j
            heads_ref[:, h * HEAD : (h + 1) * HEAD] = got_ref[2 * j * repeat + i, :, :]
    total = total_ref[...] + lax.dot_general(
        heads_ref[...], wo_ref[...], NN, preferred_element_type=F32
    )
    total_ref[...] = total
    scale = lax.rsqrt(jnp.mean(total * total, axis=-1, keepdims=True) + EPSILON)
    hat = total * scale
    hat_ref[...] = hat
    normed_ref[...] = (hat * gains_ref[1:2, :]).astype(BF16)
    both = lax.dot_general(normed_ref[...], wp_ref[...], NN, preferred_element_type=F32)
    gate, up = both[:, :ff], both[:, ff:]
    sig = jax.nn.sigmoid(gate)
    act = gate * sig
    hidden_ref[...] = (act * up).astype(BF16)
    back = lax.dot_general(cots_ref[...], down_ref[...], NT, preferred_element_type=F32)
    slope = sig * (1.0 + gate * (1.0 - sig))
    grads_ref[...] = jnp.concatenate([back * up * slope, back * act], axis=1).astype(BF16)
    part_ref[...] = lax.dot_general(grads_ref[...], wp_ref[...], NT, preferred_element_type=F32)
    total = jnp.sum(part_ref[...] * hat_ref[...], axis=0, keepdims=True)
    swiglu_ref[...] = jnp.broadcast_to(total, swiglu_ref.shape)
    for e in range(2):
        spot = pl.ds(pl.multiple_of((e * chips + q) * span, span), span)
        res_ref[e, :, :] = total_ref[spot, :]
        norm_ref[e, :, :] = part_ref[spot, :]
        for d, send_ref in enumerate(send_refs):
            spot = pl.ds(pl.multiple_of((e * chips + (q ^ (d + 1))) * span, span), span)
            send_ref[e, :, :] = part_ref[spot, :].astype(BF16)


def feed_forward_grads(
    pos_ref, normed_ref, grads_ref, hidden_ref, cots_ref, down_ref, keep_ref, send_ref, downgrad_ref, out_ref
):
    rows_here = keep_ref.shape[1]
    chips, _, span, _ = out_ref.shape
    core = pos_ref[2]
    per = HEAD // (2 * rows_here)
    for i in range(normed_ref.shape[1] // HEAD):
        if i % 4 == 0:
            wide = slice(i * HEAD, (i + 4) * HEAD)
            four = lax.dot_general(
                normed_ref[:, wide], grads_ref[...], TN, preferred_element_type=F32
            )
        grad = four[i % 4 * HEAD : (i % 4 + 1) * HEAD]
        for j in range(per):
            low = grad[2 * j * rows_here : (2 * j + 1) * rows_here]
            high = grad[(2 * j + 1) * rows_here : (2 * j + 2) * rows_here]
            keep_ref[i * per + j, :, :] = jnp.where(core == 1, high, low).astype(BF16)
            send_ref[i * per + j, :, :] = jnp.where(core == 1, low, high).astype(BF16)
    downgrad_ref[...] = lax.dot_general(
        hidden_ref[...], cots_ref[...], TN, preferred_element_type=F32
    ).astype(BF16)
    out = lax.dot_general(hidden_ref[...], down_ref[...], NN, preferred_element_type=F32)
    for e in range(2):
        for j in range(chips):
            spot = (e * chips + j) * span
            out_ref[j, e, :, :] = out[spot : spot + span].astype(BF16)


def branch_gradient(pos_ref, norm_ref, res_ref, cot_ref, gains_ref, wo_ref, *rest):
    *got_refs, resid_ref, branch_ref, heads_ref = rest
    m = pos_ref[0]
    chips = heads_ref.shape[0] // 2
    repeat = chips // (HEADS // 2)
    branches = []
    for e in range(2):
        norm = norm_ref[e, :, :]
        for got_ref in got_refs:
            norm = norm + got_ref[e, :, :].astype(F32)
        res = res_ref[e, :, :]
        scale = lax.rsqrt(jnp.mean(res * res, axis=-1, keepdims=True) + EPSILON)
        hat = res * scale
        lead = norm * gains_ref[1:2, :]
        grad = cot_ref[0, m ^ e, :, :].astype(F32) + scale * (
            lead - hat * jnp.mean(lead * hat, axis=-1, keepdims=True)
        )
        resid_ref[e, :, :] = grad
        branch = grad.astype(BF16)
        branch_ref[e, :, :] = branch
        branches.append(branch)
    back = lax.dot_general(
        jnp.concatenate(branches, axis=0), wo_ref[...], NT, preferred_element_type=F32
    ).astype(BF16)
    span = branch_ref.shape[1]
    for e in range(2):
        for j in range(chips):
            for i in range(2):
                h = i * (HEADS // 2) + j // repeat
                heads_ref[2 * j + i, e, :, :] = back[
                    e * span : (e + 1) * span, h * HEAD : (h + 1) * HEAD
                ]


def output_gradient(pos_ref, got_ref, branch_ref, all_ref, rows_ref, duo_ref):
    chips, _, span, width = branch_ref.shape
    repeat = chips // (HEADS // 2)
    q = pos_ref[1]
    share = q % repeat
    for i in range(2 * chips):
        d, e = i // 2, i % 2
        spot = pl.ds(pl.multiple_of((e * chips + (q ^ d)) * span, span), span)
        counts = ((q ^ d) % repeat == share).astype(F32)
        rows_ref[spot, :] = (branch_ref[d, e, :, :].astype(F32) * counts).astype(BF16)
    first = pl.multiple_of((q // repeat) * 2 * repeat, 2)
    for i in range(2):
        duo_ref[:, i * HEAD : (i + 1) * HEAD] = got_ref[first + i, :, :]
    both = lax.dot_general(duo_ref[...], rows_ref[...], TN, preferred_element_type=F32)
    for i in range(2):
        all_ref[i, :, :] = both[i * HEAD : (i + 1) * HEAD].astype(BF16)


def input_gradient(pos_ref, resid_ref, x_ref, gains_ref, keep_ref, *rest):
    *got_refs, out_ref = rest
    m = pos_ref[0]
    for e in range(2):
        norm = keep_ref[e, :, :]
        for got_ref in got_refs:
            norm = norm + got_ref[e, :, :].astype(F32)
        x = x_ref[m ^ e, :, :].astype(F32)
        scale = lax.rsqrt(jnp.mean(x * x, axis=-1, keepdims=True) + EPSILON)
        hat = x * scale
        lead = norm * gains_ref[0:1, :]
        out_ref[e, :, :] = (
            resid_ref[e, :, :]
            + scale * (lead - hat * jnp.mean(lead * hat, axis=-1, keepdims=True))
        ).astype(BF16)


def token_pieces(pos_ref, keep_ref, got_ref, own_ref, *send_refs):
    chips = keep_ref.shape[0] // 2
    q = pos_ref[1]
    for e in range(2):
        for d in range(chips):
            block = e * chips + (q ^ d)
            total = keep_ref[block, :, :].astype(F32) + got_ref[block, :, :].astype(F32)
            if d == 0:
                own_ref[e, :, :] = total
            else:
                send_refs[d - 1][e, :, :] = total.astype(BF16)


def merge_heads(pos_ref, keep_ref, got_ref, out_ref):
    core = pos_ref[2]
    wide = 4 * HEAD
    keep, got = keep_ref[...], got_ref[...]
    out_ref[:, :, :wide] = jnp.where(core == 1, got[:, :, :wide], keep[:, :, :wide])
    out_ref[:, :, wide : 2 * wide] = jnp.where(core == 1, keep[:, :, :wide], got[:, :, :wide])
    out_ref[:, :, 2 * wide :] = (
        keep[:, :, wide:].astype(F32) + got[:, :, wide:].astype(F32)
    ).astype(BF16)


def spread_heads(pos_ref, *refs):
    *got_refs, wq_ref, wk_ref, wv_ref, wg_ref, beta_ref, gains_ref, taps_ref, head_ref, side_ref = refs
    chips = len(got_refs)
    repeat = chips // (HEADS // 2)
    rows = wq_ref.shape[0]
    small = jnp.zeros((rows, HEAD), F32)
    heads = jnp.zeros((1, HEAD), F32)
    if repeat > 1:
        for ref in (wq_ref, wk_ref, wv_ref, wg_ref):
            ref[...] = jnp.zeros(ref.shape, F32)
    for d, got_ref in enumerate(got_refs):
        slot = (pos_ref[1] ^ d) // repeat
        for i in range(2):
            cols = pl.ds(pl.multiple_of((i * (HEADS // 2) + slot) * HEAD, HEAD), HEAD)
            for t, ref in enumerate((wq_ref, wk_ref, wv_ref, wg_ref)):
                spot = (4 * i + t) * HEAD
                value = got_ref[0:rows, spot : spot + HEAD].astype(F32)
                ref[:, cols] = value + ref[:, cols] if repeat > 1 else value
        small = small + got_ref[0:rows, 8 * HEAD :].astype(F32)
        heads = heads + got_ref[rows : rows + 1, 0:HEAD].astype(F32)
    beta_ref[...] = small[:, :HEADS]
    side_ref[...] = jnp.zeros(side_ref.shape, F32)
    side_ref[0:rows, :] = small
    across = jnp.transpose(side_ref[...])
    gains_ref[...] = across[HEADS : HEADS + 8, :rows]
    taps_ref[...] = across[HEADS + 2 : HEADS + 2 + 3 * CONV, :rows]
    head_ref[...] = heads


def spread_pair(got_ref, gate_ref, up_ref):
    chips, _, wide = got_ref.shape
    wide = wide // 4
    for j in range(chips):
        got = got_ref[j, :, :].astype(F32)
        for t, ref in enumerate((gate_ref, up_ref)):
            for e in range(2):
                part = (2 * t + e) * wide
                spot = (e * chips + j) * wide
                ref[:, spot : spot + wide] = got[:, part : part + wide]


VMEM_SPEC = pl.BlockSpec(memory_space=pltpu.VMEM)


def run_kernel(body, name, operands, out_shapes, scratch, micros, scalars=()):
    specs = [VMEM_SPEC] * len(operands)
    for i in scalars:
        specs[i] = pl.BlockSpec(memory_space=pltpu.SMEM)
    return pl.pallas_call(
        body,
        name=name,
        out_shape=[jax.ShapeDtypeStruct(*s) for s in out_shapes],
        in_specs=specs,
        out_specs=[VMEM_SPEC] * len(out_shapes),
        scratch_shapes=[pltpu.VMEM(*s) for s in scratch],
        compiler_params=pltpu.CompilerParams(vmem_limit_bytes=56 * 1024 * 1024),
        cost_estimate=pl.CostEstimate(
            flops=micros * COST, bytes_accessed=1 << 10, transcendentals=0
        ),
    )(*operands)


def tie(value, *others):
    return lax.optimization_barrier((value,) + others)[0]


def together(*values):
    return lax.optimization_barrier(values)


def swap(value, axis, mask):
    return lax.ppermute(value, axis, [(i, i ^ mask) for i in range(lax.axis_size(axis))])


def ordered(bit, mine, other):
    flag = bit == 1
    return (jnp.where(flag, other, mine), jnp.where(flag, mine, other))


def from_chips(value):
    return [value] + [swap(value, "q", d) for d in range(1, lax.axis_size("q"))]


def to_chips(blocks):
    chip = lax.axis_index("q")
    mine = [lax.dynamic_index_in_dim(blocks, chip ^ d, 0, keepdims=False) for d in range(blocks.shape[0])]
    return [mine[0]] + [swap(mine[d], "q", d) for d in range(1, len(mine))]


def gather_batch(value, axis):
    step, batch = 1, lax.axis_index("b")
    lead, rows = value.shape[:axis], value.shape[axis:]
    while step < lax.axis_size("b"):
        got = swap(value, "b", step)
        value = jnp.stack(ordered((batch // step) % 2, value, got), axis=axis)
        step *= 2
    return value.reshape(lead + (lax.axis_size("b") * rows[0],) + rows[1:])


def scatter_bit(value, axis, bit, mesh_axis, mask):
    low, high = (lax.index_in_dim(value, i, axis, keepdims=False) for i in (0, 1))
    flag = bit == 1
    keep, send = jnp.where(flag, high, low), jnp.where(flag, low, high)
    return keep.astype(F32) + swap(send.astype(BF16), mesh_axis, mask).astype(F32)


def scatter_batch(value, axis):
    batch, step = lax.axis_index("b"), lax.axis_size("b") // 2
    while step >= 1:
        shape = value.shape
        value = value.reshape(shape[:axis] + (2, shape[axis] // 2) + shape[axis + 1 :])
        value = scatter_bit(value, axis, (batch // step) % 2, "b", step)
        step //= 2
    return lax.squeeze(value, (axis,))


def token_flags(ids):
    length = ids.shape[0]
    padded = jnp.concatenate([jnp.full((CONV - 1,), -1, jnp.int32), ids])
    by_chunk = ids.reshape(length // CHUNK, CHUNK)
    before = jnp.concatenate([jnp.full((1,), -1, jnp.int32), by_chunk[:-1, -1]])
    columns = [padded[CONV - 1 - j : CONV - 1 - j + length] == ids for j in range(1, CONV)]
    columns.append((by_chunk == before[:, None]).reshape(length))
    columns.append((by_chunk == by_chunk[:, -1:]).reshape(length))
    flags = jnp.stack(columns, axis=1).astype(F32)
    return jnp.pad(flags, ((0, 8), (0, 3))), by_chunk[:, None, :], ids[:, None]


def on_device(
    inputs,
    cotangent,
    document_ids,
    query_weight,
    key_weight,
    value_weight,
    beta_weight,
    outgate_weight,
    output_weight,
    gate_weight,
    up_weight,
    down_weight,
    mixer_gain,
    swiglu_gain,
    head_gain,
    conv_weight,
):
    micro, _, span, width = inputs.shape
    chips, n_batch = lax.axis_size("q"), lax.axis_size("b")
    half_heads = HEADS // 2
    repeat = chips // half_heads
    length = micro * chips * 2 * span
    rows_w = query_weight.shape[0]
    rows_f = down_weight.shape[0]
    rows_all = n_batch * rows_w
    blocks_all = micro * chips
    ff_here = rows_f * micro * 2 * n_batch
    row, chip, core = lax.axis_index("m"), lax.axis_index("q"), lax.axis_index("c")
    share = chip % repeat
    flag_row = row == 1
    pos = jnp.stack([row, chip, core, lax.axis_index("b")]).astype(jnp.int32)

    small = jnp.concatenate(
        [
            beta_weight,
            mixer_gain[:, None],
            swiglu_gain[:, None],
            jnp.swapaxes(conv_weight, 0, 1),
            jnp.zeros((rows_w, HEAD - HEADS - 2 - 3 * CONV), BF16),
        ],
        axis=1,
    )
    mine = run_kernel(
        pack_heads,
        "pack_heads",
        (pos, query_weight, key_weight, value_weight, outgate_weight, small),
        [((rows_w, 9 * HEAD), BF16)] * chips,
        [],
        1,
        (0,),
    )
    head_s = [swap(mine[d], "q", d) for d in range(1, chips)]

    def own_slab(value):
        return jnp.where(flag_row, value[1], value[0])

    def away_slab(value):
        return jnp.where(flag_row, value[0], value[1])

    x_s, out_s = swap(away_slab(inputs[:, 0]), "m", 1), swap(output_weight, "m", 1)
    head_s, x_s, out_s = together(head_s, x_s, out_s)
    head_q = jnp.stack([mine[0]] + head_s, axis=0)
    x_own = jnp.stack([own_slab(inputs[:, 0]), x_s], axis=0)
    head_m = jnp.stack([head_q, swap(head_q, "m", 1)], axis=0)
    x_half = jnp.stack(from_chips(x_own), axis=0)
    out_b = gather_batch(jnp.stack([output_weight, out_s], axis=0), 1)
    ids = own_slab(document_ids[:, 0])
    flags, id_rows, id_cols = token_flags(ids)
    gain_vec = head_gain.astype(F32)[None, :]
    head_m, x_half, out_b, flags, id_rows, id_cols, gain_vec = together(
        head_m, x_half, out_b, flags, id_rows, id_cols, gain_vec
    )
    head_b = gather_batch(head_m.reshape(blocks_all, rows_w, 9 * HEAD), 1)
    x_sib = swap(x_half, "c", 1)
    cot_s = swap(tie(away_slab(cotangent[:, 0]), x_half), "m", 1)
    pair = jnp.stack([gate_weight, up_weight], axis=1).reshape(
        rows_w, 2, micro, chips, 2 * n_batch * rows_f
    )
    pair = jnp.moveaxis(pair, 3, 0).reshape(chips, rows_w, 2 * ff_here)
    pair_q = lax.all_to_all(tie(pair, x_half), ("q",), 0, 0, tiled=True)
    head_b, x_sib, cot_s, pair_q = together(head_b, x_sib, cot_s, pair_q)
    cot_own = jnp.stack([own_slab(cotangent[:, 0]), cot_s], axis=0)
    send = lax.dynamic_slice_in_dim(head_b, (1 - core) * 4 * HEAD, 4 * HEAD, 2)
    head_sib = swap(jnp.concatenate([send, head_b[..., 8 * HEAD :]], axis=-1), "c", 1)
    pair_s = swap(tie(pair_q, head_b), "m", 1)
    out_s = [swap(tie(out_b, head_b), "q", d) for d in range(1, chips)]

    count = length // CHUNK
    tall = ((length, HEAD), F32)
    square = ((length, CHUNK), F32)
    states = ((count * HEAD, HEAD), F32)
    thin = ((length, 1), F32)
    slabs = ((2, span, width), BF16)
    slabs_wide = ((2, span, width), F32)
    normed, w_cat, lin, taps, gains, p_pad, q_hat, k_vec, v_vec, slope_q, slope_k, slope_v, beta, t_mat, score, pseudo, weighed, step_map, step_add = run_kernel(
        mixer_prepare,
        "mixer_prepare",
        (pos, x_half, x_sib, head_b, head_sib, flags, id_cols, id_rows),
        [
            ((length, width), BF16),
            ((width, 5 * HEAD), BF16),
            tall,
            ((16, HEAD), F32),
            ((8, width), F32),
            ((length + 8, 3 * HEAD), F32),
        ]
        + [tall] * 6
        + [thin, square, square, tall, tall, states, states],
        [((HEAD, width), F32)],
        20,
        (0,),
    )
    pair_s, out_s, lin_late = together(pair_s, out_s, lin)
    pair_m = jnp.stack([pair_q, pair_s], axis=0).reshape(blocks_all, rows_w, 2 * ff_here)
    out_q = jnp.stack([out_b] + out_s, axis=0)
    cot_s = [swap(tie(cot_own, lin_late), "q", d) for d in range(1, chips)]
    down_s = swap(tie(down_weight, lin_late), "m", 1)
    pair_b = gather_batch(pair_m, 1)
    heads_here, state, pseudo, error, out_hat, out_scale = run_kernel(
        mixer_produce,
        "mixer_produce",
        (tie(lin_late, pair_m, out_q), flags, id_cols, id_rows, gain_vec)
        + (q_hat, k_vec, v_vec, score, pseudo, weighed, step_map, step_add),
        [((chips, 2, length // 2, HEAD), BF16), states, tall, tall, tall, thin],
        [],
        9,
    )

    got_heads = lax.all_to_all(
        heads_here.reshape(chips * 2, length // 2, HEAD), ("q", "c"), 0, 0, tiled=True
    )
    pair_b, down_s, cot_s = tie((pair_b, down_s, cot_s), heads_here)
    down_m = jnp.stack(ordered(row, down_weight, down_s), axis=0)
    down_b = gather_batch(down_m, 1)
    cot_half = jnp.stack([cot_own] + cot_s, axis=0)
    pair_b = pair_b.reshape(micro, chips, rows_all, 2 * ff_here)
    pair_sib = swap(pair_b, "c", 1)
    out_sib = swap(out_q, "c", 1)
    down_sib = swap(down_b, "c", 1)
    w_down = jnp.stack(ordered(core, down_b, down_sib), axis=1).reshape(ff_here, width)
    half = length // 2
    w_out, normed_two, pair_up, hidden, cot_rows, swiglu_part, res_own, norm_own, *norm_send = run_kernel(
        feed_forward,
        "feed_forward",
        (pos, got_heads, x_half, cot_half, out_q, out_sib, pair_b, pair_sib, w_down, gains),
        [
            ((width, width), BF16),
            ((half, width), BF16),
            ((half, 2 * ff_here), BF16),
            ((half, ff_here), BF16),
            ((half, width), BF16),
            ((8, width), F32),
            slabs_wide,
            slabs_wide,
        ]
        + [slabs] * (chips - 1),
        [
            ((width, 2 * ff_here), BF16),
            ((half, width), BF16),
            ((half, width), F32),
            ((half, width), F32),
            ((half, width), F32),
        ],
        12,
        (0,),
    )
    norm_got = [swap(v, "q", d + 1) for d, v in enumerate(norm_send)]
    pair_keep, pair_send, down_grad, out_part = run_kernel(
        feed_forward_grads,
        "feed_forward_grads",
        (pos, normed_two, pair_up, hidden, cot_rows, w_down),
        [
            ((blocks_all, rows_all, 2 * ff_here), BF16),
            ((blocks_all, rows_all, 2 * ff_here), BF16),
            ((ff_here, width), BF16),
            ((chips, 2, span, width), BF16),
        ],
        [],
        6,
        (0,),
    )
    norm_got, norm_own, pair_keep, pair_send, down_grad, out_part = together(
        norm_got, norm_own, pair_keep, pair_send, down_grad, out_part
    )
    grad_resid, grad_branch, grad_heads = run_kernel(
        branch_gradient,
        "branch_gradient",
        (pos, norm_own, res_own, cot_half, gains, w_out, *norm_got),
        [slabs_wide, slabs, ((chips * 2, 2, span, HEAD), BF16)],
        [],
        2,
        (0,),
    )
    dheads = lax.all_to_all(grad_heads, ("q", "c"), 0, 0, tiled=True)

    pair_got = swap(pair_send, "c", 1)
    down_grad = scatter_bit(
        down_grad.reshape(micro, 2, n_batch, rows_f, width), 1, core, "c", 1
    ).astype(BF16)
    pair_grad = pair_keep.astype(F32) + pair_got.astype(F32)
    dheads, pair_grad, down_grad = together(dheads, pair_grad, down_grad)
    pair_grad = pair_grad.reshape(blocks_all, n_batch, rows_w, 2 * ff_here)
    pair_grad = scatter_batch(pair_grad, 1).reshape(micro, chips, rows_w, 2 * ff_here)
    branch_s = [swap(grad_branch, "q", d) for d in range(1, chips)]
    grad_lin, head_part, grad_out, grad_pre, grad_state = run_kernel(
        mixer_backward_states,
        "mixer_backward_states",
        (dheads, lin, flags, gain_vec, q_hat, k_vec, beta, t_mat, score, step_map, out_hat, out_scale),
        [((length, HEAD), BF16), ((8, HEAD), F32), tall, tall, states],
        [states],
        9,
    )
    branch_s, grad_out = together(branch_s, grad_out)
    branch_all = jnp.stack([grad_branch] + branch_s, axis=0)
    (out_rows,) = run_kernel(
        output_gradient,
        "output_gradient",
        (pos, got_heads, branch_all),
        [((2, HEAD, width), BF16)],
        [((half, width), BF16), ((half, 2 * HEAD), BF16)],
        1,
        (0,),
    )
    if repeat > 1:
        head_part = jnp.where(share == 0, head_part, 0.0)
    step = repeat // 2
    while step >= 1:
        out_rows = out_rows.reshape(micro, 2, out_rows.shape[1] // 2, width)
        out_rows = scatter_bit(out_rows, 1, (share // step) % 2, "q", step)
        step //= 2
    out_rows = out_rows.astype(BF16).reshape(micro, 2, n_batch, rows_w, width)
    head_rows = jnp.pad(head_part, ((0, 0), (0, width - HEAD))).astype(BF16)
    head_rows = jnp.broadcast_to(head_rows, (micro, 2, n_batch, 8, width))
    tail = jnp.concatenate([out_rows, head_rows], axis=3)
    pair_grad, grad_out, tail = together(pair_grad, grad_out, tail)
    tail = scatter_bit(tail, 1, core, "c", 1)
    down_grad = scatter_batch(down_grad, 1)
    pair_rows = scatter_bit(pair_grad, 0, row, "m", 1).astype(BF16)
    out_got = lax.all_to_all(tie(out_part, grad_out), ("q",), 0, 0, tiled=True)
    du, grad_z = run_kernel(
        mixer_backward_tokens,
        "mixer_backward_tokens",
        (grad_out, grad_pre, grad_state, flags, id_cols, id_rows, pick_of(pos, chips), q_hat, k_vec)
        + (slope_q, slope_k, slope_v, beta, t_mat, state, pseudo, error),
        [((length + 8, 3 * HEAD), F32), ((length, HEAD), BF16)],
        [],
        10,
    )
    tail, down_grad, pair_rows, out_got, grad_z = together(
        tail, down_grad, pair_rows, out_got, grad_z
    )
    out_all = (res_own + jnp.sum(out_got.astype(F32), axis=0)).astype(BF16)

    def to_rows(value):
        keep = jnp.where(flag_row, value[1], value[0])
        send = jnp.where(flag_row, value[0], value[1])
        return jnp.stack(ordered(row, keep, swap(send, "m", 1)), axis=0)[:, None]

    tail = scatter_batch(tail, 1)
    down_grad = scatter_bit(down_grad, 0, row, "m", 1)
    pair_got = lax.all_to_all(pair_rows, ("q",), 0, 0, tiled=True)
    out_final = to_rows(out_all)
    norm_keep, norm_send, w_keep, w_send = run_kernel(
        mixer_backward_taps,
        "mixer_backward_taps",
        (du, grad_lin, grad_z, flags, taps, p_pad, pos, normed, w_cat, swiglu_part),
        [
            ((blocks_all, span, width), BF16),
            ((blocks_all, span, width), BF16),
            ((blocks_all, rows_all, 5 * HEAD), BF16),
            ((blocks_all, rows_all, 5 * HEAD), BF16),
        ],
        [((length, 5 * HEAD), BF16), ((16, HEAD), F32)],
        12,
        (6,),
    )

    tail, down_grad, pair_got, out_final, norm_send, w_send = together(
        tail, down_grad, pair_got, out_final, norm_send, w_send
    )
    tail = scatter_bit(tail, 0, row, "m", 1)
    norm_got = swap(norm_send, "c", 1)
    w_got = swap(w_send, "c", 1)
    norm_own, *norm_send = run_kernel(
        token_pieces,
        "token_pieces",
        (pos, norm_keep, norm_got),
        [slabs_wide] + [slabs] * (chips - 1),
        [],
        1,
        (0,),
    )
    (value,) = run_kernel(
        merge_heads,
        "merge_heads",
        (pos, w_keep, w_got),
        [((blocks_all, rows_all, 9 * HEAD), BF16)],
        [],
        1,
        (0,),
    )
    norm_send, value, tail = together(norm_send, value, tail)
    norm_got = [swap(v, "q", d + 1) for d, v in enumerate(norm_send)]
    value = scatter_batch(value.reshape(blocks_all, n_batch, rows_w, 9 * HEAD), 1)
    gate_grad, up_grad = run_kernel(
        spread_pair,
        "spread_pair",
        (pair_got,),
        [(gate_weight.shape[:1] + (chips * ff_here,), F32)] * 2,
        [],
        2,
    )
    value = scatter_bit(value.reshape(micro, chips, rows_w, 9 * HEAD), 0, row, "m", 1)
    (grad_own,) = run_kernel(
        input_gradient,
        "input_gradient",
        (pos, grad_resid, x_own, gains, norm_own, *norm_got),
        [slabs],
        [],
        1,
        (0,),
    )
    grad_final = to_rows(grad_own)
    head_rows = tail[rows_w:, : 9 * HEAD]
    head_rows = jnp.pad(head_rows, ((0, 0), (0, 9 * HEAD - head_rows.shape[1])))
    head_rows = jnp.broadcast_to(head_rows, (chips,) + head_rows.shape)
    value = jnp.concatenate([value, head_rows], axis=1).astype(BF16)
    *merged, beta_sum, gain_sums, tap_sums, head_sum = run_kernel(
        spread_heads,
        "spread_heads",
        (pos, *to_chips(value)),
        [((rows_w, width), F32)] * 4
        + [((rows_w, HEADS), F32), ((8, rows_w), F32), ((3 * CONV, rows_w), F32), ((1, HEAD), F32)],
        [((HEAD, HEAD), F32)],
        1,
        (0,),
    )
    return (
        out_final,
        grad_final,
        merged[0],
        merged[1],
        merged[2],
        beta_sum,
        merged[3],
        tail[:rows_w],
        gate_grad,
        up_grad,
        down_grad,
        gain_sums[0],
        gain_sums[1],
        head_sum[0],
        tap_sums,
    )


def pick_of(pos, chips):
    lane = lax.broadcasted_iota(jnp.int32, (1, HEAD), 1)
    return (lane == head_of(pos, chips)).astype(F32)


def solution(mesh):
    n_seq, n_batch = mesh.shape["seq"], mesh.shape["batch"]

    def program(*arrays):
        micro = arrays[0].shape[0]
        shape = (micro, n_seq // (2 * micro), 2, n_batch)
        fine = Mesh(mesh.devices.reshape(shape), ("m", "q", "c", "b"))
        seq, every = ("m", "q", "c"), ("m", "q", "c", "b")
        tokens, rows, vector, taps = P(None, "b", seq, None), P(every, None), P(every), P(None, every)
        return jax.shard_map(
            on_device,
            mesh=fine,
            in_specs=(tokens, tokens, P(None, "b", None))
            + (rows,) * 9
            + (vector, vector, P(), taps),
            out_specs=(tokens, tokens) + (rows,) * 9 + (vector, vector, P(), taps),
            check_vma=False,
        )(*arrays)

    return program
```

```python
from functools import partial

import jax
import jax.numpy as jnp
from jax import lax
from jax.experimental import pallas as pl
from jax.experimental.pallas import tpu as pltpu
from jax.sharding import Mesh, PartitionSpec as P

HEADS = 8
HEAD = 128
CONV = 4
EPSILON = 1e-05
UNIT_EPSILON = 1e-06
CHUNK = 128
GROUP = 4
FREE = 24
COST = 10**6
VMEM_BYTES = 56 * 1024 * 1024
F32 = jnp.float32
BF16 = jnp.bfloat16
NN = (((1,), (0,)), ((), ()))
NT = (((1,), (1,)), ((), ()))
TN = (((0,), (0,)), ((), ()))


def split(value):
    high = value.astype(BF16)
    return (high, (value - high.astype(F32)).astype(BF16))


def mm(left, right, dims):
    def dot(a, b):
        return lax.dot_general(a, b, dims, preferred_element_type=F32)

    return dot(left[0], right[0]) + (dot(left[0], right[1]) + dot(left[1], right[0]))


def block_mask(size, width):
    row = lax.broadcasted_iota(jnp.int32, (size, size), 0)
    col = lax.broadcasted_iota(jnp.int32, (size, size), 1)
    return (row // width) == (col // width)


def tri_masks(size):
    row = lax.broadcasted_iota(jnp.int32, (size, size), 0)
    col = lax.broadcasted_iota(jnp.int32, (size, size), 1)
    return (row > col, row >= col, row == col)


def unit_lower_inverses(mats):
    size = mats[0].shape[0]
    eye = tri_masks(size)[2].astype(F32)
    near = block_mask(size, 8)
    base = [split(jnp.where(near, m, 0.0)) for m in mats]
    square = [split(mm(b, b, NN)) for b in base]
    first = [eye - jnp.where(near, m, 0.0) for m in mats]
    second = [f + mm(split(f), s, NN) for f, s in zip(first, square)]
    fourth = [split(mm(s, s, NN)) for s in square]
    inverse = [f + mm(split(f), s, NN) for f, s in zip(second, fourth)]
    width = 8
    while width < size:
        inside, wider = block_mask(size, width), block_mask(size, 2 * width)
        cut = jnp.logical_and(wider, jnp.logical_not(inside))
        off = [split(jnp.where(cut, m, 0.0)) for m in mats]
        halves = [split(t) for t in inverse]
        step = [split(mm(t, o, NN)) for t, o in zip(halves, off)]
        inverse = [t - mm(s, h, NN) for t, s, h in zip(inverse, step, halves)]
        width *= 2
    return inverse


def views(ref):
    return [ref.at[i] for i in range(ref.shape[0])]


def place_of(pos_ref):
    return (pos_ref[0], pos_ref[1], pos_ref[2], pos_ref[3])


def head_of(pos_ref, chips):
    return pos_ref[2] * (HEADS // 2) + pos_ref[1] // (chips // (HEADS // 2))


def pack_heads(
    pos_ref, wq_ref, wk_ref, wv_ref, wg_ref, beta_ref, mixer_ref, swiglu_ref, conv_ref, *refs
):
    *out_refs, here_ref, side_ref, sems = refs
    chips = len(out_refs)
    repeat = chips // (HEADS // 2)
    copies = [
        pltpu.make_async_copy(ref, here_ref.at[t], sems.at[t])
        for t, ref in enumerate((wq_ref, wk_ref, wv_ref, wg_ref))
    ]
    for copy in copies:
        copy.start()
    rows, conv = here_ref.shape[1], HEADS + 2
    side_ref[...] = jnp.zeros(side_ref.shape, F32)
    side_ref[0:HEADS, 0:rows] = beta_ref[...].astype(F32)
    side_ref[HEADS : HEADS + 1, 0:rows] = mixer_ref[...].astype(F32)
    side_ref[HEADS + 1 : conv, 0:rows] = swiglu_ref[...].astype(F32)
    side_ref[conv : conv + 3 * CONV, 0:rows] = conv_ref[...].astype(F32)
    across = jnp.transpose(side_ref[...])
    side_ref[...] = across
    small = side_ref[0:rows, :].astype(BF16)
    for out_ref in out_refs:
        out_ref[:, 8 * HEAD :] = small
    for t, copy in enumerate(copies):
        copy.wait()
        for d, out_ref in enumerate(out_refs):
            slot = (pos_ref[1] ^ d) // repeat
            for i in range(2):
                cols = pl.ds(pl.multiple_of((i * (HEADS // 2) + slot) * HEAD, HEAD), HEAD)
                spot = (4 * i + t) * HEAD
                out_ref[:, spot : spot + HEAD] = here_ref[t, :, cols]


def mixer_forward(
    pos_ref,
    xown_ref,
    xsib_ref,
    wown_ref,
    wsib_ref,
    flag_ref,
    idc_ref,
    idr_ref,
    gain_ref,
    heads_ref,
    tap_ref,
    gains_ref,
    normed_out,
    wcat_out,
    p_out,
    kept_out,
    slope_out,
    found_out,
    shape_out,
    across_ref,
    normed_ref,
    wcat_ref,
    p_ref,
    kept_ref,
    slope_ref,
    found_ref,
    shape_ref,
    brief_ref,
    sems,
):
    qh_ref, k_ref, lin_ref, beta_ref, t_ref, sc_ref, map_ref = views(kept_ref)
    sq_ref, sk_ref, sv_ref = views(slope_ref)
    v_ref, pb_ref, w_ref, add_ref = views(brief_ref)
    state_ref, ps_ref, er_ref = views(found_ref)
    oh_ref, ro_ref = views(shape_ref)
    copies = []

    def send(i, source, target):
        copies.append(pltpu.make_async_copy(source, target, sems.at[i]))
        copies[-1].start()

    chips, _, span, width = xown_ref.shape
    length = normed_ref.shape[0]
    count = length // CHUNK
    strict, incl, _ = tri_masks(CHUNK)
    m, q, c, _ = place_of(pos_ref)
    head = head_of(pos_ref, chips)
    rows_here = wown_ref.shape[1]
    for i in range(wown_ref.shape[0]):
        block = (m ^ (i // chips)) * chips + (q ^ (i % chips))
        mine = pl.ds(pl.multiple_of((2 * block + c) * rows_here, rows_here), rows_here)
        theirs = pl.ds(pl.multiple_of((2 * block + 1 - c) * rows_here, rows_here), rows_here)
        cols = pl.ds(pl.multiple_of(c * 4 * HEAD, 4 * HEAD), 4 * HEAD)
        wcat_ref[mine, 0 : 4 * HEAD] = wown_ref[i, :, cols]
        wcat_ref[mine, 4 * HEAD :] = wown_ref[i, :, 8 * HEAD :]
        wcat_ref[theirs, :] = wsib_ref[i, :, :]
    for i in range(width // HEAD):
        rows = slice(i * HEAD, (i + 1) * HEAD)
        across_ref[:, rows] = jnp.transpose(wcat_ref[rows, 4 * HEAD :].astype(F32))
    gain = across_ref[HEADS : HEADS + 1, :]
    gains_ref[...] = across_ref[HEADS : HEADS + 8, :]
    mine = pl.ds(pl.multiple_of(head * HEAD, HEAD), HEAD)
    tap_ref[...] = across_ref[HEADS + 2 : HEADS + 18, mine]
    for i in range(2 * chips):
        block = (m ^ (i % 2)) * chips + (q ^ (i // 2))
        for which, ref in ((c, xown_ref), (1 - c, xsib_ref)):
            x = ref[i // 2, i % 2, :, :].astype(F32)
            scale = lax.rsqrt(jnp.mean(x * x, axis=-1, keepdims=True) + EPSILON)
            spot = pl.ds(pl.multiple_of((2 * block + which) * span, span), span)
            normed_ref[spot, :] = (x * scale * gain).astype(BF16)
    lane = lax.broadcasted_iota(jnp.int32, (1, HEAD), 1)
    pick = (lane == head).astype(F32)
    p_ref[0:8, :] = jnp.zeros((8, 3 * HEAD), F32)

    tall = 4 * CHUNK
    for n in range(length // tall):
        rows = slice(n * tall, (n + 1) * tall)
        y = lax.dot_general(normed_ref[rows, :], wcat_ref[...], NN, preferred_element_type=F32)
        p_ref[8 + n * tall : 8 + (n + 1) * tall, :] = y[:, 0 : 3 * HEAD].astype(BF16).astype(F32)
        lin_ref[rows, :] = y[:, 3 * HEAD : 4 * HEAD]
        logit = jnp.sum(y[:, 4 * HEAD :] * pick, axis=-1, keepdims=True)
        beta_ref[rows, :] = jnp.broadcast_to(jax.nn.sigmoid(logit), (tall, HEAD))
    for n in range(count):
        r0 = n * CHUNK
        rows = slice(r0, r0 + CHUNK)
        keep = [None] + [flag_ref[rows, j : j + 1] for j in range(CONV - 1)]
        for c in range(3):
            cols = slice(c * HEAD, (c + 1) * HEAD)
            pre = tap_ref[4 * c : 4 * c + 1, :] * p_ref[8 + r0 : 8 + r0 + CHUNK, cols]
            for j in range(1, CONV):
                moved = p_ref[8 + r0 - j : 8 + r0 - j + CHUNK, cols]
                pre = pre + tap_ref[4 * c + j : 4 * c + j + 1, :] * moved * keep[j]
            sig = jax.nn.sigmoid(pre)
            act = pre * sig
            slope = sig * (1.0 + pre * (1.0 - sig))
            if c == 2:
                v_ref[rows, :] = act
                sv_ref[rows, :] = slope
            else:
                scale = lax.rsqrt(jnp.sum(act * act, axis=-1, keepdims=True) + UNIT_EPSILON)
                (qh_ref if c == 0 else k_ref)[rows, :] = act * scale
                (sq_ref if c == 0 else sk_ref)[rows, :] = slope * scale
    send(0, normed_ref, normed_out)
    send(1, wcat_ref, wcat_out)
    send(2, p_ref, p_out)
    send(3, slope_ref, slope_out)
    send(4, kept_ref.at[0:4], kept_out.at[0:4])

    def prepare(group, carry):
        spots = [pl.multiple_of((group * GROUP + i) * CHUNK, CHUNK) for i in range(GROUP)]
        rows = [pl.ds(s, CHUNK) for s in spots]
        key = [split(k_ref[r, :]) for r in rows]
        same = [
            idc_ref[r, :] == idr_ref[group * GROUP + i, :, :] for i, r in enumerate(rows)
        ]
        beta = [beta_ref[r, :] for r in rows]
        mats = [
            jnp.where(jnp.logical_and(s, strict), b * mm(k, k, NT), 0.0)
            for s, b, k in zip(same, beta, key)
        ]
        inverse = unit_lower_inverses(mats)
        for i, r in enumerate(rows):
            t_ref[r, :] = inverse[i]
            inv = split(inverse[i])
            pseudo = mm(inv, split(beta[i] * v_ref[r, :]), NN)
            weighed = split(
                mm(inv, split(beta[i] * flag_ref[r, 3:4] * k_ref[r, :]), NN)
            )
            ends = split(flag_ref[r, 4:5] * k_ref[r, :])
            query = split(qh_ref[r, :] * HEAD ** (-0.5))
            sc_ref[r, :] = jnp.where(
                jnp.logical_and(same[i], incl), mm(query, key[i], NT), 0.0
            )
            pb_ref[r, :] = pseudo
            w_ref[r, :] = weighed[0].astype(F32) + weighed[1].astype(F32)
            map_ref[r, :] = mm(weighed, ends, TN)
            add_ref[r, :] = mm(split(pseudo), ends, TN)
        return carry

    lax.fori_loop(0, count // GROUP, prepare, 0)
    send(5, kept_ref.at[4:7], kept_out.at[4:7])

    state = jnp.zeros((HEAD, HEAD), F32)
    for n in range(count):
        rows = slice(n * CHUNK, (n + 1) * CHUNK)
        state_ref[rows, :] = state
        last = flag_ref[(n + 1) * CHUNK - 1 : (n + 1) * CHUNK, 3:4]
        state = last * state - mm(split(state), split(map_ref[rows, :]), NN) + add_ref[rows, :]

    def produce(group, carry):
        for i in range(GROUP):
            r = pl.ds(pl.multiple_of((group * GROUP + i) * CHUNK, CHUNK), CHUNK)
            same = idc_ref[r, :] == idr_ref[group * GROUP + i, :, :]
            key = split(k_ref[r, :])
            state_i = split(state_ref[r, :])
            flag = flag_ref[r, 3:4]
            pseudo = pb_ref[r, :] - mm(split(w_ref[r, :]), state_i, NT)
            ps_ref[r, :] = pseudo
            halves = split(pseudo)
            gram = jnp.where(jnp.logical_and(same, strict), mm(key, key, NT), 0.0)
            er_ref[r, :] = (
                v_ref[r, :] - flag * mm(key, state_i, NT) - mm(split(gram), halves, NN)
            )
            query = split(qh_ref[r, :] * HEAD ** (-0.5))
            out = flag * mm(query, state_i, NT) + mm(split(sc_ref[r, :]), halves, NN)
            scale = lax.rsqrt(jnp.mean(out * out, axis=-1, keepdims=True) + EPSILON)
            hat = out * scale
            oh_ref[r, :] = hat
            ro_ref[r, :] = jnp.broadcast_to(scale, (CHUNK, HEAD))
            lin = lin_ref[r, :]
            made = (hat * gain_ref[...] * (lin * jax.nn.sigmoid(lin))).astype(BF16)
            half = CHUNK // 2
            spot = pl.ds(pl.multiple_of((group * GROUP + i) * half, half), half)
            for chip in range(heads_ref.shape[0]):
                heads_ref[chip, 0, spot, :] = made[:half]
                heads_ref[chip, 1, spot, :] = made[half:]
        return carry

    lax.fori_loop(0, count // GROUP, produce, 0)
    send(6, found_ref, found_out)
    send(7, shape_ref, shape_out)
    for copy in copies:
        copy.wait()


def head_fold(rows):
    row = lax.broadcasted_iota(jnp.int32, (HEAD, HEAD), 0)
    lane = lax.broadcasted_iota(jnp.int32, (HEAD, HEAD), 1)
    return (lane // (HEAD // rows) == row % rows).astype(F32)


def head_place(rows):
    row = lax.broadcasted_iota(jnp.int32, (HEAD, HEAD), 0)
    lane = lax.broadcasted_iota(jnp.int32, (HEAD, HEAD), 1)
    return (lane == FREE + row % (HEAD // rows)).astype(F32)


def mixer_backward(
    small_rows,
    pos_ref,
    dh_ref,
    flag_ref,
    idc_ref,
    idr_ref,
    gain_ref,
    tap_ref,
    swiglu_ref,
    kept_in,
    shape_in,
    found_in,
    slope_in,
    p_in,
    normed_in,
    wcat_in,
    dnkeep_ref,
    dnsend_ref,
    dwkeep_ref,
    dwsend_ref,
    kept_ref,
    shape_ref,
    found_ref,
    slope_ref,
    p_ref,
    normed_ref,
    wcat_ref,
    back3_ref,
    back_ref,
    du_ref,
    dcat_ref,
    tapgrad_ref,
    headgrad_ref,
    sems,
):
    copies = [
        pltpu.make_async_copy(source, target, sems.at[i])
        for i, (source, target) in enumerate(
            (
                (kept_in, kept_ref),
                (shape_in, shape_ref),
                (found_in, found_ref),
                (slope_in, slope_ref),
                (p_in, p_ref),
                (normed_in, normed_ref),
                (wcat_in, wcat_ref),
            )
        )
    ]
    for copy in copies:
        copy.start()
    qh_ref, k_ref, lin_ref, beta_ref, t_ref, sc_ref, map_ref = views(kept_ref)
    sq_ref, sk_ref, sv_ref = views(slope_ref)
    state_ref, ps_ref, er_ref = views(found_ref)
    oh_ref, ro_ref = views(shape_ref)
    do_ref, dpre_ref, dstate_ref = views(back3_ref)
    length = lin_ref.shape[0]
    blocks, rows_here, _ = dwkeep_ref.shape
    chips = blocks // 2
    repeat = chips // (HEADS // 2)
    span = length // (2 * blocks)
    core, share = pos_ref[2], pos_ref[1] % repeat
    head = head_of(pos_ref, chips)
    lane = lax.broadcasted_iota(jnp.int32, (1, HEAD), 1)
    pick = (lane == head).astype(F32)
    strict, incl, _ = tri_masks(CHUNK)
    copies[0].wait()
    copies[1].wait()
    count = length // CHUNK
    scale_q = HEAD ** (-0.5)
    headgrad_ref[...] = jnp.zeros(headgrad_ref.shape, F32)

    def first(group, carry):
        for i in range(GROUP):
            r = pl.ds(pl.multiple_of((group * GROUP + i) * CHUNK, CHUNK), CHUNK)
            block = group * GROUP + i
            pair = [dh_ref[2 * (block % chips) + j, block // chips, :, :] for j in range(2)]
            grad = jnp.concatenate(pair, axis=0).astype(F32)
            lin = lin_ref[r, :]
            sig = jax.nn.sigmoid(lin)
            swish = lin * sig
            hat = oh_ref[r, :]
            gain = gain_ref[...]
            both = grad * hat
            headgrad_ref[0:1, :] += jnp.sum(both * swish, axis=0, keepdims=True)
            dcat_ref[r, 3 * HEAD : 4 * HEAD] = (
                both * gain * (sig * (1.0 + lin * (1.0 - sig)))
            ).astype(BF16)
            lead = grad * gain * swish
            grad_out = ro_ref[r, :] * (
                lead - hat * jnp.mean(lead * hat, axis=-1, keepdims=True)
            )
            do_ref[r, :] = grad_out
            flag = flag_ref[r, 3:4]
            direct = mm(split(sc_ref[r, :]), split(grad_out), TN)
            dpre_ref[r, :] = direct
            zed = mm(split(t_ref[r, :]), split(direct), TN)
            back_ref[r, :] = mm(
                split(flag * grad_out), split(qh_ref[r, :] * scale_q), TN
            ) - mm(split(beta_ref[r, :] * flag * zed), split(k_ref[r, :]), TN)
        return carry

    lax.fori_loop(0, count // GROUP, first, 0)
    grad_state = jnp.zeros((HEAD, HEAD), F32)
    for n in reversed(range(count)):
        rows = slice(n * CHUNK, (n + 1) * CHUNK)
        dstate_ref[rows, :] = grad_state
        last = flag_ref[(n + 1) * CHUNK - 1 : (n + 1) * CHUNK, 3:4]
        grad_state = (
            last * grad_state
            - mm(split(grad_state), split(map_ref[rows, :]), NT)
            + back_ref[rows, :]
        )
    copies[2].wait()
    copies[3].wait()
    du_ref[length : length + 8, :] = jnp.zeros((8, 3 * HEAD), F32)

    def second(group, carry):
        for i in range(GROUP):
            r = pl.ds(pl.multiple_of((group * GROUP + i) * CHUNK, CHUNK), CHUNK)
            same = idc_ref[r, :] == idr_ref[group * GROUP + i, :, :]
            low = jnp.logical_and(same, strict)
            full = jnp.logical_and(same, incl)
            flag = flag_ref[r, 3:4]
            ends = flag_ref[r, 4:5]
            beta = beta_ref[r, :]
            key_f = k_ref[r, :]
            key = split(key_f)
            q_hat = qh_ref[r, :]
            query = split(q_hat * scale_q)
            state_i = split(state_ref[r, :])
            dstate = split(dstate_ref[r, :])
            grad_out = split(do_ref[r, :])
            pseudo = split(ps_ref[r, :])
            dpre = dpre_ref[r, :] + ends * mm(key, dstate, NT)
            zed = mm(split(t_ref[r, :]), split(dpre), TN)
            zeds = split(zed)
            dscore = split(jnp.where(full, mm(grad_out, pseudo, NT), 0.0))
            grad_q = flag * mm(grad_out, state_i, NN) + mm(dscore, key, NN)
            dgram = split(jnp.where(low, -beta * mm(zeds, pseudo, NT), 0.0))
            grad_v = beta * zed
            grad_k = (
                mm(dscore, query, TN)
                + ends * mm(pseudo, dstate, NN)
                + mm(dgram, key, NN)
                + mm(dgram, key, TN)
                - flag * mm(split(grad_v), state_i, NN)
            )
            grad_b = jnp.sum(zed * er_ref[r, :], axis=-1, keepdims=True)
            dz = grad_b * beta * (1.0 - beta)
            dcat_ref[r, 4 * HEAD : 5 * HEAD] = (dz * pick).astype(BF16)
            lead = scale_q * grad_q
            du_ref[r, 0:HEAD] = sq_ref[r, :] * (
                lead - q_hat * jnp.sum(lead * q_hat, axis=-1, keepdims=True)
            )
            du_ref[r, HEAD : 2 * HEAD] = sk_ref[r, :] * (
                grad_k - key_f * jnp.sum(grad_k * key_f, axis=-1, keepdims=True)
            )
            du_ref[r, 2 * HEAD : 3 * HEAD] = sv_ref[r, :] * grad_v
        return carry

    lax.fori_loop(0, count // GROUP, second, 0)
    copies[4].wait()
    sums = [[jnp.zeros((1, HEAD), F32) for _ in range(CONV)] for _ in range(3)]
    for n in range(count):
        r0 = n * CHUNK
        rows = slice(r0, r0 + CHUNK)
        for c in range(3):
            cols = slice(c * HEAD, (c + 1) * HEAD)
            here = du_ref[rows, cols]
            grad = tap_ref[4 * c : 4 * c + 1, :] * here
            sums[c][0] += jnp.sum(
                here * p_ref[8 + r0 : 8 + r0 + CHUNK, cols], axis=0, keepdims=True
            )
            for j in range(1, CONV):
                after = slice(r0 + j, r0 + j + CHUNK)
                grad = grad + tap_ref[4 * c + j : 4 * c + j + 1, :] * (
                    du_ref[after, cols] * flag_ref[after, j - 1 : j]
                )
                moved = p_ref[8 + r0 - j : 8 + r0 - j + CHUNK, cols]
                sums[c][j] += jnp.sum(
                    here * flag_ref[rows, j - 1 : j] * moved, axis=0, keepdims=True
                )
            dcat_ref[rows, cols] = grad.astype(BF16)
    tapgrad_ref[...] = jnp.concatenate(
        [sums[c][j] for c in range(3) for j in range(CONV)]
        + [jnp.zeros((4, HEAD), F32)],
        axis=0,
    )
    if repeat > 1:
        for n in range(count):
            counts = (n % chips % repeat == share).astype(F32)
            rows = slice(n * CHUNK, (n + 1) * CHUNK)
            dcat_ref[rows, :] = (dcat_ref[rows, :].astype(F32) * counts).astype(BF16)
        tapgrad_ref[...] = tapgrad_ref[...] * (share == 0).astype(F32)
    width = normed_ref.shape[1]
    copies[5].wait()
    copies[6].wait()

    tall = 4 * CHUNK
    for n in range(length // tall):
        rows = slice(n * tall, (n + 1) * tall)
        part = lax.dot_general(dcat_ref[rows, :], wcat_ref[...], NT, preferred_element_type=F32)
        for j in range(4):
            low = part[2 * j * span : (2 * j + 1) * span]
            high = part[(2 * j + 1) * span : (2 * j + 2) * span]
            dnkeep_ref[4 * n + j, :, :] = jnp.where(core == 1, high, low).astype(BF16)
            dnsend_ref[4 * n + j, :, :] = jnp.where(core == 1, low, high).astype(BF16)
    fold, place = head_fold(small_rows), head_place(small_rows)
    total = headgrad_ref[0:1, :] * (share == 0).astype(F32)
    spread = mm(split(fold * total), split(place), NN)
    for i in range(width // HEAD):
        cols = slice(i * HEAD, (i + 1) * HEAD)
        if i % 4 == 0:
            wide = slice(i * HEAD, (i + 4) * HEAD)
            four = lax.dot_general(
                normed_ref[:, wide], dcat_ref[...], TN, preferred_element_type=F32
            )
        grad = four[i % 4 * HEAD : (i % 4 + 1) * HEAD]
        mats = wcat_ref[cols, :].astype(F32)
        gain = mats[:, 4 * HEAD + HEADS : 4 * HEAD + HEADS + 1]
        gain_grad = jnp.sum(grad * mats, axis=-1, keepdims=True) / gain
        here = (head == i).astype(F32)
        lines = jnp.concatenate(
            [
                jnp.zeros((HEADS, HEAD), F32),
                jnp.zeros((1, HEAD), F32),
                swiglu_ref[0:1, cols],
                tapgrad_ref[0 : 3 * CONV, :] * here,
                jnp.zeros((HEAD - HEADS - 2 - 3 * CONV, HEAD), F32),
            ],
            axis=0,
        )
        lane = lax.broadcasted_iota(jnp.int32, (1, HEAD), 1)
        small = (
            grad[:, 4 * HEAD :] + jnp.transpose(lines) + gain_grad * (lane == HEADS) + spread
        )
        grad = jnp.concatenate([grad[:, : 4 * HEAD], small], axis=1)
        per = HEAD // (2 * rows_here)
        for j in range(per):
            low = grad[2 * j * rows_here : (2 * j + 1) * rows_here]
            high = grad[(2 * j + 1) * rows_here : (2 * j + 2) * rows_here]
            dwkeep_ref[i * per + j, :, :] = jnp.where(core == 1, high, low).astype(BF16)
            dwsend_ref[i * per + j, :, :] = jnp.where(core == 1, low, high).astype(BF16)


def feed_forward(
    pos_ref,
    got_ref,
    xown_ref,
    cot_ref,
    oown_ref,
    osib_ref,
    pown_ref,
    psib_ref,
    down_ref,
    gains_ref,
    wo_ref,
    normed_ref,
    grads_ref,
    hidden_ref,
    cots_ref,
    swiglu_ref,
    res_ref,
    norm_ref,
    *rest,
):
    chips, _, span, width = xown_ref.shape
    send_refs, (wp_ref, heads_ref, total_ref, hat_ref, part_ref) = rest[: chips - 1], rest[chips - 1 :]
    repeat = chips // (HEADS // 2)
    tokens = 2 * chips * span
    ff = down_ref.shape[0]
    m, q, c, _ = place_of(pos_ref)
    rows_here = oown_ref.shape[2]
    for i in range(2 * chips):
        d, e = i // 2, i % 2
        block = (m ^ e) * chips + (q ^ d)
        other = (m ^ e) * chips + d
        for which, o_ref, p_ref in ((c, oown_ref, pown_ref), (1 - c, osib_ref, psib_ref)):
            spot = pl.ds(pl.multiple_of((2 * other + which) * rows_here, rows_here), rows_here)
            wo_ref[spot, :] = o_ref[d, e, :, :]
            wp_ref[spot, :] = p_ref[e, d, :, :]
        spot = pl.ds(pl.multiple_of(block * span, span), span)
        cots_ref[spot, :] = cot_ref[d, e, :, :]
        total_ref[spot, :] = xown_ref[d, e, :, :].astype(F32)
    for i in range(2):
        for j in range(HEADS // 2):
            h = i * (HEADS // 2) + j
            heads_ref[:, h * HEAD : (h + 1) * HEAD] = got_ref[2 * j * repeat + i, :, :]
    total = total_ref[...] + lax.dot_general(
        heads_ref[...], wo_ref[...], NN, preferred_element_type=F32
    )
    total_ref[...] = total
    scale = lax.rsqrt(jnp.mean(total * total, axis=-1, keepdims=True) + EPSILON)
    hat = total * scale
    hat_ref[...] = hat
    normed_ref[...] = (hat * gains_ref[1:2, :]).astype(BF16)
    both = lax.dot_general(normed_ref[...], wp_ref[...], NN, preferred_element_type=F32)
    gate, up = both[:, :ff], both[:, ff:]
    sig = jax.nn.sigmoid(gate)
    act = gate * sig
    hidden_ref[...] = (act * up).astype(BF16)
    back = lax.dot_general(cots_ref[...], down_ref[...], NT, preferred_element_type=F32)
    slope = sig * (1.0 + gate * (1.0 - sig))
    grads_ref[...] = jnp.concatenate([back * up * slope, back * act], axis=1).astype(BF16)
    part_ref[...] = lax.dot_general(grads_ref[...], wp_ref[...], NT, preferred_element_type=F32)
    total = jnp.sum(part_ref[...] * hat_ref[...], axis=0, keepdims=True)
    swiglu_ref[...] = jnp.broadcast_to(total, swiglu_ref.shape)
    for e in range(2):
        spot = pl.ds(pl.multiple_of((e * chips + q) * span, span), span)
        res_ref[e, :, :] = total_ref[spot, :]
        norm_ref[e, :, :] = part_ref[spot, :]
        for d, send_ref in enumerate(send_refs):
            spot = pl.ds(pl.multiple_of((e * chips + (q ^ (d + 1))) * span, span), span)
            send_ref[e, :, :] = part_ref[spot, :].astype(BF16)


def feed_forward_grads(
    pos_ref, normed_ref, grads_ref, hidden_ref, cots_ref, down_ref,
    keep_ref, send_ref, downkeep_ref, downsend_ref, out_ref,
):
    rows_here = keep_ref.shape[1]
    chips, _, span, _ = out_ref.shape
    core = pos_ref[2]
    per = HEAD // (2 * rows_here)
    for i in range(normed_ref.shape[1] // HEAD):
        if i % 4 == 0:
            wide = slice(i * HEAD, (i + 4) * HEAD)
            four = lax.dot_general(
                normed_ref[:, wide], grads_ref[...], TN, preferred_element_type=F32
            )
        grad = four[i % 4 * HEAD : (i % 4 + 1) * HEAD]
        for j in range(per):
            low = grad[2 * j * rows_here : (2 * j + 1) * rows_here]
            high = grad[(2 * j + 1) * rows_here : (2 * j + 2) * rows_here]
            keep_ref[i * per + j, :, :] = jnp.where(core == 1, high, low).astype(BF16)
            send_ref[i * per + j, :, :] = jnp.where(core == 1, low, high).astype(BF16)
    down = lax.dot_general(hidden_ref[...], cots_ref[...], TN, preferred_element_type=F32)
    rows = downkeep_ref.shape[1]
    for e in range(2):
        low = down[2 * e * rows : (2 * e + 1) * rows]
        high = down[(2 * e + 1) * rows : (2 * e + 2) * rows]
        downkeep_ref[e, :, :] = jnp.where(core == 1, high, low).astype(BF16)
        downsend_ref[e, :, :] = jnp.where(core == 1, low, high).astype(BF16)
    out = lax.dot_general(hidden_ref[...], down_ref[...], NN, preferred_element_type=F32)
    for e in range(2):
        for j in range(chips):
            spot = (e * chips + j) * span
            out_ref[j, e, :, :] = out[spot : spot + span].astype(BF16)


def branch_gradient(pos_ref, norm_ref, res_ref, cot_ref, gains_ref, wo_ref, *rest):
    *got_refs, resid_ref, branch_ref, heads_ref = rest
    m = pos_ref[0]
    chips = heads_ref.shape[0] // 2
    repeat = chips // (HEADS // 2)
    branches = []
    for e in range(2):
        norm = norm_ref[e, :, :]
        for got_ref in got_refs:
            norm = norm + got_ref[e, :, :].astype(F32)
        res = res_ref[e, :, :]
        scale = lax.rsqrt(jnp.mean(res * res, axis=-1, keepdims=True) + EPSILON)
        hat = res * scale
        lead = norm * gains_ref[1:2, :]
        grad = cot_ref[0, m ^ e, :, :].astype(F32) + scale * (
            lead - hat * jnp.mean(lead * hat, axis=-1, keepdims=True)
        )
        resid_ref[e, :, :] = grad
        branch = grad.astype(BF16)
        branch_ref[e, :, :] = branch
        branches.append(branch)
    back = lax.dot_general(
        jnp.concatenate(branches, axis=0), wo_ref[...], NT, preferred_element_type=F32
    ).astype(BF16)
    span = branch_ref.shape[1]
    for e in range(2):
        for j in range(chips):
            for i in range(2):
                h = i * (HEADS // 2) + j // repeat
                heads_ref[2 * j + i, e, :, :] = back[
                    e * span : (e + 1) * span, h * HEAD : (h + 1) * HEAD
                ]


def output_gradient(pos_ref, got_ref, *refs):
    *branch_refs, all_ref, rows_ref, duo_ref = refs
    chips = len(branch_refs)
    span = branch_refs[0].shape[1]
    repeat = chips // (HEADS // 2)
    q = pos_ref[1]
    share = q % repeat
    for d, branch_ref in enumerate(branch_refs):
        for e in range(2):
            spot = pl.ds(pl.multiple_of((e * chips + (q ^ d)) * span, span), span)
            value = branch_ref[e, :, :]
            if repeat > 1:
                counts = ((q ^ d) % repeat == share).astype(F32)
                value = (value.astype(F32) * counts).astype(BF16)
            rows_ref[spot, :] = value
    first = pl.multiple_of((q // repeat) * 2 * repeat, 2)
    for i in range(2):
        duo_ref[:, i * HEAD : (i + 1) * HEAD] = got_ref[first + i, :, :]
    both = lax.dot_general(duo_ref[...], rows_ref[...], TN, preferred_element_type=F32)
    for i in range(2):
        all_ref[i, :, :] = both[i * HEAD : (i + 1) * HEAD].astype(BF16)


def input_gradient(pos_ref, resid_ref, x_ref, gains_ref, got_ref, out_ref):
    m = pos_ref[0]
    for e in range(2):
        norm = got_ref[0, e, :, :].astype(F32)
        for j in range(1, got_ref.shape[0]):
            norm = norm + got_ref[j, e, :, :].astype(F32)
        x = x_ref[m ^ e, :, :].astype(F32)
        scale = lax.rsqrt(jnp.mean(x * x, axis=-1, keepdims=True) + EPSILON)
        hat = x * scale
        lead = norm * gains_ref[0:1, :]
        out_ref[e, :, :] = (
            resid_ref[e, :, :]
            + scale * (lead - hat * jnp.mean(lead * hat, axis=-1, keepdims=True))
        ).astype(BF16)


def token_pieces(keep_ref, got_ref, out_ref):
    chips = out_ref.shape[0]
    for e in range(2):
        for j in range(chips):
            block = e * chips + j
            out_ref[j, e, :, :] = (
                keep_ref[block, :, :].astype(F32) + got_ref[block, :, :].astype(F32)
            ).astype(BF16)


def merge_heads(pos_ref, keep_ref, got_ref, *out_refs):
    m, _, core, batch = place_of(pos_ref)
    wide = 4 * HEAD

    def merge(out_ref, keep, got):
        out_ref[..., :wide] = jnp.where(core == 1, got[..., :wide], keep[..., :wide])
        out_ref[..., wide : 2 * wide] = jnp.where(core == 1, keep[..., :wide], got[..., :wide])
        out_ref[..., 2 * wide :] = (
            keep[..., wide:].astype(F32) + got[..., wide:].astype(F32)
        ).astype(BF16)

    if len(out_refs) == 1:
        merge(out_refs[0], keep_ref[...], got_ref[...])
        return
    chips, rows, _ = out_refs[0].shape
    for i, out_ref in enumerate(out_refs):
        spot = pl.ds(pl.multiple_of((batch ^ (i % 2)) * rows, rows), rows)
        for j in range(chips):
            block = (m ^ (i // 2)) * chips + j
            merge(out_ref.at[j], keep_ref[block, spot, :], got_ref[block, spot, :])


def add_partners(pos_ref, *refs):
    in_refs, out_refs = refs[:4], refs[4:]
    for d, out_ref in enumerate(out_refs):
        j = pos_ref[1] ^ d
        total = in_refs[0][j, :, :].astype(F32)
        for in_ref in in_refs[1:]:
            total = total + in_ref[j, :, :].astype(F32)
        out_ref[...] = total.astype(BF16)


def spread_heads(pos_ref, *refs):
    *got_refs, wq_ref, wk_ref, wv_ref, wg_ref, beta_ref, gains_ref, taps_ref, head_ref, side_ref = refs
    chips = len(got_refs)
    repeat = chips // (HEADS // 2)
    rows = wq_ref.shape[0]
    small = jnp.zeros((rows, HEAD), F32)
    if repeat > 1:
        for ref in (wq_ref, wk_ref, wv_ref, wg_ref):
            ref[...] = jnp.zeros(ref.shape, F32)
    for d, got_ref in enumerate(got_refs):
        slot = (pos_ref[1] ^ d) // repeat
        for i in range(2):
            cols = pl.ds(pl.multiple_of((i * (HEADS // 2) + slot) * HEAD, HEAD), HEAD)
            for t, ref in enumerate((wq_ref, wk_ref, wv_ref, wg_ref)):
                spot = (4 * i + t) * HEAD
                value = got_ref[0:rows, spot : spot + HEAD].astype(F32)
                ref[:, cols] = value + ref[:, cols] if repeat > 1 else value
        small = small + got_ref[0:rows, 8 * HEAD :].astype(F32)
    side_ref[...] = jnp.zeros(side_ref.shape, F32)
    side_ref[0:rows, :] = small
    across = jnp.transpose(side_ref[...])
    beta_ref[...] = across[:HEADS, :rows]
    gains_ref[...] = across[HEADS : HEADS + 8, :rows]
    taps_ref[...] = across[HEADS + 2 : HEADS + 2 + 3 * CONV, :rows]
    found = mm(split(side_ref[...]), split(head_place(rows)), NT)
    first = lax.broadcasted_iota(jnp.int32, (HEAD, HEAD), 0) < rows
    head_ref[...] = jnp.sum(
        jnp.where(first, found * head_fold(rows), 0.0), axis=0, keepdims=True
    )


def spread_pair(got_ref, gate_ref, up_ref):
    chips, _, wide = got_ref.shape
    wide = wide // 4
    for j in range(chips):
        got = got_ref[j, :, :].astype(F32)
        for t, ref in enumerate((gate_ref, up_ref)):
            for e in range(2):
                part = (2 * t + e) * wide
                spot = (e * chips + j) * wide
                ref[:, spot : spot + wide] = got[:, part : part + wide]


VMEM_SPEC = pl.BlockSpec(memory_space=pltpu.VMEM)


def run_kernel(body, name, operands, out_shapes, scratch, micros, scalars=(), stays=(), leaves=()):
    specs = [VMEM_SPEC] * len(operands)
    for i in scalars:
        specs[i] = pl.BlockSpec(memory_space=pltpu.SMEM)
    for i in stays:
        specs[i] = pl.BlockSpec(memory_space=pl.ANY)
    room = [pltpu.VMEM(*s) for s in scratch]
    if stays or leaves:
        room.append(pltpu.SemaphoreType.DMA((len(stays) + len(leaves) + 1,)))
    outs = [VMEM_SPEC] * len(out_shapes)
    for i in leaves:
        outs[i] = pl.BlockSpec(memory_space=pl.ANY)
    return pl.pallas_call(
        body,
        name=name,
        out_shape=[jax.ShapeDtypeStruct(*s) for s in out_shapes],
        in_specs=specs,
        out_specs=outs,
        scratch_shapes=room,
        compiler_params=pltpu.CompilerParams(vmem_limit_bytes=VMEM_BYTES),
        cost_estimate=pl.CostEstimate(
            flops=micros * COST, bytes_accessed=1 << 10, transcendentals=0
        ),
    )(*operands)


def tie(value, *others):
    return lax.optimization_barrier((value,) + others)[0]


def together(*values):
    return lax.optimization_barrier(values)


def swap(value, axis, mask):
    return lax.ppermute(value, axis, [(i, i ^ mask) for i in range(lax.axis_size(axis))])


def ordered(bit, mine, other):
    flag = bit == 1
    return (jnp.where(flag, other, mine), jnp.where(flag, mine, other))


def from_chips(value):
    return [value] + [swap(value, "q", d) for d in range(1, lax.axis_size("q"))]


def to_chips(blocks):
    chip = lax.axis_index("q")
    mine = [lax.dynamic_index_in_dim(blocks, chip ^ d, 0, keepdims=False) for d in range(blocks.shape[0])]
    return [mine[0]] + [swap(mine[d], "q", d) for d in range(1, len(mine))]


def gather_batch_start(value, axis):
    step, batch = 1, lax.axis_index("b")
    lead, rows = value.shape[:axis], value.shape[axis:]
    while 2 * step < lax.axis_size("b"):
        got = swap(value, "b", step)
        value = jnp.stack(ordered((batch // step) % 2, value, got), axis=axis)
        step *= 2
    value = value.reshape(lead + (step * rows[0],) + rows[1:])
    return value, swap(value, "b", step)


def gather_batch_end(value, got, axis):
    lead, rows = value.shape[:axis], value.shape[axis:]
    high = lax.axis_index("b") // (lax.axis_size("b") // 2) == 1
    value = jnp.stack(ordered(high.astype(jnp.int32), value, got), axis=axis)
    return value.reshape(lead + (2 * rows[0],) + rows[1:])


def gather_batch(value, axis):
    return gather_batch_end(*gather_batch_start(value, axis), axis)


def scatter_bit(value, axis, bit, mesh_axis, mask):
    low, high = (lax.index_in_dim(value, i, axis, keepdims=False) for i in (0, 1))
    flag = bit == 1
    keep, send = jnp.where(flag, high, low), jnp.where(flag, low, high)
    return keep.astype(F32) + swap(send.astype(BF16), mesh_axis, mask).astype(F32)


def scatter_batch(value, axis, left=1):
    batch, step = lax.axis_index("b"), lax.axis_size("b") // 2
    while step >= left:
        shape = value.shape
        value = value.reshape(shape[:axis] + (2, shape[axis] // 2) + shape[axis + 1 :])
        value = scatter_bit(value, axis, (batch // step) % 2, "b", step)
        step //= 2
    return lax.squeeze(value, (axis,)) if left == 1 else value


def token_flags(ids):
    length = ids.shape[0]
    padded = jnp.concatenate([jnp.full((CONV - 1,), -1, jnp.int32), ids])
    by_chunk = ids.reshape(length // CHUNK, CHUNK)
    before = jnp.concatenate([jnp.full((1,), -1, jnp.int32), by_chunk[:-1, -1]])
    columns = [padded[CONV - 1 - j : CONV - 1 - j + length] == ids for j in range(1, CONV)]
    columns.append((by_chunk == before[:, None]).reshape(length))
    columns.append((by_chunk == by_chunk[:, -1:]).reshape(length))
    flags = jnp.stack(columns, axis=1).astype(F32)
    return jnp.pad(flags, ((0, 8), (0, 3))), by_chunk[:, None, :], ids[:, None]


def on_device(
    inputs,
    cotangent,
    document_ids,
    query_weight,
    key_weight,
    value_weight,
    beta_weight,
    outgate_weight,
    output_weight,
    gate_weight,
    up_weight,
    down_weight,
    mixer_gain,
    swiglu_gain,
    head_gain,
    conv_weight,
):
    micro, _, span, width = inputs.shape
    chips, n_batch = lax.axis_size("q"), lax.axis_size("b")
    half_heads = HEADS // 2
    repeat = chips // half_heads
    length = micro * chips * 2 * span
    rows_w = query_weight.shape[0]
    rows_f = down_weight.shape[0]
    rows_all = n_batch * rows_w
    blocks_all = micro * chips
    ff_here = rows_f * micro * 2 * n_batch
    row, chip, core = lax.axis_index("m"), lax.axis_index("q"), lax.axis_index("c")
    share = chip % repeat
    flag_row = row == 1
    pos = jnp.stack([row, chip, core, lax.axis_index("b")]).astype(jnp.int32)

    mine = run_kernel(
        pack_heads,
        "pack_heads",
        (pos, query_weight, key_weight, value_weight, outgate_weight, beta_weight.T)
        + (mixer_gain[None, :], swiglu_gain[None, :], conv_weight),
        [((rows_w, 9 * HEAD), BF16)] * chips,
        [((4, rows_w, width), BF16), ((HEAD, HEAD), F32)],
        1,
        (0,),
        (1, 2, 3, 4),
    )
    head_s = [swap(mine[d], "q", d) for d in range(1, chips)]

    def own_slab(value):
        return jnp.where(flag_row, value[1], value[0])

    def away_slab(value):
        return jnp.where(flag_row, value[0], value[1])

    x_s = swap(away_slab(inputs[:, 0]), "m", 1)
    head_s, x_s = together(head_s, x_s)
    head_q = jnp.stack([mine[0]] + head_s, axis=0)
    x_own = jnp.stack([own_slab(inputs[:, 0]), x_s], axis=0)
    head_m = jnp.stack([head_q, swap(head_q, "m", 1)], axis=0)
    x_half = jnp.stack(from_chips(x_own), axis=0)
    out_s = swap(tie(output_weight, x_s), "m", 1)
    ids = own_slab(document_ids[:, 0])
    flags, id_rows, id_cols = token_flags(ids)
    gain_vec = head_gain.astype(F32)[None, :]
    pair = jnp.stack([gate_weight, up_weight], axis=1).reshape(
        rows_w, 2, micro, chips, 2 * n_batch * rows_f
    )
    pair = jnp.moveaxis(pair, 3, 0).reshape(chips, rows_w, 2 * ff_here)
    cot_away = away_slab(cotangent[:, 0])
    head_m, x_half, out_s, flags, id_rows, id_cols, gain_vec, pair, cot_away = together(
        head_m, x_half, out_s, flags, id_rows, id_cols, gain_vec, pair, cot_away
    )
    head_b = gather_batch(head_m.reshape(blocks_all, rows_w, 9 * HEAD), 1)
    x_sib = swap(x_half, "c", 1)
    cot_s = swap(cot_away, "m", 1)
    down_s = swap(tie(down_weight, x_half), "m", 1)
    out_b = gather_batch(jnp.stack([output_weight, out_s], axis=0), 1)
    pair_q = lax.all_to_all(pair, ("q",), 0, 0, tiled=True)
    head_b, x_sib, cot_s, down_s, out_b, pair_q = together(
        head_b, x_sib, cot_s, down_s, out_b, pair_q
    )
    send = lax.dynamic_slice_in_dim(head_b, (1 - core) * 4 * HEAD, 4 * HEAD, 2)
    head_sib = swap(jnp.concatenate([send, head_b[..., 8 * HEAD :]], axis=-1), "c", 1)
    pair_s = swap(pair_q, "m", 1)
    cot_own = jnp.stack([own_slab(cotangent[:, 0]), cot_s], axis=0)
    down_m, down_got = gather_batch_start(jnp.stack(ordered(row, down_weight, down_s), axis=0), 1)
    out_q = lax.all_to_all(
        jnp.broadcast_to(out_b, (chips,) + out_b.shape), ("q",), 0, 0, tiled=True
    )
    cot_got = [swap(cot_own, "q", d) for d in range(1, chips)]

    count = length // CHUNK
    def tall(n):
        return ((n, length, HEAD), F32)

    slabs = ((2, span, width), BF16)
    slabs_wide = ((2, span, width), F32)
    saved = [
        ((length, width), BF16),
        ((width, 5 * HEAD), BF16),
        ((length + 8, 3 * HEAD), F32),
        tall(7),
        tall(3),
        tall(3),
        tall(2),
    ]
    heads_here, taps, gains, normed, w_cat, p_pad, kept, slopes, found, shaped = run_kernel(
        mixer_forward,
        "mixer_forward",
        (pos, x_half, x_sib, head_b, head_sib, flags, id_cols, id_rows, gain_vec),
        [((chips, 2, length // 2, HEAD), BF16), ((16, HEAD), F32), ((8, width), F32)] + saved,
        [((HEAD, width), F32)] + saved + [tall(4)],
        25,
        (0,),
        (),
        tuple(range(3, 10)),
    )
    pair_s, down_got, out_q, cot_got = tie((pair_s, down_got, out_q, cot_got), heads_here)

    got_heads = lax.all_to_all(
        heads_here.reshape(chips * 2, length // 2, HEAD), ("q", "c"), 0, 0, tiled=True
    )
    pair_m = jnp.stack([pair_q, pair_s], axis=0).reshape(blocks_all, rows_w, 2 * ff_here)
    pair_b = gather_batch(pair_m, 1).reshape(micro, chips, rows_all, 2 * ff_here)
    cot_half = jnp.stack([cot_own] + cot_got, axis=0)
    down_b = gather_batch_end(down_m, down_got, 1)
    out_sib = swap(out_q, "c", 1)
    down_sib = swap(down_b, "c", 1)
    pair_sib = swap(pair_b, "c", 1)
    w_down = jnp.stack(ordered(core, down_b, down_sib), axis=1).reshape(ff_here, width)
    half = length // 2
    w_out, normed_two, pair_up, hidden, cot_rows, swiglu_part, res_own, norm_own, *norm_send = run_kernel(
        feed_forward,
        "feed_forward",
        (pos, got_heads, x_half, cot_half, out_q, out_sib, pair_b, pair_sib, w_down, gains),
        [
            ((width, width), BF16),
            ((half, width), BF16),
            ((half, 2 * ff_here), BF16),
            ((half, ff_here), BF16),
            ((half, width), BF16),
            ((8, width), F32),
            slabs_wide,
            slabs_wide,
        ]
        + [slabs] * (chips - 1),
        [
            ((width, 2 * ff_here), BF16),
            ((half, width), BF16),
            ((half, width), F32),
            ((half, width), F32),
            ((half, width), F32),
        ],
        12,
        (0,),
    )
    norm_got = [swap(v, "q", d + 1) for d, v in enumerate(norm_send)]
    pair_keep, pair_send, down_keep, down_send, out_part = run_kernel(
        feed_forward_grads,
        "feed_forward_grads",
        (pos, normed_two, pair_up, hidden, cot_rows, w_down),
        [
            ((blocks_all, rows_all, 2 * ff_here), BF16),
            ((blocks_all, rows_all, 2 * ff_here), BF16),
            ((micro, n_batch * rows_f, width), BF16),
            ((micro, n_batch * rows_f, width), BF16),
            ((chips, 2, span, width), BF16),
        ],
        [],
        6,
        (0,),
    )
    norm_got, norm_own, pair_send, down_send = together(norm_got, norm_own, pair_send, down_send)
    grad_resid, grad_branch, grad_heads = run_kernel(
        branch_gradient,
        "branch_gradient",
        (pos, norm_own, res_own, cot_own[None], gains, w_out, *norm_got),
        [slabs_wide, slabs, ((chips * 2, 2, span, HEAD), BF16)],
        [],
        2,
        (0,),
    )

    pair_got = swap(pair_send, "c", 1)
    down_got = swap(down_send, "c", 1)
    dheads = lax.all_to_all(grad_heads, ("q", "c"), 0, 0, tiled=True)
    grad_branch, pair_got, down_got = together(grad_branch, pair_got, down_got)
    pair_grad = (pair_keep.astype(F32) + pair_got.astype(F32)).astype(BF16)
    down_grad = (down_keep.astype(F32) + down_got.astype(F32)).astype(BF16)
    down_grad = down_grad.reshape(micro, n_batch, rows_f, width)
    dheads, pair_grad, down_grad, grad_branch, out_part = together(
        dheads, pair_grad, down_grad, grad_branch, out_part
    )
    out_got = lax.all_to_all(out_part, ("q",), 0, 0, tiled=True)
    branch_got = [swap(grad_branch, "q", d) for d in range(1, chips)]
    pair_grad = pair_grad.reshape(micro, chips, n_batch, rows_w, 2 * ff_here)
    pair_keep = lax.dynamic_index_in_dim(pair_grad, row, 0, keepdims=False)
    pair_got = swap(lax.dynamic_index_in_dim(pair_grad, 1 - row, 0, keepdims=False), "m", 1)
    down_grad = scatter_batch(down_grad, 1)

    def to_rows(value):
        keep = jnp.where(flag_row, value[1], value[0])
        send = jnp.where(flag_row, value[0], value[1])
        return jnp.stack(ordered(row, keep, swap(send, "m", 1)), axis=0)[:, None]

    blocks_out = ((blocks_all, span, width), BF16)
    weights_out = ((blocks_all, rows_all, 5 * HEAD), BF16)
    norm_keep, norm_send, w_keep, w_send = run_kernel(
        partial(mixer_backward, rows_w),
        "mixer_backward",
        (pos, dheads, flags, id_cols, id_rows, gain_vec, taps, swiglu_part)
        + (kept, shaped, found, slopes, p_pad, normed, w_cat),
        [blocks_out, blocks_out, weights_out, weights_out],
        [saved[i] for i in (3, 6, 5, 4, 2, 0, 1)]
        + [
            tall(3),
            ((length, HEAD), F32),
            ((length + 8, 3 * HEAD), F32),
            ((length, 5 * HEAD), BF16),
            ((16, HEAD), F32),
            ((8, HEAD), F32),
        ],
        25,
        (0,),
        tuple(range(8, 15)),
    )
    pair_got, down_grad, branch_got, out_got, w_send, norm_send = together(
        pair_got, down_grad, branch_got, out_got, w_send, norm_send
    )

    norm_got = swap(norm_send, "c", 1)
    w_got = swap(w_send, "c", 1)
    (out_rows,) = run_kernel(
        output_gradient,
        "output_gradient",
        (pos, got_heads, grad_branch, *branch_got),
        [((2, HEAD, width), BF16)],
        [((half, width), BF16), ((half, 2 * HEAD), BF16)],
        1,
        (0,),
    )
    w_got, out_rows = together(w_got, out_rows)
    piece = ((chips, rows_w, 9 * HEAD), BF16)
    if n_batch == 2:
        value = run_kernel(
            merge_heads, "merge_heads", (pos, w_keep, w_got), [piece] * 4, [], 1, (0,)
        )
    else:
        merged_all = ((blocks_all, rows_all, 9 * HEAD), BF16)
        (value,) = run_kernel(
            merge_heads, "merge_heads", (pos, w_keep, w_got), [merged_all], [], 1, (0,)
        )
        value = value.reshape(blocks_all, n_batch, rows_w, 9 * HEAD)
        value = scatter_batch(value, 1, 2).reshape(micro, chips, 2, rows_w, 9 * HEAD)
        batch = lax.axis_index("b") % 2
        value = [
            lax.dynamic_index_in_dim(
                lax.dynamic_index_in_dim(value, row ^ (i // 2), 0, keepdims=False),
                batch ^ (i % 2),
                1,
                keepdims=False,
            ).astype(BF16)
            for i in range(4)
        ]
    value, norm_got, out_rows, pair_got = together(value, norm_got, out_rows, pair_got)
    (norm_send,) = run_kernel(
        token_pieces,
        "token_pieces",
        (norm_keep, norm_got),
        [((chips, 2, span, width), BF16)],
        [],
        1,
    )
    step = repeat // 2
    while step >= 1:
        out_rows = out_rows.reshape(micro, 2, out_rows.shape[1] // 2, width)
        out_rows = scatter_bit(out_rows, 1, (share // step) % 2, "q", step)
        step //= 2
    out_rows = out_rows.reshape(micro, 2, n_batch, rows_w, width)
    norm_got = lax.all_to_all(norm_send, ("q",), 0, 0, tiled=True)
    value_got = [
        swap(value[1], "b", 1),
        swap(value[2], "m", 1),
        swap(value[3], ("m", "b"), n_batch + 1),
    ]
    pair_rows = (pair_keep.astype(F32) + pair_got.astype(F32)).astype(BF16)
    pair_rows = scatter_batch(pair_rows, 1)
    out_rows = scatter_bit(out_rows, 1, core, "c", 1)
    norm_got, pair_rows, out_rows = together(norm_got, pair_rows, out_rows)
    pair_got = lax.all_to_all(pair_rows.astype(BF16), ("q",), 0, 0, tiled=True)
    out_rows = scatter_batch(out_rows, 1)
    (grad_own,) = run_kernel(
        input_gradient,
        "input_gradient",
        (pos, grad_resid, x_own, gains, norm_got),
        [slabs],
        [],
        1,
        (0,),
    )
    grad_final = to_rows(grad_own)
    value_got, out_rows, down_grad, out_got = together(value_got, out_rows, down_grad, out_got)
    head_got = run_kernel(
        add_partners,
        "add_partners",
        (pos, value[0], *value_got),
        [((rows_w, 9 * HEAD), BF16)] * chips,
        [],
        1,
        (0,),
    )
    head_got = [head_got[0]] + [swap(head_got[d], "q", d) for d in range(1, chips)]
    outproj_grad = scatter_bit(out_rows, 0, row, "m", 1)
    down_grad = scatter_bit(down_grad, 0, row, "m", 1)
    out_all = (res_own + jnp.sum(out_got.astype(F32), axis=0)).astype(BF16)
    out_final = to_rows(out_all)
    gate_grad, up_grad = run_kernel(
        spread_pair,
        "spread_pair",
        (pair_got,),
        [(gate_weight.shape[:1] + (chips * ff_here,), F32)] * 2,
        [],
        2,
    )
    *merged, beta_sum, gain_sums, tap_sums, head_sum = run_kernel(
        spread_heads,
        "spread_heads",
        (pos, *head_got),
        [((rows_w, width), F32)] * 4
        + [((HEADS, rows_w), F32), ((8, rows_w), F32), ((3 * CONV, rows_w), F32), ((1, HEAD), F32)],
        [((HEAD, HEAD), F32)],
        1,
        (0,),
    )
    return (
        out_final,
        grad_final,
        merged[0],
        merged[1],
        merged[2],
        beta_sum.T,
        merged[3],
        outproj_grad,
        gate_grad,
        up_grad,
        down_grad,
        gain_sums[0],
        gain_sums[1],
        head_sum[0],
        tap_sums,
    )


def solution(mesh):
    n_seq, n_batch = mesh.shape["seq"], mesh.shape["batch"]

    def program(*arrays):
        micro = arrays[0].shape[0]
        shape = (micro, n_seq // (2 * micro), 2, n_batch)
        fine = Mesh(mesh.devices.reshape(shape), ("m", "q", "c", "b"))
        seq, every = ("m", "q", "c"), ("m", "q", "c", "b")
        tokens, rows, vector, taps = P(None, "b", seq, None), P(every, None), P(every), P(None, every)
        return jax.shard_map(
            on_device,
            mesh=fine,
            in_specs=(tokens, tokens, P(None, "b", None))
            + (rows,) * 9
            + (vector, vector, P(), taps),
            out_specs=(tokens, tokens) + (rows,) * 9 + (vector, vector, P(), taps),
            check_vma=False,
        )(*arrays)

    return program
```

```python
from functools import partial

import jax
import jax.numpy as jnp
from jax import lax
from jax.experimental import pallas as pl
from jax.experimental.pallas import tpu as pltpu
from jax.sharding import Mesh, PartitionSpec as P

HEADS = 8
HEAD = 128
CONV = 4
EPSILON = 1e-05
UNIT_EPSILON = 1e-06
CHUNK = 128
GROUP = 4
FREE = 24
COST = 10**6
MEGA = 1024 * 1024
VMEM_BYTES = 56 * MEGA
ROOM = {"branch_gradient": 12, "output_gradient": 12, "token_pieces": 12, "merge_heads": 12, "add_partners": 12, "input_gradient": 12, "spread_heads": 12, "spread_pair": 12, "feed_forward": 32, "feed_forward_grads": 24}
F32 = jnp.float32
BF16 = jnp.bfloat16
NN = (((1,), (0,)), ((), ()))
NT = (((1,), (1,)), ((), ()))
TN = (((0,), (0,)), ((), ()))


def split(value):
    high = value.astype(BF16)
    return (high, (value - high.astype(F32)).astype(BF16))


def mm(left, right, dims):
    def dot(a, b):
        return lax.dot_general(a, b, dims, preferred_element_type=F32)

    return dot(left[0], right[0]) + (dot(left[0], right[1]) + dot(left[1], right[0]))


def block_mask(size, width):
    row = lax.broadcasted_iota(jnp.int32, (size, size), 0)
    col = lax.broadcasted_iota(jnp.int32, (size, size), 1)
    return (row // width) == (col // width)


def tri_masks(size):
    row = lax.broadcasted_iota(jnp.int32, (size, size), 0)
    col = lax.broadcasted_iota(jnp.int32, (size, size), 1)
    return (row > col, row >= col, row == col)


def unit_lower_inverses(mats):
    size = mats[0].shape[0]
    eye = tri_masks(size)[2].astype(F32)
    near = block_mask(size, 8)
    base = [split(jnp.where(near, m, 0.0)) for m in mats]
    square = [split(mm(b, b, NN)) for b in base]
    first = [eye - jnp.where(near, m, 0.0) for m in mats]
    second = [f + mm(split(f), s, NN) for f, s in zip(first, square)]
    fourth = [split(mm(s, s, NN)) for s in square]
    inverse = [f + mm(split(f), s, NN) for f, s in zip(second, fourth)]
    width = 8
    while width < size:
        inside, wider = block_mask(size, width), block_mask(size, 2 * width)
        cut = jnp.logical_and(wider, jnp.logical_not(inside))
        off = [split(jnp.where(cut, m, 0.0)) for m in mats]
        halves = [split(t) for t in inverse]
        step = [split(mm(t, o, NN)) for t, o in zip(halves, off)]
        inverse = [t - mm(s, h, NN) for t, s, h in zip(inverse, step, halves)]
        width *= 2
    return inverse


def views(ref):
    return [ref.at[i] for i in range(ref.shape[0])]


def place_of(pos_ref):
    return (pos_ref[0], pos_ref[1], pos_ref[2], pos_ref[3])


def head_of(pos_ref, chips):
    return pos_ref[2] * (HEADS // 2) + pos_ref[1] // (chips // (HEADS // 2))


def pack_heads(
    pos_ref, wq_ref, wk_ref, wv_ref, wg_ref, beta_ref, mixer_ref, swiglu_ref, conv_ref, *refs
):
    *out_refs, here_ref, side_ref, sems = refs
    chips = len(out_refs)
    repeat = chips // (HEADS // 2)
    copies = [
        pltpu.make_async_copy(ref, here_ref.at[t], sems.at[t])
        for t, ref in enumerate((wq_ref, wk_ref, wv_ref, wg_ref))
    ]
    for copy in copies:
        copy.start()
    rows, conv = here_ref.shape[1], HEADS + 2
    side_ref[...] = jnp.zeros(side_ref.shape, F32)
    side_ref[0:HEADS, 0:rows] = beta_ref[...].astype(F32)
    side_ref[HEADS : HEADS + 1, 0:rows] = mixer_ref[...].astype(F32)
    side_ref[HEADS + 1 : conv, 0:rows] = swiglu_ref[...].astype(F32)
    side_ref[conv : conv + 3 * CONV, 0:rows] = conv_ref[...].astype(F32)
    across = jnp.transpose(side_ref[...])
    side_ref[...] = across
    small = side_ref[0:rows, :].astype(BF16)
    for out_ref in out_refs:
        out_ref[:, 8 * HEAD :] = small
    for t, copy in enumerate(copies):
        copy.wait()
        for d, out_ref in enumerate(out_refs):
            slot = (pos_ref[1] ^ d) // repeat
            for i in range(2):
                cols = pl.ds(pl.multiple_of((i * (HEADS // 2) + slot) * HEAD, HEAD), HEAD)
                spot = (4 * i + t) * HEAD
                out_ref[:, spot : spot + HEAD] = here_ref[t, :, cols]


def mixer_forward(
    pos_ref,
    xown_ref,
    xsib_ref,
    wown_ref,
    wsib_ref,
    flag_ref,
    idc_ref,
    idr_ref,
    gain_ref,
    heads_ref,
    tap_ref,
    gains_ref,
    normed_out,
    wcat_out,
    p_out,
    kept_out,
    slope_out,
    found_out,
    shape_out,
    across_ref,
    normed_ref,
    wcat_ref,
    p_ref,
    kept_ref,
    slope_ref,
    found_ref,
    shape_ref,
    brief_ref,
    sems,
):
    qh_ref, k_ref, lin_ref, beta_ref, t_ref, sc_ref, map_ref = views(kept_ref)
    sq_ref, sk_ref, sv_ref = views(slope_ref)
    v_ref, pb_ref, w_ref, add_ref = views(brief_ref)
    state_ref, ps_ref, er_ref = views(found_ref)
    oh_ref, ro_ref = views(shape_ref)
    copies = []

    def send(i, source, target):
        copies.append(pltpu.make_async_copy(source, target, sems.at[i]))
        copies[-1].start()

    chips, _, span, width = xown_ref.shape
    length = normed_ref.shape[0]
    count = length // CHUNK
    strict, incl, _ = tri_masks(CHUNK)
    m, q, c, _ = place_of(pos_ref)
    head = head_of(pos_ref, chips)
    rows_here = wown_ref.shape[1]
    for i in range(wown_ref.shape[0]):
        block = (m ^ (i // chips)) * chips + (q ^ (i % chips))
        mine = pl.ds(pl.multiple_of((2 * block + c) * rows_here, rows_here), rows_here)
        theirs = pl.ds(pl.multiple_of((2 * block + 1 - c) * rows_here, rows_here), rows_here)
        cols = pl.ds(pl.multiple_of(c * 4 * HEAD, 4 * HEAD), 4 * HEAD)
        wcat_ref[mine, 0 : 4 * HEAD] = wown_ref[i, :, cols]
        wcat_ref[mine, 4 * HEAD :] = wown_ref[i, :, 8 * HEAD :]
        wcat_ref[theirs, :] = wsib_ref[i, :, :]
    for i in range(width // HEAD):
        rows = slice(i * HEAD, (i + 1) * HEAD)
        across_ref[:, rows] = jnp.transpose(wcat_ref[rows, 4 * HEAD :].astype(F32))
    gain = across_ref[HEADS : HEADS + 1, :]
    gains_ref[...] = across_ref[HEADS : HEADS + 8, :]
    mine = pl.ds(pl.multiple_of(head * HEAD, HEAD), HEAD)
    tap_ref[...] = across_ref[HEADS + 2 : HEADS + 18, mine]
    for i in range(2 * chips):
        block = (m ^ (i % 2)) * chips + (q ^ (i // 2))
        for which, ref in ((c, xown_ref), (1 - c, xsib_ref)):
            x = ref[i // 2, i % 2, :, :].astype(F32)
            scale = lax.rsqrt(jnp.mean(x * x, axis=-1, keepdims=True) + EPSILON)
            spot = pl.ds(pl.multiple_of((2 * block + which) * span, span), span)
            normed_ref[spot, :] = (x * scale * gain).astype(BF16)
    lane = lax.broadcasted_iota(jnp.int32, (1, HEAD), 1)
    pick = (lane == head).astype(F32)
    p_ref[0:8, :] = jnp.zeros((8, 3 * HEAD), F32)

    tall = 4 * CHUNK
    for n in range(length // tall):
        rows = slice(n * tall, (n + 1) * tall)
        y = lax.dot_general(normed_ref[rows, :], wcat_ref[...], NN, preferred_element_type=F32)
        p_ref[8 + n * tall : 8 + (n + 1) * tall, :] = y[:, 0 : 3 * HEAD].astype(BF16).astype(F32)
        lin_ref[rows, :] = y[:, 3 * HEAD : 4 * HEAD]
        logit = jnp.sum(y[:, 4 * HEAD :] * pick, axis=-1, keepdims=True)
        beta_ref[rows, :] = jnp.broadcast_to(jax.nn.sigmoid(logit), (tall, HEAD))
    for n in range(count):
        r0 = n * CHUNK
        rows = slice(r0, r0 + CHUNK)
        keep = [None] + [flag_ref[rows, j : j + 1] for j in range(CONV - 1)]
        for c in range(3):
            cols = slice(c * HEAD, (c + 1) * HEAD)
            pre = tap_ref[4 * c : 4 * c + 1, :] * p_ref[8 + r0 : 8 + r0 + CHUNK, cols]
            for j in range(1, CONV):
                moved = p_ref[8 + r0 - j : 8 + r0 - j + CHUNK, cols]
                pre = pre + tap_ref[4 * c + j : 4 * c + j + 1, :] * moved * keep[j]
            sig = jax.nn.sigmoid(pre)
            act = pre * sig
            slope = sig * (1.0 + pre * (1.0 - sig))
            if c == 2:
                v_ref[rows, :] = act
                sv_ref[rows, :] = slope
            else:
                scale = lax.rsqrt(jnp.sum(act * act, axis=-1, keepdims=True) + UNIT_EPSILON)
                (qh_ref if c == 0 else k_ref)[rows, :] = act * scale
                (sq_ref if c == 0 else sk_ref)[rows, :] = slope * scale
    send(0, normed_ref, normed_out)
    send(1, wcat_ref, wcat_out)
    send(2, p_ref, p_out)
    send(3, slope_ref, slope_out)
    send(4, kept_ref.at[0:4], kept_out.at[0:4])

    def prepare(group, carry):
        spots = [pl.multiple_of((group * GROUP + i) * CHUNK, CHUNK) for i in range(GROUP)]
        rows = [pl.ds(s, CHUNK) for s in spots]
        key = [split(k_ref[r, :]) for r in rows]
        same = [
            idc_ref[r, :] == idr_ref[group * GROUP + i, :, :] for i, r in enumerate(rows)
        ]
        beta = [beta_ref[r, :] for r in rows]
        mats = [
            jnp.where(jnp.logical_and(s, strict), b * mm(k, k, NT), 0.0)
            for s, b, k in zip(same, beta, key)
        ]
        inverse = unit_lower_inverses(mats)
        for i, r in enumerate(rows):
            t_ref[r, :] = inverse[i]
            inv = split(inverse[i])
            pseudo = mm(inv, split(beta[i] * v_ref[r, :]), NN)
            weighed = split(
                mm(inv, split(beta[i] * flag_ref[r, 3:4] * k_ref[r, :]), NN)
            )
            ends = split(flag_ref[r, 4:5] * k_ref[r, :])
            query = split(qh_ref[r, :] * HEAD ** (-0.5))
            sc_ref[r, :] = jnp.where(
                jnp.logical_and(same[i], incl), mm(query, key[i], NT), 0.0
            )
            pb_ref[r, :] = pseudo
            w_ref[r, :] = weighed[0].astype(F32) + weighed[1].astype(F32)
            map_ref[r, :] = mm(weighed, ends, TN)
            add_ref[r, :] = mm(split(pseudo), ends, TN)
        return carry

    lax.fori_loop(0, count // GROUP, prepare, 0)
    send(5, kept_ref.at[4:7], kept_out.at[4:7])

    state = jnp.zeros((HEAD, HEAD), F32)
    for n in range(count):
        rows = slice(n * CHUNK, (n + 1) * CHUNK)
        state_ref[rows, :] = state
        last = flag_ref[(n + 1) * CHUNK - 1 : (n + 1) * CHUNK, 3:4]
        state = last * state - mm(split(state), split(map_ref[rows, :]), NN) + add_ref[rows, :]

    def produce(group, carry):
        for i in range(GROUP):
            r = pl.ds(pl.multiple_of((group * GROUP + i) * CHUNK, CHUNK), CHUNK)
            same = idc_ref[r, :] == idr_ref[group * GROUP + i, :, :]
            key = split(k_ref[r, :])
            state_i = split(state_ref[r, :])
            flag = flag_ref[r, 3:4]
            pseudo = pb_ref[r, :] - mm(split(w_ref[r, :]), state_i, NT)
            ps_ref[r, :] = pseudo
            halves = split(pseudo)
            gram = jnp.where(jnp.logical_and(same, strict), mm(key, key, NT), 0.0)
            er_ref[r, :] = (
                v_ref[r, :] - flag * mm(key, state_i, NT) - mm(split(gram), halves, NN)
            )
            query = split(qh_ref[r, :] * HEAD ** (-0.5))
            out = flag * mm(query, state_i, NT) + mm(split(sc_ref[r, :]), halves, NN)
            scale = lax.rsqrt(jnp.mean(out * out, axis=-1, keepdims=True) + EPSILON)
            hat = out * scale
            oh_ref[r, :] = hat
            ro_ref[r, :] = jnp.broadcast_to(scale, (CHUNK, HEAD))
            lin = lin_ref[r, :]
            made = (hat * gain_ref[...] * (lin * jax.nn.sigmoid(lin))).astype(BF16)
            half = CHUNK // 2
            spot = pl.ds(pl.multiple_of((group * GROUP + i) * half, half), half)
            for chip in range(heads_ref.shape[0]):
                heads_ref[chip, 0, spot, :] = made[:half]
                heads_ref[chip, 1, spot, :] = made[half:]
        return carry

    lax.fori_loop(0, count // GROUP, produce, 0)
    send(6, found_ref, found_out)
    send(7, shape_ref, shape_out)
    for copy in copies:
        copy.wait()


def head_fold(rows):
    row = lax.broadcasted_iota(jnp.int32, (HEAD, HEAD), 0)
    lane = lax.broadcasted_iota(jnp.int32, (HEAD, HEAD), 1)
    return (lane // (HEAD // rows) == row % rows).astype(F32)


def head_place(rows):
    row = lax.broadcasted_iota(jnp.int32, (HEAD, HEAD), 0)
    lane = lax.broadcasted_iota(jnp.int32, (HEAD, HEAD), 1)
    return (lane == FREE + row % (HEAD // rows)).astype(F32)


def mixer_backward(
    small_rows,
    pos_ref,
    dh_ref,
    flag_ref,
    idc_ref,
    idr_ref,
    gain_ref,
    tap_ref,
    swiglu_ref,
    kept_in,
    shape_in,
    found_in,
    slope_in,
    p_in,
    normed_in,
    wcat_in,
    dnkeep_ref,
    dnsend_ref,
    dwkeep_ref,
    dwsend_ref,
    kept_ref,
    shape_ref,
    found_ref,
    slope_ref,
    p_ref,
    normed_ref,
    wcat_ref,
    back3_ref,
    back_ref,
    du_ref,
    dcat_ref,
    tapgrad_ref,
    headgrad_ref,
    sems,
):
    copies = [
        pltpu.make_async_copy(source, target, sems.at[i])
        for i, (source, target) in enumerate(
            (
                (kept_in, kept_ref),
                (shape_in, shape_ref),
                (found_in, found_ref),
                (slope_in, slope_ref),
                (p_in, p_ref),
                (normed_in, normed_ref),
                (wcat_in, wcat_ref),
            )
        )
    ]
    for copy in copies:
        copy.start()
    qh_ref, k_ref, lin_ref, beta_ref, t_ref, sc_ref, map_ref = views(kept_ref)
    sq_ref, sk_ref, sv_ref = views(slope_ref)
    state_ref, ps_ref, er_ref = views(found_ref)
    oh_ref, ro_ref = views(shape_ref)
    do_ref, dpre_ref, dstate_ref = views(back3_ref)
    length = lin_ref.shape[0]
    blocks, rows_here, _ = dwkeep_ref.shape
    chips = blocks // 2
    repeat = chips // (HEADS // 2)
    span = length // (2 * blocks)
    core, share = pos_ref[2], pos_ref[1] % repeat
    head = head_of(pos_ref, chips)
    lane = lax.broadcasted_iota(jnp.int32, (1, HEAD), 1)
    pick = (lane == head).astype(F32)
    strict, incl, _ = tri_masks(CHUNK)
    copies[0].wait()
    copies[1].wait()
    count = length // CHUNK
    scale_q = HEAD ** (-0.5)
    headgrad_ref[...] = jnp.zeros(headgrad_ref.shape, F32)

    def first(group, carry):
        for i in range(GROUP):
            r = pl.ds(pl.multiple_of((group * GROUP + i) * CHUNK, CHUNK), CHUNK)
            block = group * GROUP + i
            pair = [dh_ref[2 * (block % chips) + j, block // chips, :, :] for j in range(2)]
            grad = jnp.concatenate(pair, axis=0).astype(F32)
            lin = lin_ref[r, :]
            sig = jax.nn.sigmoid(lin)
            swish = lin * sig
            hat = oh_ref[r, :]
            gain = gain_ref[...]
            both = grad * hat
            headgrad_ref[0:1, :] += jnp.sum(both * swish, axis=0, keepdims=True)
            dcat_ref[r, 3 * HEAD : 4 * HEAD] = (
                both * gain * (sig * (1.0 + lin * (1.0 - sig)))
            ).astype(BF16)
            lead = grad * gain * swish
            grad_out = ro_ref[r, :] * (
                lead - hat * jnp.mean(lead * hat, axis=-1, keepdims=True)
            )
            do_ref[r, :] = grad_out
            flag = flag_ref[r, 3:4]
            direct = mm(split(sc_ref[r, :]), split(grad_out), TN)
            dpre_ref[r, :] = direct
            zed = mm(split(t_ref[r, :]), split(direct), TN)
            back_ref[r, :] = mm(
                split(flag * grad_out), split(qh_ref[r, :] * scale_q), TN
            ) - mm(split(beta_ref[r, :] * flag * zed), split(k_ref[r, :]), TN)
        return carry

    lax.fori_loop(0, count // GROUP, first, 0)
    grad_state = jnp.zeros((HEAD, HEAD), F32)
    for n in reversed(range(count)):
        rows = slice(n * CHUNK, (n + 1) * CHUNK)
        dstate_ref[rows, :] = grad_state
        last = flag_ref[(n + 1) * CHUNK - 1 : (n + 1) * CHUNK, 3:4]
        grad_state = (
            last * grad_state
            - mm(split(grad_state), split(map_ref[rows, :]), NT)
            + back_ref[rows, :]
        )
    copies[2].wait()
    copies[3].wait()
    du_ref[length : length + 8, :] = jnp.zeros((8, 3 * HEAD), F32)

    def second(group, carry):
        for i in range(GROUP):
            r = pl.ds(pl.multiple_of((group * GROUP + i) * CHUNK, CHUNK), CHUNK)
            same = idc_ref[r, :] == idr_ref[group * GROUP + i, :, :]
            low = jnp.logical_and(same, strict)
            full = jnp.logical_and(same, incl)
            flag = flag_ref[r, 3:4]
            ends = flag_ref[r, 4:5]
            beta = beta_ref[r, :]
            key_f = k_ref[r, :]
            key = split(key_f)
            q_hat = qh_ref[r, :]
            query = split(q_hat * scale_q)
            state_i = split(state_ref[r, :])
            dstate = split(dstate_ref[r, :])
            grad_out = split(do_ref[r, :])
            pseudo = split(ps_ref[r, :])
            dpre = dpre_ref[r, :] + ends * mm(key, dstate, NT)
            zed = mm(split(t_ref[r, :]), split(dpre), TN)
            zeds = split(zed)
            dscore = split(jnp.where(full, mm(grad_out, pseudo, NT), 0.0))
            grad_q = flag * mm(grad_out, state_i, NN) + mm(dscore, key, NN)
            dgram = split(jnp.where(low, -beta * mm(zeds, pseudo, NT), 0.0))
            grad_v = beta * zed
            grad_k = (
                mm(dscore, query, TN)
                + ends * mm(pseudo, dstate, NN)
                + mm(dgram, key, NN)
                + mm(dgram, key, TN)
                - flag * mm(split(grad_v), state_i, NN)
            )
            grad_b = jnp.sum(zed * er_ref[r, :], axis=-1, keepdims=True)
            dz = grad_b * beta * (1.0 - beta)
            dcat_ref[r, 4 * HEAD : 5 * HEAD] = (dz * pick).astype(BF16)
            lead = scale_q * grad_q
            du_ref[r, 0:HEAD] = sq_ref[r, :] * (
                lead - q_hat * jnp.sum(lead * q_hat, axis=-1, keepdims=True)
            )
            du_ref[r, HEAD : 2 * HEAD] = sk_ref[r, :] * (
                grad_k - key_f * jnp.sum(grad_k * key_f, axis=-1, keepdims=True)
            )
            du_ref[r, 2 * HEAD : 3 * HEAD] = sv_ref[r, :] * grad_v
        return carry

    lax.fori_loop(0, count // GROUP, second, 0)
    copies[4].wait()
    sums = [[jnp.zeros((1, HEAD), F32) for _ in range(CONV)] for _ in range(3)]
    for n in range(count):
        r0 = n * CHUNK
        rows = slice(r0, r0 + CHUNK)
        for c in range(3):
            cols = slice(c * HEAD, (c + 1) * HEAD)
            here = du_ref[rows, cols]
            grad = tap_ref[4 * c : 4 * c + 1, :] * here
            sums[c][0] += jnp.sum(
                here * p_ref[8 + r0 : 8 + r0 + CHUNK, cols], axis=0, keepdims=True
            )
            for j in range(1, CONV):
                after = slice(r0 + j, r0 + j + CHUNK)
                grad = grad + tap_ref[4 * c + j : 4 * c + j + 1, :] * (
                    du_ref[after, cols] * flag_ref[after, j - 1 : j]
                )
                moved = p_ref[8 + r0 - j : 8 + r0 - j + CHUNK, cols]
                sums[c][j] += jnp.sum(
                    here * flag_ref[rows, j - 1 : j] * moved, axis=0, keepdims=True
                )
            dcat_ref[rows, cols] = grad.astype(BF16)
    tapgrad_ref[...] = jnp.concatenate(
        [sums[c][j] for c in range(3) for j in range(CONV)]
        + [jnp.zeros((4, HEAD), F32)],
        axis=0,
    )
    if repeat > 1:
        for n in range(count):
            counts = (n % chips % repeat == share).astype(F32)
            rows = slice(n * CHUNK, (n + 1) * CHUNK)
            dcat_ref[rows, :] = (dcat_ref[rows, :].astype(F32) * counts).astype(BF16)
        tapgrad_ref[...] = tapgrad_ref[...] * (share == 0).astype(F32)
    width = normed_ref.shape[1]
    copies[5].wait()
    copies[6].wait()

    tall = 4 * CHUNK
    for n in range(length // tall):
        rows = slice(n * tall, (n + 1) * tall)
        part = lax.dot_general(dcat_ref[rows, :], wcat_ref[...], NT, preferred_element_type=F32)
        for j in range(4):
            low = part[2 * j * span : (2 * j + 1) * span]
            high = part[(2 * j + 1) * span : (2 * j + 2) * span]
            dnkeep_ref[4 * n + j, :, :] = jnp.where(core == 1, high, low).astype(BF16)
            dnsend_ref[4 * n + j, :, :] = jnp.where(core == 1, low, high).astype(BF16)
    fold, place = head_fold(small_rows), head_place(small_rows)
    total = headgrad_ref[0:1, :] * (share == 0).astype(F32)
    spread = mm(split(fold * total), split(place), NN)
    for i in range(width // HEAD):
        cols = slice(i * HEAD, (i + 1) * HEAD)
        if i % 4 == 0:
            wide = slice(i * HEAD, (i + 4) * HEAD)
            four = lax.dot_general(
                normed_ref[:, wide], dcat_ref[...], TN, preferred_element_type=F32
            )
        grad = four[i % 4 * HEAD : (i % 4 + 1) * HEAD]
        mats = wcat_ref[cols, :].astype(F32)
        gain = mats[:, 4 * HEAD + HEADS : 4 * HEAD + HEADS + 1]
        gain_grad = jnp.sum(grad * mats, axis=-1, keepdims=True) / gain
        here = (head == i).astype(F32)
        lines = jnp.concatenate(
            [
                jnp.zeros((HEADS, HEAD), F32),
                jnp.zeros((1, HEAD), F32),
                swiglu_ref[0:1, cols],
                tapgrad_ref[0 : 3 * CONV, :] * here,
                jnp.zeros((HEAD - HEADS - 2 - 3 * CONV, HEAD), F32),
            ],
            axis=0,
        )
        lane = lax.broadcasted_iota(jnp.int32, (1, HEAD), 1)
        small = (
            grad[:, 4 * HEAD :] + jnp.transpose(lines) + gain_grad * (lane == HEADS) + spread
        )
        grad = jnp.concatenate([grad[:, : 4 * HEAD], small], axis=1)
        per = HEAD // (2 * rows_here)
        for j in range(per):
            low = grad[2 * j * rows_here : (2 * j + 1) * rows_here]
            high = grad[(2 * j + 1) * rows_here : (2 * j + 2) * rows_here]
            dwkeep_ref[i * per + j, :, :] = jnp.where(core == 1, high, low).astype(BF16)
            dwsend_ref[i * per + j, :, :] = jnp.where(core == 1, low, high).astype(BF16)


def feed_forward(
    pos_ref,
    got_ref,
    xown_ref,
    cot_ref,
    oown_ref,
    osib_ref,
    pown_ref,
    psib_ref,
    down_ref,
    gains_ref,
    wo_ref,
    normed_ref,
    grads_ref,
    hidden_ref,
    cots_ref,
    swiglu_ref,
    res_ref,
    norm_ref,
    *rest,
):
    chips, _, span, width = xown_ref.shape
    send_refs, (wp_ref, heads_ref, total_ref, hat_ref, part_ref) = rest[: chips - 1], rest[chips - 1 :]
    repeat = chips // (HEADS // 2)
    tokens = 2 * chips * span
    ff = down_ref.shape[0]
    m, q, c, _ = place_of(pos_ref)
    rows_here = oown_ref.shape[2]
    for i in range(2 * chips):
        d, e = i // 2, i % 2
        block = (m ^ e) * chips + (q ^ d)
        other = (m ^ e) * chips + d
        for which, o_ref, p_ref in ((c, oown_ref, pown_ref), (1 - c, osib_ref, psib_ref)):
            spot = pl.ds(pl.multiple_of((2 * other + which) * rows_here, rows_here), rows_here)
            wo_ref[spot, :] = o_ref[d, e, :, :]
            wp_ref[spot, :] = p_ref[e, d, :, :]
        spot = pl.ds(pl.multiple_of(block * span, span), span)
        cots_ref[spot, :] = cot_ref[d, e, :, :]
        total_ref[spot, :] = xown_ref[d, e, :, :].astype(F32)
    for i in range(2):
        for j in range(HEADS // 2):
            h = i * (HEADS // 2) + j
            heads_ref[:, h * HEAD : (h + 1) * HEAD] = got_ref[2 * j * repeat + i, :, :]
    total = total_ref[...] + lax.dot_general(
        heads_ref[...], wo_ref[...], NN, preferred_element_type=F32
    )
    total_ref[...] = total
    scale = lax.rsqrt(jnp.mean(total * total, axis=-1, keepdims=True) + EPSILON)
    hat = total * scale
    hat_ref[...] = hat
    normed_ref[...] = (hat * gains_ref[1:2, :]).astype(BF16)
    both = lax.dot_general(normed_ref[...], wp_ref[...], NN, preferred_element_type=F32)
    gate, up = both[:, :ff], both[:, ff:]
    sig = jax.nn.sigmoid(gate)
    act = gate * sig
    hidden_ref[...] = (act * up).astype(BF16)
    back = lax.dot_general(cots_ref[...], down_ref[...], NT, preferred_element_type=F32)
    slope = sig * (1.0 + gate * (1.0 - sig))
    grads_ref[...] = jnp.concatenate([back * up * slope, back * act], axis=1).astype(BF16)
    part_ref[...] = lax.dot_general(grads_ref[...], wp_ref[...], NT, preferred_element_type=F32)
    total = jnp.sum(part_ref[...] * hat_ref[...], axis=0, keepdims=True)
    swiglu_ref[...] = jnp.broadcast_to(total, swiglu_ref.shape)
    for e in range(2):
        spot = pl.ds(pl.multiple_of((e * chips + q) * span, span), span)
        res_ref[e, :, :] = total_ref[spot, :]
        norm_ref[e, :, :] = part_ref[spot, :]
        for d, send_ref in enumerate(send_refs):
            spot = pl.ds(pl.multiple_of((e * chips + (q ^ (d + 1))) * span, span), span)
            send_ref[e, :, :] = part_ref[spot, :].astype(BF16)


def feed_forward_grads(
    pos_ref, normed_ref, grads_ref, hidden_ref, cots_ref, down_ref,
    keep_ref, send_ref, downkeep_ref, downsend_ref, out_ref,
):
    rows_here = keep_ref.shape[1]
    chips, _, span, _ = out_ref.shape
    core = pos_ref[2]
    per = HEAD // (2 * rows_here)
    for i in range(normed_ref.shape[1] // HEAD):
        if i % 4 == 0:
            wide = slice(i * HEAD, (i + 4) * HEAD)
            four = lax.dot_general(
                normed_ref[:, wide], grads_ref[...], TN, preferred_element_type=F32
            )
        grad = four[i % 4 * HEAD : (i % 4 + 1) * HEAD]
        for j in range(per):
            low = grad[2 * j * rows_here : (2 * j + 1) * rows_here]
            high = grad[(2 * j + 1) * rows_here : (2 * j + 2) * rows_here]
            keep_ref[i * per + j, :, :] = jnp.where(core == 1, high, low).astype(BF16)
            send_ref[i * per + j, :, :] = jnp.where(core == 1, low, high).astype(BF16)
    down = lax.dot_general(hidden_ref[...], cots_ref[...], TN, preferred_element_type=F32)
    rows = downkeep_ref.shape[1]
    for e in range(2):
        low = down[2 * e * rows : (2 * e + 1) * rows]
        high = down[(2 * e + 1) * rows : (2 * e + 2) * rows]
        downkeep_ref[e, :, :] = jnp.where(core == 1, high, low).astype(BF16)
        downsend_ref[e, :, :] = jnp.where(core == 1, low, high).astype(BF16)
    out = lax.dot_general(hidden_ref[...], down_ref[...], NN, preferred_element_type=F32)
    for e in range(2):
        for j in range(chips):
            spot = (e * chips + j) * span
            out_ref[j, e, :, :] = out[spot : spot + span].astype(BF16)


def branch_gradient(pos_ref, norm_ref, res_ref, cot_ref, gains_ref, wo_ref, *rest):
    *got_refs, resid_ref, branch_ref, heads_ref = rest
    m = pos_ref[0]
    chips = heads_ref.shape[0] // 2
    repeat = chips // (HEADS // 2)
    branches = []
    for e in range(2):
        norm = norm_ref[e, :, :]
        for got_ref in got_refs:
            norm = norm + got_ref[e, :, :].astype(F32)
        res = res_ref[e, :, :]
        scale = lax.rsqrt(jnp.mean(res * res, axis=-1, keepdims=True) + EPSILON)
        hat = res * scale
        lead = norm * gains_ref[1:2, :]
        grad = cot_ref[0, m ^ e, :, :].astype(F32) + scale * (
            lead - hat * jnp.mean(lead * hat, axis=-1, keepdims=True)
        )
        resid_ref[e, :, :] = grad
        branch = grad.astype(BF16)
        branch_ref[e, :, :] = branch
        branches.append(branch)
    back = lax.dot_general(
        jnp.concatenate(branches, axis=0), wo_ref[...], NT, preferred_element_type=F32
    ).astype(BF16)
    span = branch_ref.shape[1]
    for e in range(2):
        for j in range(chips):
            for i in range(2):
                h = i * (HEADS // 2) + j // repeat
                heads_ref[2 * j + i, e, :, :] = back[
                    e * span : (e + 1) * span, h * HEAD : (h + 1) * HEAD
                ]


def output_gradient(pos_ref, got_ref, *refs):
    *branch_refs, all_ref, rows_ref, duo_ref = refs
    chips = len(branch_refs)
    span = branch_refs[0].shape[1]
    repeat = chips // (HEADS // 2)
    q = pos_ref[1]
    share = q % repeat
    for d, branch_ref in enumerate(branch_refs):
        for e in range(2):
            spot = pl.ds(pl.multiple_of((e * chips + (q ^ d)) * span, span), span)
            value = branch_ref[e, :, :]
            if repeat > 1:
                counts = ((q ^ d) % repeat == share).astype(F32)
                value = (value.astype(F32) * counts).astype(BF16)
            rows_ref[spot, :] = value
    first = pl.multiple_of((q // repeat) * 2 * repeat, 2)
    for i in range(2):
        duo_ref[:, i * HEAD : (i + 1) * HEAD] = got_ref[first + i, :, :]
    both = lax.dot_general(duo_ref[...], rows_ref[...], TN, preferred_element_type=F32)
    for i in range(2):
        all_ref[i, :, :] = both[i * HEAD : (i + 1) * HEAD].astype(BF16)


def input_gradient(pos_ref, resid_ref, x_ref, gains_ref, got_ref, out_ref):
    m = pos_ref[0]
    for e in range(2):
        norm = got_ref[0, e, :, :].astype(F32)
        for j in range(1, got_ref.shape[0]):
            norm = norm + got_ref[j, e, :, :].astype(F32)
        x = x_ref[m ^ e, :, :].astype(F32)
        scale = lax.rsqrt(jnp.mean(x * x, axis=-1, keepdims=True) + EPSILON)
        hat = x * scale
        lead = norm * gains_ref[0:1, :]
        out_ref[e, :, :] = (
            resid_ref[e, :, :]
            + scale * (lead - hat * jnp.mean(lead * hat, axis=-1, keepdims=True))
        ).astype(BF16)


def token_pieces(keep_ref, got_ref, out_ref):
    chips = out_ref.shape[0]
    for e in range(2):
        for j in range(chips):
            block = e * chips + j
            out_ref[j, e, :, :] = (
                keep_ref[block, :, :].astype(F32) + got_ref[block, :, :].astype(F32)
            ).astype(BF16)


def merge_heads(pos_ref, keep_ref, got_ref, *out_refs):
    m, _, core, batch = place_of(pos_ref)
    wide = 4 * HEAD

    def merge(out_ref, keep, got):
        out_ref[..., :wide] = jnp.where(core == 1, got[..., :wide], keep[..., :wide])
        out_ref[..., wide : 2 * wide] = jnp.where(core == 1, keep[..., :wide], got[..., :wide])
        out_ref[..., 2 * wide :] = (
            keep[..., wide:].astype(F32) + got[..., wide:].astype(F32)
        ).astype(BF16)

    if len(out_refs) == 1:
        merge(out_refs[0], keep_ref[...], got_ref[...])
        return
    chips, rows, _ = out_refs[0].shape
    for i, out_ref in enumerate(out_refs):
        spot = pl.ds(pl.multiple_of((batch ^ (i % 2)) * rows, rows), rows)
        for j in range(chips):
            block = (m ^ (i // 2)) * chips + j
            merge(out_ref.at[j], keep_ref[block, spot, :], got_ref[block, spot, :])


def add_partners(pos_ref, *refs):
    in_refs, out_refs = refs[:4], refs[4:]
    for d, out_ref in enumerate(out_refs):
        j = pos_ref[1] ^ d
        total = in_refs[0][j, :, :].astype(F32)
        for in_ref in in_refs[1:]:
            total = total + in_ref[j, :, :].astype(F32)
        out_ref[...] = total.astype(BF16)


def spread_heads(pos_ref, *refs):
    *got_refs, wq_ref, wk_ref, wv_ref, wg_ref, beta_ref, gains_ref, taps_ref, head_ref, side_ref = refs
    chips = len(got_refs)
    repeat = chips // (HEADS // 2)
    rows = wq_ref.shape[0]
    small = jnp.zeros((rows, HEAD), F32)
    if repeat > 1:
        for ref in (wq_ref, wk_ref, wv_ref, wg_ref):
            ref[...] = jnp.zeros(ref.shape, F32)
    for d, got_ref in enumerate(got_refs):
        slot = (pos_ref[1] ^ d) // repeat
        for i in range(2):
            cols = pl.ds(pl.multiple_of((i * (HEADS // 2) + slot) * HEAD, HEAD), HEAD)
            for t, ref in enumerate((wq_ref, wk_ref, wv_ref, wg_ref)):
                spot = (4 * i + t) * HEAD
                value = got_ref[0:rows, spot : spot + HEAD].astype(F32)
                ref[:, cols] = value + ref[:, cols] if repeat > 1 else value
        small = small + got_ref[0:rows, 8 * HEAD :].astype(F32)
    side_ref[...] = jnp.zeros(side_ref.shape, F32)
    side_ref[0:rows, :] = small
    across = jnp.transpose(side_ref[...])
    beta_ref[...] = across[:HEADS, :rows]
    gains_ref[...] = across[HEADS : HEADS + 8, :rows]
    taps_ref[...] = across[HEADS + 2 : HEADS + 2 + 3 * CONV, :rows]
    found = mm(split(side_ref[...]), split(head_place(rows)), NT)
    first = lax.broadcasted_iota(jnp.int32, (HEAD, HEAD), 0) < rows
    head_ref[...] = jnp.sum(
        jnp.where(first, found * head_fold(rows), 0.0), axis=0, keepdims=True
    )


def spread_pair(got_ref, gate_ref, up_ref):
    chips, _, wide = got_ref.shape
    wide = wide // 4
    for j in range(chips):
        got = got_ref[j, :, :].astype(F32)
        for t, ref in enumerate((gate_ref, up_ref)):
            for e in range(2):
                part = (2 * t + e) * wide
                spot = (e * chips + j) * wide
                ref[:, spot : spot + wide] = got[:, part : part + wide]


VMEM_SPEC = pl.BlockSpec(memory_space=pltpu.VMEM)


def run_kernel(body, name, operands, out_shapes, scratch, micros, scalars=(), stays=(), leaves=(), scale=1):
    specs = [VMEM_SPEC] * len(operands)
    for i in scalars:
        specs[i] = pl.BlockSpec(memory_space=pltpu.SMEM)
    for i in stays:
        specs[i] = pl.BlockSpec(memory_space=pl.ANY)
    room = [pltpu.VMEM(*s) for s in scratch]
    if stays or leaves:
        room.append(pltpu.SemaphoreType.DMA((len(stays) + len(leaves) + 1,)))
    outs = [VMEM_SPEC] * len(out_shapes)
    for i in leaves:
        outs[i] = pl.BlockSpec(memory_space=pl.ANY)
    return pl.pallas_call(
        body,
        name=name,
        out_shape=[jax.ShapeDtypeStruct(*s) for s in out_shapes],
        in_specs=specs,
        out_specs=outs,
        scratch_shapes=room,
        compiler_params=pltpu.CompilerParams(vmem_limit_bytes=min(ROOM.get(name, 56) * scale * MEGA, VMEM_BYTES)),
        cost_estimate=pl.CostEstimate(
            flops=micros * COST, bytes_accessed=1 << 10, transcendentals=0
        ),
    )(*operands)


def tie(value, *others):
    return lax.optimization_barrier((value,) + others)[0]


def together(*values):
    return lax.optimization_barrier(values)


def swap(value, axis, mask):
    return lax.ppermute(value, axis, [(i, i ^ mask) for i in range(lax.axis_size(axis))])


def ordered(bit, mine, other):
    flag = bit == 1
    return (jnp.where(flag, other, mine), jnp.where(flag, mine, other))


def from_chips(value):
    return [value] + [swap(value, "q", d) for d in range(1, lax.axis_size("q"))]


def to_chips(blocks):
    chip = lax.axis_index("q")
    mine = [lax.dynamic_index_in_dim(blocks, chip ^ d, 0, keepdims=False) for d in range(blocks.shape[0])]
    return [mine[0]] + [swap(mine[d], "q", d) for d in range(1, len(mine))]


def gather_batch_start(value, axis):
    step, batch = 1, lax.axis_index("b")
    lead, rows = value.shape[:axis], value.shape[axis:]
    while 2 * step < lax.axis_size("b"):
        got = swap(value, "b", step)
        value = jnp.stack(ordered((batch // step) % 2, value, got), axis=axis)
        step *= 2
    value = value.reshape(lead + (step * rows[0],) + rows[1:])
    return value, swap(value, "b", step)


def gather_batch_end(value, got, axis):
    lead, rows = value.shape[:axis], value.shape[axis:]
    high = lax.axis_index("b") // (lax.axis_size("b") // 2) == 1
    value = jnp.stack(ordered(high.astype(jnp.int32), value, got), axis=axis)
    return value.reshape(lead + (2 * rows[0],) + rows[1:])


def gather_batch(value, axis):
    return gather_batch_end(*gather_batch_start(value, axis), axis)


def scatter_bit(value, axis, bit, mesh_axis, mask):
    low, high = (lax.index_in_dim(value, i, axis, keepdims=False) for i in (0, 1))
    flag = bit == 1
    keep, send = jnp.where(flag, high, low), jnp.where(flag, low, high)
    return keep.astype(F32) + swap(send.astype(BF16), mesh_axis, mask).astype(F32)


def scatter_batch(value, axis, left=1):
    batch, step = lax.axis_index("b"), lax.axis_size("b") // 2
    while step >= left:
        shape = value.shape
        value = value.reshape(shape[:axis] + (2, shape[axis] // 2) + shape[axis + 1 :])
        value = scatter_bit(value, axis, (batch // step) % 2, "b", step)
        step //= 2
    return lax.squeeze(value, (axis,)) if left == 1 else value


def token_flags(ids):
    length = ids.shape[0]
    padded = jnp.concatenate([jnp.full((CONV - 1,), -1, jnp.int32), ids])
    by_chunk = ids.reshape(length // CHUNK, CHUNK)
    before = jnp.concatenate([jnp.full((1,), -1, jnp.int32), by_chunk[:-1, -1]])
    columns = [padded[CONV - 1 - j : CONV - 1 - j + length] == ids for j in range(1, CONV)]
    columns.append((by_chunk == before[:, None]).reshape(length))
    columns.append((by_chunk == by_chunk[:, -1:]).reshape(length))
    flags = jnp.stack(columns, axis=1).astype(F32)
    return jnp.pad(flags, ((0, 8), (0, 3))), by_chunk[:, None, :], ids[:, None]


def on_device(
    inputs,
    cotangent,
    document_ids,
    query_weight,
    key_weight,
    value_weight,
    beta_weight,
    outgate_weight,
    output_weight,
    gate_weight,
    up_weight,
    down_weight,
    mixer_gain,
    swiglu_gain,
    head_gain,
    conv_weight,
):
    micro, _, span, width = inputs.shape
    chips, n_batch = lax.axis_size("q"), lax.axis_size("b")
    half_heads = HEADS // 2
    repeat = chips // half_heads
    length = micro * chips * 2 * span
    rows_w = query_weight.shape[0]
    rows_f = down_weight.shape[0]
    rows_all = n_batch * rows_w
    blocks_all = micro * chips
    ff_here = rows_f * micro * 2 * n_batch
    row, chip, core = lax.axis_index("m"), lax.axis_index("q"), lax.axis_index("c")
    share = chip % repeat
    flag_row = row == 1
    pos = jnp.stack([row, chip, core, lax.axis_index("b")]).astype(jnp.int32)

    mine = run_kernel(
        pack_heads,
        "pack_heads",
        (pos, query_weight, key_weight, value_weight, outgate_weight, beta_weight.T)
        + (mixer_gain[None, :], swiglu_gain[None, :], conv_weight),
        [((rows_w, 9 * HEAD), BF16)] * chips,
        [((4, rows_w, width), BF16), ((HEAD, HEAD), F32)],
        1,
        (0,),
        (1, 2, 3, 4),
    )
    head_s = [swap(mine[d], "q", d) for d in range(1, chips)]

    def own_slab(value):
        return jnp.where(flag_row, value[1], value[0])

    def away_slab(value):
        return jnp.where(flag_row, value[0], value[1])

    x_s = swap(away_slab(inputs[:, 0]), "m", 1)
    head_s, x_s = together(head_s, x_s)
    head_q = jnp.stack([mine[0]] + head_s, axis=0)
    x_own = jnp.stack([own_slab(inputs[:, 0]), x_s], axis=0)
    head_m = jnp.stack([head_q, swap(head_q, "m", 1)], axis=0)
    x_half = jnp.stack(from_chips(x_own), axis=0)
    out_s = swap(tie(output_weight, x_s), "m", 1)
    ids = own_slab(document_ids[:, 0])
    flags, id_rows, id_cols = token_flags(ids)
    gain_vec = head_gain.astype(F32)[None, :]
    pair = jnp.stack([gate_weight, up_weight], axis=1).reshape(
        rows_w, 2, micro, chips, 2 * n_batch * rows_f
    )
    pair = jnp.moveaxis(pair, 3, 0).reshape(chips, rows_w, 2 * ff_here)
    cot_away = away_slab(cotangent[:, 0])
    head_m, x_half, out_s, flags, id_rows, id_cols, gain_vec, pair, cot_away = together(
        head_m, x_half, out_s, flags, id_rows, id_cols, gain_vec, pair, cot_away
    )
    head_b = gather_batch(head_m.reshape(blocks_all, rows_w, 9 * HEAD), 1)
    x_sib = swap(x_half, "c", 1)
    cot_s = swap(cot_away, "m", 1)
    down_s = swap(tie(down_weight, x_half), "m", 1)
    out_b = gather_batch(jnp.stack([output_weight, out_s], axis=0), 1)
    pair_q = lax.all_to_all(pair, ("q",), 0, 0, tiled=True)
    head_b, x_sib, cot_s, down_s, out_b, pair_q = together(
        head_b, x_sib, cot_s, down_s, out_b, pair_q
    )
    send = lax.dynamic_slice_in_dim(head_b, (1 - core) * 4 * HEAD, 4 * HEAD, 2)
    head_sib = swap(jnp.concatenate([send, head_b[..., 8 * HEAD :]], axis=-1), "c", 1)
    pair_s = swap(pair_q, "m", 1)
    cot_own = jnp.stack([own_slab(cotangent[:, 0]), cot_s], axis=0)
    down_m, down_got = gather_batch_start(jnp.stack(ordered(row, down_weight, down_s), axis=0), 1)
    out_q = lax.all_to_all(
        jnp.broadcast_to(out_b, (chips,) + out_b.shape), ("q",), 0, 0, tiled=True
    )
    cot_got = [swap(cot_own, "q", d) for d in range(1, chips)]

    count = length // CHUNK
    run = partial(run_kernel, scale=max(1, length // 1024))

    def tall(n):
        return ((n, length, HEAD), F32)

    slabs = ((2, span, width), BF16)
    slabs_wide = ((2, span, width), F32)
    saved = [
        ((length, width), BF16),
        ((width, 5 * HEAD), BF16),
        ((length + 8, 3 * HEAD), F32),
        tall(7),
        tall(3),
        tall(3),
        tall(2),
    ]
    heads_here, taps, gains, normed, w_cat, p_pad, kept, slopes, found, shaped = run(
        mixer_forward,
        "mixer_forward",
        (pos, x_half, x_sib, head_b, head_sib, flags, id_cols, id_rows, gain_vec),
        [((chips, 2, length // 2, HEAD), BF16), ((16, HEAD), F32), ((8, width), F32)] + saved,
        [((HEAD, width), F32)] + saved + [tall(4)],
        25,
        (0,),
        (),
        tuple(range(3, 10)),
    )
    pair_s, down_got, out_q, cot_got = tie((pair_s, down_got, out_q, cot_got), heads_here)

    got_heads = lax.all_to_all(
        heads_here.reshape(chips * 2, length // 2, HEAD), ("q", "c"), 0, 0, tiled=True
    )
    pair_m = jnp.stack([pair_q, pair_s], axis=0).reshape(blocks_all, rows_w, 2 * ff_here)
    pair_b = gather_batch(pair_m, 1).reshape(micro, chips, rows_all, 2 * ff_here)
    cot_half = jnp.stack([cot_own] + cot_got, axis=0)
    down_b = gather_batch_end(down_m, down_got, 1)
    out_sib = swap(out_q, "c", 1)
    down_sib = swap(down_b, "c", 1)
    pair_sib = swap(pair_b, "c", 1)
    w_down = jnp.stack(ordered(core, down_b, down_sib), axis=1).reshape(ff_here, width)
    half = length // 2
    w_out, normed_two, pair_up, hidden, cot_rows, swiglu_part, res_own, norm_own, *norm_send = run(
        feed_forward,
        "feed_forward",
        (pos, got_heads, x_half, cot_half, out_q, out_sib, pair_b, pair_sib, w_down, gains),
        [
            ((width, width), BF16),
            ((half, width), BF16),
            ((half, 2 * ff_here), BF16),
            ((half, ff_here), BF16),
            ((half, width), BF16),
            ((8, width), F32),
            slabs_wide,
            slabs_wide,
        ]
        + [slabs] * (chips - 1),
        [
            ((width, 2 * ff_here), BF16),
            ((half, width), BF16),
            ((half, width), F32),
            ((half, width), F32),
            ((half, width), F32),
        ],
        12,
        (0,),
    )
    norm_got = [swap(v, "q", d + 1) for d, v in enumerate(norm_send)]
    pair_keep, pair_send, down_keep, down_send, out_part = run(
        feed_forward_grads,
        "feed_forward_grads",
        (pos, normed_two, pair_up, hidden, cot_rows, w_down),
        [
            ((blocks_all, rows_all, 2 * ff_here), BF16),
            ((blocks_all, rows_all, 2 * ff_here), BF16),
            ((micro, n_batch * rows_f, width), BF16),
            ((micro, n_batch * rows_f, width), BF16),
            ((chips, 2, span, width), BF16),
        ],
        [],
        6,
        (0,),
    )
    norm_got, norm_own, pair_send, down_send = together(norm_got, norm_own, pair_send, down_send)
    grad_resid, grad_branch, grad_heads = run(
        branch_gradient,
        "branch_gradient",
        (pos, norm_own, res_own, cot_own[None], gains, w_out, *norm_got),
        [slabs_wide, slabs, ((chips * 2, 2, span, HEAD), BF16)],
        [],
        2,
        (0,),
    )

    pair_got = swap(pair_send, "c", 1)
    down_got = swap(down_send, "c", 1)
    dheads = lax.all_to_all(grad_heads, ("q", "c"), 0, 0, tiled=True)
    grad_branch, pair_got, down_got = together(grad_branch, pair_got, down_got)
    pair_grad = (pair_keep.astype(F32) + pair_got.astype(F32)).astype(BF16)
    down_grad = (down_keep.astype(F32) + down_got.astype(F32)).astype(BF16)
    down_grad = down_grad.reshape(micro, n_batch, rows_f, width)
    dheads, pair_grad, down_grad, grad_branch, out_part = together(
        dheads, pair_grad, down_grad, grad_branch, out_part
    )
    out_got = lax.all_to_all(out_part, ("q",), 0, 0, tiled=True)
    branch_got = [swap(grad_branch, "q", d) for d in range(1, chips)]
    pair_grad = pair_grad.reshape(micro, chips, n_batch, rows_w, 2 * ff_here)
    pair_keep = lax.dynamic_index_in_dim(pair_grad, row, 0, keepdims=False)
    pair_got = swap(lax.dynamic_index_in_dim(pair_grad, 1 - row, 0, keepdims=False), "m", 1)
    down_grad = scatter_batch(down_grad, 1)

    def to_rows(value):
        keep = jnp.where(flag_row, value[1], value[0])
        send = jnp.where(flag_row, value[0], value[1])
        return jnp.stack(ordered(row, keep, swap(send, "m", 1)), axis=0)[:, None]

    blocks_out = ((blocks_all, span, width), BF16)
    weights_out = ((blocks_all, rows_all, 5 * HEAD), BF16)
    norm_keep, norm_send, w_keep, w_send = run(
        partial(mixer_backward, rows_w),
        "mixer_backward",
        (pos, dheads, flags, id_cols, id_rows, gain_vec, taps, swiglu_part)
        + (kept, shaped, found, slopes, p_pad, normed, w_cat),
        [blocks_out, blocks_out, weights_out, weights_out],
        [saved[i] for i in (3, 6, 5, 4, 2, 0, 1)]
        + [
            tall(3),
            ((length, HEAD), F32),
            ((length + 8, 3 * HEAD), F32),
            ((length, 5 * HEAD), BF16),
            ((16, HEAD), F32),
            ((8, HEAD), F32),
        ],
        25,
        (0,),
        tuple(range(8, 15)),
    )
    pair_got, down_grad, branch_got, out_got, w_send, norm_send = together(
        pair_got, down_grad, branch_got, out_got, w_send, norm_send
    )

    norm_got = swap(norm_send, "c", 1)
    w_got = swap(w_send, "c", 1)
    (out_rows,) = run(
        output_gradient,
        "output_gradient",
        (pos, got_heads, grad_branch, *branch_got),
        [((2, HEAD, width), BF16)],
        [((half, width), BF16), ((half, 2 * HEAD), BF16)],
        1,
        (0,),
    )
    w_got, out_rows = together(w_got, out_rows)
    piece = ((chips, rows_w, 9 * HEAD), BF16)
    if n_batch == 2:
        value = run(
            merge_heads, "merge_heads", (pos, w_keep, w_got), [piece] * 4, [], 1, (0,)
        )
    else:
        merged_all = ((blocks_all, rows_all, 9 * HEAD), BF16)
        (value,) = run(
            merge_heads, "merge_heads", (pos, w_keep, w_got), [merged_all], [], 1, (0,)
        )
        value = value.reshape(blocks_all, n_batch, rows_w, 9 * HEAD)
        value = scatter_batch(value, 1, 2).reshape(micro, chips, 2, rows_w, 9 * HEAD)
        batch = lax.axis_index("b") % 2
        value = [
            lax.dynamic_index_in_dim(
                lax.dynamic_index_in_dim(value, row ^ (i // 2), 0, keepdims=False),
                batch ^ (i % 2),
                1,
                keepdims=False,
            ).astype(BF16)
            for i in range(4)
        ]
    value, norm_got, out_rows, pair_got = together(value, norm_got, out_rows, pair_got)
    (norm_send,) = run(
        token_pieces,
        "token_pieces",
        (norm_keep, norm_got),
        [((chips, 2, span, width), BF16)],
        [],
        1,
    )
    step = repeat // 2
    while step >= 1:
        out_rows = out_rows.reshape(micro, 2, out_rows.shape[1] // 2, width)
        out_rows = scatter_bit(out_rows, 1, (share // step) % 2, "q", step)
        step //= 2
    out_rows = out_rows.reshape(micro, 2, n_batch, rows_w, width)
    norm_got = lax.all_to_all(norm_send, ("q",), 0, 0, tiled=True)
    value_got = [
        swap(value[1], "b", 1),
        swap(value[2], "m", 1),
        swap(value[3], ("m", "b"), n_batch + 1),
    ]
    pair_rows = (pair_keep.astype(F32) + pair_got.astype(F32)).astype(BF16)
    pair_rows = scatter_batch(pair_rows, 1)
    out_rows = scatter_bit(out_rows, 1, core, "c", 1)
    norm_got, pair_rows, out_rows = together(norm_got, pair_rows, out_rows)
    pair_got = lax.all_to_all(pair_rows.astype(BF16), ("q",), 0, 0, tiled=True)
    out_rows = scatter_batch(out_rows, 1)
    (grad_own,) = run(
        input_gradient,
        "input_gradient",
        (pos, grad_resid, x_own, gains, norm_got),
        [slabs],
        [],
        1,
        (0,),
    )
    grad_final = to_rows(grad_own)
    value_got, out_rows, down_grad, out_got = together(value_got, out_rows, down_grad, out_got)
    head_got = run(
        add_partners,
        "add_partners",
        (pos, value[0], *value_got),
        [((rows_w, 9 * HEAD), BF16)] * chips,
        [],
        1,
        (0,),
    )
    head_got = [head_got[0]] + [swap(head_got[d], "q", d) for d in range(1, chips)]
    outproj_grad = scatter_bit(out_rows, 0, row, "m", 1)
    down_grad = scatter_bit(down_grad, 0, row, "m", 1)
    out_all = (res_own + jnp.sum(out_got.astype(F32), axis=0)).astype(BF16)
    out_final = to_rows(out_all)
    gate_grad, up_grad = run(
        spread_pair,
        "spread_pair",
        (pair_got,),
        [(gate_weight.shape[:1] + (chips * ff_here,), F32)] * 2,
        [],
        2,
    )
    *merged, beta_sum, gain_sums, tap_sums, head_sum = run(
        spread_heads,
        "spread_heads",
        (pos, *head_got),
        [((rows_w, width), F32)] * 4
        + [((HEADS, rows_w), F32), ((8, rows_w), F32), ((3 * CONV, rows_w), F32), ((1, HEAD), F32)],
        [((HEAD, HEAD), F32)],
        1,
        (0,),
    )
    return (
        out_final,
        grad_final,
        merged[0],
        merged[1],
        merged[2],
        beta_sum.T,
        merged[3],
        outproj_grad,
        gate_grad,
        up_grad,
        down_grad,
        gain_sums[0],
        gain_sums[1],
        head_sum[0],
        tap_sums,
    )


def solution(mesh):
    n_seq, n_batch = mesh.shape["seq"], mesh.shape["batch"]

    def program(*arrays):
        micro = arrays[0].shape[0]
        shape = (micro, n_seq // (2 * micro), 2, n_batch)
        fine = Mesh(mesh.devices.reshape(shape), ("m", "q", "c", "b"))
        seq, every = ("m", "q", "c"), ("m", "q", "c", "b")
        tokens, rows, vector, taps = P(None, "b", seq, None), P(every, None), P(every), P(None, every)
        return jax.shard_map(
            on_device,
            mesh=fine,
            in_specs=(tokens, tokens, P(None, "b", None))
            + (rows,) * 9
            + (vector, vector, P(), taps),
            out_specs=(tokens, tokens) + (rows,) * 9 + (vector, vector, P(), taps),
            check_vma=False,
        )(*arrays)

    return program
```

```python
from functools import partial

import jax
import jax.numpy as jnp
from jax import lax
from jax.experimental import pallas as pl
from jax.experimental.pallas import tpu as pltpu
from jax.sharding import Mesh, PartitionSpec as P

HEADS = 8
HEAD = 128
CONV = 4
EPSILON = 1e-05
UNIT_EPSILON = 1e-06
CHUNK = 128
GROUP = 8
FREE = 24
COST = 10**6
MEGA = 1024 * 1024
VMEM_BYTES = 56 * MEGA
ROOM = {"branch_gradient": 12, "output_gradient": 12, "token_pieces": 12, "merge_heads": 12, "add_partners": 12, "input_gradient": 12, "spread_heads": 12, "spread_pair": 12, "feed_forward": 32, "feed_forward_grads": 24}
F32 = jnp.float32
BF16 = jnp.bfloat16
NN = (((1,), (0,)), ((), ()))
NT = (((1,), (1,)), ((), ()))
TN = (((0,), (0,)), ((), ()))


def split(value):
    high = value.astype(BF16)
    return (high, (value - high.astype(F32)).astype(BF16))


def mm(left, right, dims):
    def dot(a, b):
        return lax.dot_general(a, b, dims, preferred_element_type=F32)

    return dot(left[0], right[0]) + (dot(left[0], right[1]) + dot(left[1], right[0]))


def long_mm(left, right, dims):
    ((a_dim,), (b_dim,)), _ = dims
    long_left = jnp.concatenate([left[0], left[0], left[1]], axis=a_dim)
    long_right = jnp.concatenate([right[0], right[1], right[0]], axis=b_dim)
    return lax.dot_general(long_left, long_right, dims, preferred_element_type=F32)


def block_mask(size, width):
    row = lax.broadcasted_iota(jnp.int32, (size, size), 0)
    col = lax.broadcasted_iota(jnp.int32, (size, size), 1)
    return (row // width) == (col // width)


def tri_masks(size):
    row = lax.broadcasted_iota(jnp.int32, (size, size), 0)
    col = lax.broadcasted_iota(jnp.int32, (size, size), 1)
    return (row > col, row >= col, row == col)


def unit_lower_inverses(mats):
    size = mats[0].shape[0]
    eye = tri_masks(size)[2].astype(F32)
    near = block_mask(size, 8)
    base = [split(jnp.where(near, m, 0.0)) for m in mats]
    square = [split(long_mm(b, b, NN)) for b in base]
    first = [eye - jnp.where(near, m, 0.0) for m in mats]
    second = [f + long_mm(split(f), s, NN) for f, s in zip(first, square)]
    fourth = [split(long_mm(s, s, NN)) for s in square]
    inverse = [f + long_mm(split(f), s, NN) for f, s in zip(second, fourth)]
    width = 8
    while width < size:
        inside, wider = block_mask(size, width), block_mask(size, 2 * width)
        cut = jnp.logical_and(wider, jnp.logical_not(inside))
        off = [split(jnp.where(cut, m, 0.0)) for m in mats]
        halves = [split(t) for t in inverse]
        step = [split(long_mm(t, o, NN)) for t, o in zip(halves, off)]
        inverse = [t - long_mm(s, h, NN) for t, s, h in zip(inverse, step, halves)]
        width *= 2
    return inverse


def views(ref):
    return [ref.at[i] for i in range(ref.shape[0])]


def place_of(pos_ref):
    return (pos_ref[0], pos_ref[1], pos_ref[2], pos_ref[3])


def head_of(pos_ref, chips):
    return pos_ref[2] * (HEADS // 2) + pos_ref[1] // (chips // (HEADS // 2))


def pack_heads(
    pos_ref, wq_ref, wk_ref, wv_ref, wg_ref, beta_ref, mixer_ref, swiglu_ref, conv_ref, *refs
):
    *out_refs, here_ref, side_ref, sems = refs
    chips = len(out_refs)
    repeat = chips // (HEADS // 2)
    copies = [
        pltpu.make_async_copy(ref, here_ref.at[t], sems.at[t])
        for t, ref in enumerate((wq_ref, wk_ref, wv_ref, wg_ref))
    ]
    for copy in copies:
        copy.start()
    rows, conv = here_ref.shape[1], HEADS + 2
    side_ref[...] = jnp.zeros(side_ref.shape, F32)
    side_ref[0:HEADS, 0:rows] = beta_ref[...].astype(F32)
    side_ref[HEADS : HEADS + 1, 0:rows] = mixer_ref[...].astype(F32)
    side_ref[HEADS + 1 : conv, 0:rows] = swiglu_ref[...].astype(F32)
    side_ref[conv : conv + 3 * CONV, 0:rows] = conv_ref[...].astype(F32)
    across = jnp.transpose(side_ref[...])
    side_ref[...] = across
    small = side_ref[0:rows, :].astype(BF16)
    for out_ref in out_refs:
        out_ref[:, 8 * HEAD :] = small
    for t, copy in enumerate(copies):
        copy.wait()
        for d, out_ref in enumerate(out_refs):
            slot = (pos_ref[1] ^ d) // repeat
            for i in range(2):
                cols = pl.ds(pl.multiple_of((i * (HEADS // 2) + slot) * HEAD, HEAD), HEAD)
                spot = (4 * i + t) * HEAD
                out_ref[:, spot : spot + HEAD] = here_ref[t, :, cols]


def mixer_forward(
    pos_ref,
    xown_ref,
    xsib_ref,
    wown_ref,
    wsib_ref,
    flag_ref,
    idc_ref,
    idr_ref,
    gain_ref,
    heads_ref,
    tap_ref,
    gains_ref,
    normed_out,
    wcat_out,
    p_out,
    kept_out,
    slope_out,
    found_out,
    shape_out,
    across_ref,
    normed_ref,
    wcat_ref,
    p_ref,
    kept_ref,
    slope_ref,
    found_ref,
    shape_ref,
    brief_ref,
    sems,
):
    qh_ref, k_ref, lin_ref, beta_ref, t_ref, sc_ref, map_ref = views(kept_ref)
    sq_ref, sk_ref, sv_ref = views(slope_ref)
    v_ref, pb_ref, w_ref, add_ref = views(brief_ref)
    state_ref, ps_ref, er_ref = views(found_ref)
    oh_ref, ro_ref = views(shape_ref)
    copies = []

    def send(i, source, target):
        copies.append(pltpu.make_async_copy(source, target, sems.at[i]))
        copies[-1].start()

    chips, _, span, width = xown_ref.shape
    length = normed_ref.shape[0]
    count = length // CHUNK
    strict, incl, _ = tri_masks(CHUNK)
    m, q, c, _ = place_of(pos_ref)
    head = head_of(pos_ref, chips)
    rows_here = wown_ref.shape[1]
    for i in range(wown_ref.shape[0]):
        block = (m ^ (i // chips)) * chips + (q ^ (i % chips))
        mine = pl.ds(pl.multiple_of((2 * block + c) * rows_here, rows_here), rows_here)
        theirs = pl.ds(pl.multiple_of((2 * block + 1 - c) * rows_here, rows_here), rows_here)
        cols = pl.ds(pl.multiple_of(c * 4 * HEAD, 4 * HEAD), 4 * HEAD)
        wcat_ref[mine, 0 : 4 * HEAD] = wown_ref[i, :, cols]
        wcat_ref[mine, 4 * HEAD :] = wown_ref[i, :, 8 * HEAD :]
        wcat_ref[theirs, :] = wsib_ref[i, :, :]
    for i in range(width // HEAD):
        rows = slice(i * HEAD, (i + 1) * HEAD)
        across_ref[:, rows] = jnp.transpose(wcat_ref[rows, 4 * HEAD :].astype(F32))
    gain = across_ref[HEADS : HEADS + 1, :]
    gains_ref[...] = across_ref[HEADS : HEADS + 8, :]
    mine = pl.ds(pl.multiple_of(head * HEAD, HEAD), HEAD)
    tap_ref[...] = across_ref[HEADS + 2 : HEADS + 18, mine]
    for i in range(2 * chips):
        block = (m ^ (i % 2)) * chips + (q ^ (i // 2))
        for which, ref in ((c, xown_ref), (1 - c, xsib_ref)):
            x = ref[i // 2, i % 2, :, :].astype(F32)
            scale = lax.rsqrt(jnp.mean(x * x, axis=-1, keepdims=True) + EPSILON)
            spot = pl.ds(pl.multiple_of((2 * block + which) * span, span), span)
            normed_ref[spot, :] = (x * scale * gain).astype(BF16)
    lane = lax.broadcasted_iota(jnp.int32, (1, HEAD), 1)
    pick = (lane == head).astype(F32)
    p_ref[0:8, :] = jnp.zeros((8, 3 * HEAD), F32)

    tall = 4 * CHUNK
    for n in range(length // tall):
        rows = slice(n * tall, (n + 1) * tall)
        y = lax.dot_general(normed_ref[rows, :], wcat_ref[...], NN, preferred_element_type=F32)
        p_ref[8 + n * tall : 8 + (n + 1) * tall, :] = y[:, 0 : 3 * HEAD].astype(BF16).astype(F32)
        lin_ref[rows, :] = y[:, 3 * HEAD : 4 * HEAD]
        logit = jnp.sum(y[:, 4 * HEAD :] * pick, axis=-1, keepdims=True)
        beta_ref[rows, :] = jnp.broadcast_to(jax.nn.sigmoid(logit), (tall, HEAD))
    for n in range(count):
        r0 = n * CHUNK
        rows = slice(r0, r0 + CHUNK)
        keep = [None] + [flag_ref[rows, j : j + 1] for j in range(CONV - 1)]
        for c in range(3):
            cols = slice(c * HEAD, (c + 1) * HEAD)
            pre = tap_ref[4 * c : 4 * c + 1, :] * p_ref[8 + r0 : 8 + r0 + CHUNK, cols]
            for j in range(1, CONV):
                moved = p_ref[8 + r0 - j : 8 + r0 - j + CHUNK, cols]
                pre = pre + tap_ref[4 * c + j : 4 * c + j + 1, :] * moved * keep[j]
            sig = jax.nn.sigmoid(pre)
            act = pre * sig
            slope = sig * (1.0 + pre * (1.0 - sig))
            if c == 2:
                v_ref[rows, :] = act
                sv_ref[rows, :] = slope
            else:
                scale = lax.rsqrt(jnp.sum(act * act, axis=-1, keepdims=True) + UNIT_EPSILON)
                (qh_ref if c == 0 else k_ref)[rows, :] = act * scale
                (sq_ref if c == 0 else sk_ref)[rows, :] = slope * scale
    send(0, normed_ref, normed_out)
    send(1, wcat_ref, wcat_out)
    send(2, p_ref, p_out)
    send(3, slope_ref, slope_out)
    send(4, kept_ref.at[0:4], kept_out.at[0:4])

    def prepare(group, carry):
        spots = [pl.multiple_of((group * GROUP + i) * CHUNK, CHUNK) for i in range(GROUP)]
        rows = [pl.ds(s, CHUNK) for s in spots]
        key = [split(k_ref[r, :]) for r in rows]
        same = [
            idc_ref[r, :] == idr_ref[group * GROUP + i, :, :] for i, r in enumerate(rows)
        ]
        beta = [beta_ref[r, :] for r in rows]
        mats = [
            jnp.where(jnp.logical_and(s, strict), b * long_mm(k, k, NT), 0.0)
            for s, b, k in zip(same, beta, key)
        ]
        inverse = unit_lower_inverses(mats)
        for i, r in enumerate(rows):
            t_ref[r, :] = inverse[i]
            inv = split(inverse[i])
            pseudo = long_mm(inv, split(beta[i] * v_ref[r, :]), NN)
            weighed = split(
                long_mm(inv, split(beta[i] * flag_ref[r, 3:4] * k_ref[r, :]), NN)
            )
            ends = split(flag_ref[r, 4:5] * k_ref[r, :])
            query = split(qh_ref[r, :] * HEAD ** (-0.5))
            sc_ref[r, :] = jnp.where(
                jnp.logical_and(same[i], incl), long_mm(query, key[i], NT), 0.0
            )
            pb_ref[r, :] = pseudo
            w_ref[r, :] = weighed[0].astype(F32) + weighed[1].astype(F32)
            map_ref[r, :] = long_mm(weighed, ends, TN)
            add_ref[r, :] = long_mm(split(pseudo), ends, TN)
        return carry

    lax.fori_loop(0, count // GROUP, prepare, 0)
    send(5, kept_ref.at[4:7], kept_out.at[4:7])

    state = jnp.zeros((HEAD, HEAD), F32)
    for n in range(count):
        rows = slice(n * CHUNK, (n + 1) * CHUNK)
        state_ref[rows, :] = state
        last = flag_ref[(n + 1) * CHUNK - 1 : (n + 1) * CHUNK, 3:4]
        state = last * state - long_mm(split(state), split(map_ref[rows, :]), NN) + add_ref[rows, :]

    def produce(group, carry):
        for i in range(GROUP):
            r = pl.ds(pl.multiple_of((group * GROUP + i) * CHUNK, CHUNK), CHUNK)
            same = idc_ref[r, :] == idr_ref[group * GROUP + i, :, :]
            key = split(k_ref[r, :])
            state_i = split(state_ref[r, :])
            flag = flag_ref[r, 3:4]
            pseudo = pb_ref[r, :] - long_mm(split(w_ref[r, :]), state_i, NT)
            ps_ref[r, :] = pseudo
            halves = split(pseudo)
            gram = jnp.where(jnp.logical_and(same, strict), long_mm(key, key, NT), 0.0)
            er_ref[r, :] = (
                v_ref[r, :] - flag * long_mm(key, state_i, NT) - long_mm(split(gram), halves, NN)
            )
            query = split(qh_ref[r, :] * HEAD ** (-0.5))
            out = flag * long_mm(query, state_i, NT) + long_mm(split(sc_ref[r, :]), halves, NN)
            scale = lax.rsqrt(jnp.mean(out * out, axis=-1, keepdims=True) + EPSILON)
            hat = out * scale
            oh_ref[r, :] = hat
            ro_ref[r, :] = jnp.broadcast_to(scale, (CHUNK, HEAD))
            lin = lin_ref[r, :]
            made = (hat * gain_ref[...] * (lin * jax.nn.sigmoid(lin))).astype(BF16)
            half = CHUNK // 2
            spot = pl.ds(pl.multiple_of((group * GROUP + i) * half, half), half)
            for chip in range(heads_ref.shape[0]):
                heads_ref[chip, 0, spot, :] = made[:half]
                heads_ref[chip, 1, spot, :] = made[half:]
        return carry

    lax.fori_loop(0, count // GROUP, produce, 0)
    send(6, found_ref, found_out)
    send(7, shape_ref, shape_out)
    for copy in copies:
        copy.wait()


def head_fold(rows):
    row = lax.broadcasted_iota(jnp.int32, (HEAD, HEAD), 0)
    lane = lax.broadcasted_iota(jnp.int32, (HEAD, HEAD), 1)
    return (lane // (HEAD // rows) == row % rows).astype(F32)


def head_place(rows):
    row = lax.broadcasted_iota(jnp.int32, (HEAD, HEAD), 0)
    lane = lax.broadcasted_iota(jnp.int32, (HEAD, HEAD), 1)
    return (lane == FREE + row % (HEAD // rows)).astype(F32)


def mixer_backward(
    small_rows,
    pos_ref,
    dh_ref,
    flag_ref,
    idc_ref,
    idr_ref,
    gain_ref,
    tap_ref,
    swiglu_ref,
    kept_in,
    shape_in,
    found_in,
    slope_in,
    p_in,
    normed_in,
    wcat_in,
    dnkeep_ref,
    dnsend_ref,
    dwkeep_ref,
    dwsend_ref,
    kept_ref,
    shape_ref,
    found_ref,
    slope_ref,
    p_ref,
    normed_ref,
    wcat_ref,
    back3_ref,
    back_ref,
    du_ref,
    dcat_ref,
    tapgrad_ref,
    headgrad_ref,
    sems,
):
    copies = [
        pltpu.make_async_copy(source, target, sems.at[i])
        for i, (source, target) in enumerate(
            (
                (kept_in, kept_ref),
                (shape_in, shape_ref),
                (found_in, found_ref),
                (slope_in, slope_ref),
                (p_in, p_ref),
                (normed_in, normed_ref),
                (wcat_in, wcat_ref),
            )
        )
    ]
    for copy in copies:
        copy.start()
    qh_ref, k_ref, lin_ref, beta_ref, t_ref, sc_ref, map_ref = views(kept_ref)
    sq_ref, sk_ref, sv_ref = views(slope_ref)
    state_ref, ps_ref, er_ref = views(found_ref)
    oh_ref, ro_ref = views(shape_ref)
    do_ref, dpre_ref, dstate_ref = views(back3_ref)
    length = lin_ref.shape[0]
    blocks, rows_here, _ = dwkeep_ref.shape
    chips = blocks // 2
    repeat = chips // (HEADS // 2)
    span = length // (2 * blocks)
    core, share = pos_ref[2], pos_ref[1] % repeat
    head = head_of(pos_ref, chips)
    lane = lax.broadcasted_iota(jnp.int32, (1, HEAD), 1)
    pick = (lane == head).astype(F32)
    strict, incl, _ = tri_masks(CHUNK)
    copies[0].wait()
    copies[1].wait()
    count = length // CHUNK
    scale_q = HEAD ** (-0.5)
    headgrad_ref[...] = jnp.zeros(headgrad_ref.shape, F32)

    def first(group, carry):
        for i in range(GROUP):
            r = pl.ds(pl.multiple_of((group * GROUP + i) * CHUNK, CHUNK), CHUNK)
            block = group * GROUP + i
            pair = [dh_ref[2 * (block % chips) + j, block // chips, :, :] for j in range(2)]
            grad = jnp.concatenate(pair, axis=0).astype(F32)
            lin = lin_ref[r, :]
            sig = jax.nn.sigmoid(lin)
            swish = lin * sig
            hat = oh_ref[r, :]
            gain = gain_ref[...]
            both = grad * hat
            headgrad_ref[0:1, :] += jnp.sum(both * swish, axis=0, keepdims=True)
            dcat_ref[r, 3 * HEAD : 4 * HEAD] = (
                both * gain * (sig * (1.0 + lin * (1.0 - sig)))
            ).astype(BF16)
            lead = grad * gain * swish
            grad_out = ro_ref[r, :] * (
                lead - hat * jnp.mean(lead * hat, axis=-1, keepdims=True)
            )
            do_ref[r, :] = grad_out
            flag = flag_ref[r, 3:4]
            direct = mm(split(sc_ref[r, :]), split(grad_out), TN)
            dpre_ref[r, :] = direct
            zed = mm(split(t_ref[r, :]), split(direct), TN)
            back_ref[r, :] = mm(
                split(flag * grad_out), split(qh_ref[r, :] * scale_q), TN
            ) - mm(split(beta_ref[r, :] * flag * zed), split(k_ref[r, :]), TN)
        return carry

    lax.fori_loop(0, count // GROUP, first, 0)
    grad_state = jnp.zeros((HEAD, HEAD), F32)
    for n in reversed(range(count)):
        rows = slice(n * CHUNK, (n + 1) * CHUNK)
        dstate_ref[rows, :] = grad_state
        last = flag_ref[(n + 1) * CHUNK - 1 : (n + 1) * CHUNK, 3:4]
        grad_state = (
            last * grad_state
            - mm(split(grad_state), split(map_ref[rows, :]), NT)
            + back_ref[rows, :]
        )
    copies[2].wait()
    copies[3].wait()
    du_ref[length : length + 8, :] = jnp.zeros((8, 3 * HEAD), F32)

    def second(group, carry):
        for i in range(GROUP):
            r = pl.ds(pl.multiple_of((group * GROUP + i) * CHUNK, CHUNK), CHUNK)
            same = idc_ref[r, :] == idr_ref[group * GROUP + i, :, :]
            low = jnp.logical_and(same, strict)
            full = jnp.logical_and(same, incl)
            flag = flag_ref[r, 3:4]
            ends = flag_ref[r, 4:5]
            beta = beta_ref[r, :]
            key_f = k_ref[r, :]
            key = split(key_f)
            q_hat = qh_ref[r, :]
            query = split(q_hat * scale_q)
            state_i = split(state_ref[r, :])
            dstate = split(dstate_ref[r, :])
            grad_out = split(do_ref[r, :])
            pseudo = split(ps_ref[r, :])
            dpre = dpre_ref[r, :] + ends * mm(key, dstate, NT)
            zed = mm(split(t_ref[r, :]), split(dpre), TN)
            zeds = split(zed)
            dscore = split(jnp.where(full, mm(grad_out, pseudo, NT), 0.0))
            grad_q = flag * mm(grad_out, state_i, NN) + mm(dscore, key, NN)
            dgram = split(jnp.where(low, -beta * mm(zeds, pseudo, NT), 0.0))
            grad_v = beta * zed
            grad_k = (
                mm(dscore, query, TN)
                + ends * mm(pseudo, dstate, NN)
                + mm(dgram, key, NN)
                + mm(dgram, key, TN)
                - flag * mm(split(grad_v), state_i, NN)
            )
            grad_b = jnp.sum(zed * er_ref[r, :], axis=-1, keepdims=True)
            dz = grad_b * beta * (1.0 - beta)
            dcat_ref[r, 4 * HEAD : 5 * HEAD] = (dz * pick).astype(BF16)
            lead = scale_q * grad_q
            du_ref[r, 0:HEAD] = sq_ref[r, :] * (
                lead - q_hat * jnp.sum(lead * q_hat, axis=-1, keepdims=True)
            )
            du_ref[r, HEAD : 2 * HEAD] = sk_ref[r, :] * (
                grad_k - key_f * jnp.sum(grad_k * key_f, axis=-1, keepdims=True)
            )
            du_ref[r, 2 * HEAD : 3 * HEAD] = sv_ref[r, :] * grad_v
        return carry

    lax.fori_loop(0, count // GROUP, second, 0)
    copies[4].wait()
    sums = [[jnp.zeros((1, HEAD), F32) for _ in range(CONV)] for _ in range(3)]
    for n in range(count):
        r0 = n * CHUNK
        rows = slice(r0, r0 + CHUNK)
        for c in range(3):
            cols = slice(c * HEAD, (c + 1) * HEAD)
            here = du_ref[rows, cols]
            grad = tap_ref[4 * c : 4 * c + 1, :] * here
            sums[c][0] += jnp.sum(
                here * p_ref[8 + r0 : 8 + r0 + CHUNK, cols], axis=0, keepdims=True
            )
            for j in range(1, CONV):
                after = slice(r0 + j, r0 + j + CHUNK)
                grad = grad + tap_ref[4 * c + j : 4 * c + j + 1, :] * (
                    du_ref[after, cols] * flag_ref[after, j - 1 : j]
                )
                moved = p_ref[8 + r0 - j : 8 + r0 - j + CHUNK, cols]
                sums[c][j] += jnp.sum(
                    here * flag_ref[rows, j - 1 : j] * moved, axis=0, keepdims=True
                )
            dcat_ref[rows, cols] = grad.astype(BF16)
    tapgrad_ref[...] = jnp.concatenate(
        [sums[c][j] for c in range(3) for j in range(CONV)]
        + [jnp.zeros((4, HEAD), F32)],
        axis=0,
    )
    if repeat > 1:
        for n in range(count):
            counts = (n % chips % repeat == share).astype(F32)
            rows = slice(n * CHUNK, (n + 1) * CHUNK)
            dcat_ref[rows, :] = (dcat_ref[rows, :].astype(F32) * counts).astype(BF16)
        tapgrad_ref[...] = tapgrad_ref[...] * (share == 0).astype(F32)
    width = normed_ref.shape[1]
    copies[5].wait()
    copies[6].wait()

    tall = 4 * CHUNK
    for n in range(length // tall):
        rows = slice(n * tall, (n + 1) * tall)
        part = lax.dot_general(dcat_ref[rows, :], wcat_ref[...], NT, preferred_element_type=F32)
        for j in range(4):
            low = part[2 * j * span : (2 * j + 1) * span]
            high = part[(2 * j + 1) * span : (2 * j + 2) * span]
            dnkeep_ref[4 * n + j, :, :] = jnp.where(core == 1, high, low).astype(BF16)
            dnsend_ref[4 * n + j, :, :] = jnp.where(core == 1, low, high).astype(BF16)
    fold, place = head_fold(small_rows), head_place(small_rows)
    total = headgrad_ref[0:1, :] * (share == 0).astype(F32)
    spread = mm(split(fold * total), split(place), NN)
    for i in range(width // HEAD):
        cols = slice(i * HEAD, (i + 1) * HEAD)
        if i % 4 == 0:
            wide = slice(i * HEAD, (i + 4) * HEAD)
            four = lax.dot_general(
                normed_ref[:, wide], dcat_ref[...], TN, preferred_element_type=F32
            )
        grad = four[i % 4 * HEAD : (i % 4 + 1) * HEAD]
        mats = wcat_ref[cols, :].astype(F32)
        gain = mats[:, 4 * HEAD + HEADS : 4 * HEAD + HEADS + 1]
        gain_grad = jnp.sum(grad * mats, axis=-1, keepdims=True) / gain
        here = (head == i).astype(F32)
        lines = jnp.concatenate(
            [
                jnp.zeros((HEADS, HEAD), F32),
                jnp.zeros((1, HEAD), F32),
                swiglu_ref[0:1, cols],
                tapgrad_ref[0 : 3 * CONV, :] * here,
                jnp.zeros((HEAD - HEADS - 2 - 3 * CONV, HEAD), F32),
            ],
            axis=0,
        )
        lane = lax.broadcasted_iota(jnp.int32, (1, HEAD), 1)
        small = (
            grad[:, 4 * HEAD :] + jnp.transpose(lines) + gain_grad * (lane == HEADS) + spread
        )
        grad = jnp.concatenate([grad[:, : 4 * HEAD], small], axis=1)
        per = HEAD // (2 * rows_here)
        for j in range(per):
            low = grad[2 * j * rows_here : (2 * j + 1) * rows_here]
            high = grad[(2 * j + 1) * rows_here : (2 * j + 2) * rows_here]
            dwkeep_ref[i * per + j, :, :] = jnp.where(core == 1, high, low).astype(BF16)
            dwsend_ref[i * per + j, :, :] = jnp.where(core == 1, low, high).astype(BF16)


def feed_forward(
    pos_ref,
    got_ref,
    xown_ref,
    cot_ref,
    oown_ref,
    osib_ref,
    pown_ref,
    psib_ref,
    down_ref,
    gains_ref,
    wo_ref,
    normed_ref,
    grads_ref,
    hidden_ref,
    cots_ref,
    swiglu_ref,
    res_ref,
    norm_ref,
    *rest,
):
    chips, _, span, width = xown_ref.shape
    send_refs, (wp_ref, heads_ref, total_ref, hat_ref, part_ref) = rest[: chips - 1], rest[chips - 1 :]
    repeat = chips // (HEADS // 2)
    tokens = 2 * chips * span
    ff = down_ref.shape[0]
    m, q, c, _ = place_of(pos_ref)
    rows_here = oown_ref.shape[2]
    for i in range(2 * chips):
        d, e = i // 2, i % 2
        block = (m ^ e) * chips + (q ^ d)
        other = (m ^ e) * chips + d
        for which, o_ref, p_ref in ((c, oown_ref, pown_ref), (1 - c, osib_ref, psib_ref)):
            spot = pl.ds(pl.multiple_of((2 * other + which) * rows_here, rows_here), rows_here)
            wo_ref[spot, :] = o_ref[d, e, :, :]
            wp_ref[spot, :] = p_ref[e, d, :, :]
        spot = pl.ds(pl.multiple_of(block * span, span), span)
        cots_ref[spot, :] = cot_ref[d, e, :, :]
        total_ref[spot, :] = xown_ref[d, e, :, :].astype(F32)
    for i in range(2):
        for j in range(HEADS // 2):
            h = i * (HEADS // 2) + j
            heads_ref[:, h * HEAD : (h + 1) * HEAD] = got_ref[2 * j * repeat + i, :, :]
    total = total_ref[...] + lax.dot_general(
        heads_ref[...], wo_ref[...], NN, preferred_element_type=F32
    )
    total_ref[...] = total
    scale = lax.rsqrt(jnp.mean(total * total, axis=-1, keepdims=True) + EPSILON)
    hat = total * scale
    hat_ref[...] = hat
    normed_ref[...] = (hat * gains_ref[1:2, :]).astype(BF16)
    both = lax.dot_general(normed_ref[...], wp_ref[...], NN, preferred_element_type=F32)
    gate, up = both[:, :ff], both[:, ff:]
    sig = jax.nn.sigmoid(gate)
    act = gate * sig
    hidden_ref[...] = (act * up).astype(BF16)
    back = lax.dot_general(cots_ref[...], down_ref[...], NT, preferred_element_type=F32)
    slope = sig * (1.0 + gate * (1.0 - sig))
    grads_ref[...] = jnp.concatenate([back * up * slope, back * act], axis=1).astype(BF16)
    part_ref[...] = lax.dot_general(grads_ref[...], wp_ref[...], NT, preferred_element_type=F32)
    total = jnp.sum(part_ref[...] * hat_ref[...], axis=0, keepdims=True)
    swiglu_ref[...] = jnp.broadcast_to(total, swiglu_ref.shape)
    for e in range(2):
        spot = pl.ds(pl.multiple_of((e * chips + q) * span, span), span)
        res_ref[e, :, :] = total_ref[spot, :]
        norm_ref[e, :, :] = part_ref[spot, :]
        for d, send_ref in enumerate(send_refs):
            spot = pl.ds(pl.multiple_of((e * chips + (q ^ (d + 1))) * span, span), span)
            send_ref[e, :, :] = part_ref[spot, :].astype(BF16)


def feed_forward_grads(
    pos_ref, normed_ref, grads_ref, hidden_ref, cots_ref, down_ref,
    keep_ref, send_ref, downkeep_ref, downsend_ref, out_ref,
):
    rows_here = keep_ref.shape[1]
    chips, _, span, _ = out_ref.shape
    core = pos_ref[2]
    per = HEAD // (2 * rows_here)
    for i in range(normed_ref.shape[1] // HEAD):
        if i % 4 == 0:
            wide = slice(i * HEAD, (i + 4) * HEAD)
            four = lax.dot_general(
                normed_ref[:, wide], grads_ref[...], TN, preferred_element_type=F32
            )
        grad = four[i % 4 * HEAD : (i % 4 + 1) * HEAD]
        for j in range(per):
            low = grad[2 * j * rows_here : (2 * j + 1) * rows_here]
            high = grad[(2 * j + 1) * rows_here : (2 * j + 2) * rows_here]
            keep_ref[i * per + j, :, :] = jnp.where(core == 1, high, low).astype(BF16)
            send_ref[i * per + j, :, :] = jnp.where(core == 1, low, high).astype(BF16)
    down = lax.dot_general(hidden_ref[...], cots_ref[...], TN, preferred_element_type=F32)
    rows = downkeep_ref.shape[1]
    for e in range(2):
        low = down[2 * e * rows : (2 * e + 1) * rows]
        high = down[(2 * e + 1) * rows : (2 * e + 2) * rows]
        downkeep_ref[e, :, :] = jnp.where(core == 1, high, low).astype(BF16)
        downsend_ref[e, :, :] = jnp.where(core == 1, low, high).astype(BF16)
    out = lax.dot_general(hidden_ref[...], down_ref[...], NN, preferred_element_type=F32)
    for e in range(2):
        for j in range(chips):
            spot = (e * chips + j) * span
            out_ref[j, e, :, :] = out[spot : spot + span].astype(BF16)


def branch_gradient(pos_ref, norm_ref, res_ref, cot_ref, gains_ref, wo_ref, *rest):
    *got_refs, resid_ref, branch_ref, heads_ref = rest
    m = pos_ref[0]
    chips = heads_ref.shape[0] // 2
    repeat = chips // (HEADS // 2)
    branches = []
    for e in range(2):
        norm = norm_ref[e, :, :]
        for got_ref in got_refs:
            norm = norm + got_ref[e, :, :].astype(F32)
        res = res_ref[e, :, :]
        scale = lax.rsqrt(jnp.mean(res * res, axis=-1, keepdims=True) + EPSILON)
        hat = res * scale
        lead = norm * gains_ref[1:2, :]
        grad = cot_ref[0, m ^ e, :, :].astype(F32) + scale * (
            lead - hat * jnp.mean(lead * hat, axis=-1, keepdims=True)
        )
        resid_ref[e, :, :] = grad
        branch = grad.astype(BF16)
        branch_ref[e, :, :] = branch
        branches.append(branch)
    back = lax.dot_general(
        jnp.concatenate(branches, axis=0), wo_ref[...], NT, preferred_element_type=F32
    ).astype(BF16)
    span = branch_ref.shape[1]
    for e in range(2):
        for j in range(chips):
            for i in range(2):
                h = i * (HEADS // 2) + j // repeat
                heads_ref[2 * j + i, e, :, :] = back[
                    e * span : (e + 1) * span, h * HEAD : (h + 1) * HEAD
                ]


def output_gradient(pos_ref, got_ref, *refs):
    *branch_refs, all_ref, rows_ref, duo_ref = refs
    chips = len(branch_refs)
    span = branch_refs[0].shape[1]
    repeat = chips // (HEADS // 2)
    q = pos_ref[1]
    share = q % repeat
    for d, branch_ref in enumerate(branch_refs):
        for e in range(2):
            spot = pl.ds(pl.multiple_of((e * chips + (q ^ d)) * span, span), span)
            value = branch_ref[e, :, :]
            if repeat > 1:
                counts = ((q ^ d) % repeat == share).astype(F32)
                value = (value.astype(F32) * counts).astype(BF16)
            rows_ref[spot, :] = value
    first = pl.multiple_of((q // repeat) * 2 * repeat, 2)
    for i in range(2):
        duo_ref[:, i * HEAD : (i + 1) * HEAD] = got_ref[first + i, :, :]
    both = lax.dot_general(duo_ref[...], rows_ref[...], TN, preferred_element_type=F32)
    for i in range(2):
        all_ref[i, :, :] = both[i * HEAD : (i + 1) * HEAD].astype(BF16)


def input_gradient(pos_ref, resid_ref, x_ref, gains_ref, got_ref, out_ref):
    m = pos_ref[0]
    for e in range(2):
        norm = got_ref[0, e, :, :].astype(F32)
        for j in range(1, got_ref.shape[0]):
            norm = norm + got_ref[j, e, :, :].astype(F32)
        x = x_ref[m ^ e, :, :].astype(F32)
        scale = lax.rsqrt(jnp.mean(x * x, axis=-1, keepdims=True) + EPSILON)
        hat = x * scale
        lead = norm * gains_ref[0:1, :]
        out_ref[e, :, :] = (
            resid_ref[e, :, :]
            + scale * (lead - hat * jnp.mean(lead * hat, axis=-1, keepdims=True))
        ).astype(BF16)


def token_pieces(keep_ref, got_ref, out_ref):
    chips = out_ref.shape[0]
    for e in range(2):
        for j in range(chips):
            block = e * chips + j
            out_ref[j, e, :, :] = (
                keep_ref[block, :, :].astype(F32) + got_ref[block, :, :].astype(F32)
            ).astype(BF16)


def merge_heads(pos_ref, keep_ref, got_ref, *out_refs):
    m, _, core, batch = place_of(pos_ref)
    wide = 4 * HEAD

    def merge(out_ref, keep, got):
        out_ref[..., :wide] = jnp.where(core == 1, got[..., :wide], keep[..., :wide])
        out_ref[..., wide : 2 * wide] = jnp.where(core == 1, keep[..., :wide], got[..., :wide])
        out_ref[..., 2 * wide :] = (
            keep[..., wide:].astype(F32) + got[..., wide:].astype(F32)
        ).astype(BF16)

    if len(out_refs) == 1:
        merge(out_refs[0], keep_ref[...], got_ref[...])
        return
    chips, rows, _ = out_refs[0].shape
    for i, out_ref in enumerate(out_refs):
        spot = pl.ds(pl.multiple_of((batch ^ (i % 2)) * rows, rows), rows)
        for j in range(chips):
            block = (m ^ (i // 2)) * chips + j
            merge(out_ref.at[j], keep_ref[block, spot, :], got_ref[block, spot, :])


def add_partners(pos_ref, *refs):
    in_refs, out_refs = refs[:4], refs[4:]
    for d, out_ref in enumerate(out_refs):
        j = pos_ref[1] ^ d
        total = in_refs[0][j, :, :].astype(F32)
        for in_ref in in_refs[1:]:
            total = total + in_ref[j, :, :].astype(F32)
        out_ref[...] = total.astype(BF16)


def spread_heads(pos_ref, *refs):
    *got_refs, wq_ref, wk_ref, wv_ref, wg_ref, beta_ref, gains_ref, taps_ref, head_ref, side_ref = refs
    chips = len(got_refs)
    repeat = chips // (HEADS // 2)
    rows = wq_ref.shape[0]
    small = jnp.zeros((rows, HEAD), F32)
    if repeat > 1:
        for ref in (wq_ref, wk_ref, wv_ref, wg_ref):
            ref[...] = jnp.zeros(ref.shape, F32)
    for d, got_ref in enumerate(got_refs):
        slot = (pos_ref[1] ^ d) // repeat
        for i in range(2):
            cols = pl.ds(pl.multiple_of((i * (HEADS // 2) + slot) * HEAD, HEAD), HEAD)
            for t, ref in enumerate((wq_ref, wk_ref, wv_ref, wg_ref)):
                spot = (4 * i + t) * HEAD
                value = got_ref[0:rows, spot : spot + HEAD].astype(F32)
                ref[:, cols] = value + ref[:, cols] if repeat > 1 else value
        small = small + got_ref[0:rows, 8 * HEAD :].astype(F32)
    side_ref[...] = jnp.zeros(side_ref.shape, F32)
    side_ref[0:rows, :] = small
    across = jnp.transpose(side_ref[...])
    beta_ref[...] = across[:HEADS, :rows]
    gains_ref[...] = across[HEADS : HEADS + 8, :rows]
    taps_ref[...] = across[HEADS + 2 : HEADS + 2 + 3 * CONV, :rows]
    found = mm(split(side_ref[...]), split(head_place(rows)), NT)
    first = lax.broadcasted_iota(jnp.int32, (HEAD, HEAD), 0) < rows
    head_ref[...] = jnp.sum(
        jnp.where(first, found * head_fold(rows), 0.0), axis=0, keepdims=True
    )


def spread_pair(got_ref, gate_ref, up_ref):
    chips, _, wide = got_ref.shape
    wide = wide // 4
    for j in range(chips):
        got = got_ref[j, :, :].astype(F32)
        for t, ref in enumerate((gate_ref, up_ref)):
            for e in range(2):
                part = (2 * t + e) * wide
                spot = (e * chips + j) * wide
                ref[:, spot : spot + wide] = got[:, part : part + wide]


VMEM_SPEC = pl.BlockSpec(memory_space=pltpu.VMEM)


def run_kernel(body, name, operands, out_shapes, scratch, micros, scalars=(), stays=(), leaves=(), scale=1):
    specs = [VMEM_SPEC] * len(operands)
    for i in scalars:
        specs[i] = pl.BlockSpec(memory_space=pltpu.SMEM)
    for i in stays:
        specs[i] = pl.BlockSpec(memory_space=pl.ANY)
    room = [pltpu.VMEM(*s) for s in scratch]
    if stays or leaves:
        room.append(pltpu.SemaphoreType.DMA((len(stays) + len(leaves) + 1,)))
    outs = [VMEM_SPEC] * len(out_shapes)
    for i in leaves:
        outs[i] = pl.BlockSpec(memory_space=pl.ANY)
    return pl.pallas_call(
        body,
        name=name,
        out_shape=[jax.ShapeDtypeStruct(*s) for s in out_shapes],
        in_specs=specs,
        out_specs=outs,
        scratch_shapes=room,
        compiler_params=pltpu.CompilerParams(vmem_limit_bytes=min(ROOM.get(name, 56) * scale * MEGA, VMEM_BYTES)),
        cost_estimate=pl.CostEstimate(
            flops=micros * COST, bytes_accessed=1 << 10, transcendentals=0
        ),
    )(*operands)


def tie(value, *others):
    return lax.optimization_barrier((value,) + others)[0]


def together(*values):
    return lax.optimization_barrier(values)


def swap(value, axis, mask):
    return lax.ppermute(value, axis, [(i, i ^ mask) for i in range(lax.axis_size(axis))])


def ordered(bit, mine, other):
    flag = bit == 1
    return (jnp.where(flag, other, mine), jnp.where(flag, mine, other))


def from_chips(value):
    return [value] + [swap(value, "q", d) for d in range(1, lax.axis_size("q"))]


def to_chips(blocks):
    chip = lax.axis_index("q")
    mine = [lax.dynamic_index_in_dim(blocks, chip ^ d, 0, keepdims=False) for d in range(blocks.shape[0])]
    return [mine[0]] + [swap(mine[d], "q", d) for d in range(1, len(mine))]


def gather_batch_start(value, axis):
    step, batch = 1, lax.axis_index("b")
    lead, rows = value.shape[:axis], value.shape[axis:]
    while 2 * step < lax.axis_size("b"):
        got = swap(value, "b", step)
        value = jnp.stack(ordered((batch // step) % 2, value, got), axis=axis)
        step *= 2
    value = value.reshape(lead + (step * rows[0],) + rows[1:])
    return value, swap(value, "b", step)


def gather_batch_end(value, got, axis):
    lead, rows = value.shape[:axis], value.shape[axis:]
    high = lax.axis_index("b") // (lax.axis_size("b") // 2) == 1
    value = jnp.stack(ordered(high.astype(jnp.int32), value, got), axis=axis)
    return value.reshape(lead + (2 * rows[0],) + rows[1:])


def gather_batch(value, axis):
    return gather_batch_end(*gather_batch_start(value, axis), axis)


def scatter_bit(value, axis, bit, mesh_axis, mask):
    low, high = (lax.index_in_dim(value, i, axis, keepdims=False) for i in (0, 1))
    flag = bit == 1
    keep, send = jnp.where(flag, high, low), jnp.where(flag, low, high)
    return keep.astype(F32) + swap(send.astype(BF16), mesh_axis, mask).astype(F32)


def scatter_batch(value, axis, left=1):
    batch, step = lax.axis_index("b"), lax.axis_size("b") // 2
    while step >= left:
        shape = value.shape
        value = value.reshape(shape[:axis] + (2, shape[axis] // 2) + shape[axis + 1 :])
        value = scatter_bit(value, axis, (batch // step) % 2, "b", step)
        step //= 2
    return lax.squeeze(value, (axis,)) if left == 1 else value


def token_flags(ids):
    length = ids.shape[0]
    padded = jnp.concatenate([jnp.full((CONV - 1,), -1, jnp.int32), ids])
    by_chunk = ids.reshape(length // CHUNK, CHUNK)
    before = jnp.concatenate([jnp.full((1,), -1, jnp.int32), by_chunk[:-1, -1]])
    columns = [padded[CONV - 1 - j : CONV - 1 - j + length] == ids for j in range(1, CONV)]
    columns.append((by_chunk == before[:, None]).reshape(length))
    columns.append((by_chunk == by_chunk[:, -1:]).reshape(length))
    flags = jnp.stack(columns, axis=1).astype(F32)
    return jnp.pad(flags, ((0, 8), (0, 3))), by_chunk[:, None, :], ids[:, None]


def on_device(
    inputs,
    cotangent,
    document_ids,
    query_weight,
    key_weight,
    value_weight,
    beta_weight,
    outgate_weight,
    output_weight,
    gate_weight,
    up_weight,
    down_weight,
    mixer_gain,
    swiglu_gain,
    head_gain,
    conv_weight,
):
    micro, _, span, width = inputs.shape
    chips, n_batch = lax.axis_size("q"), lax.axis_size("b")
    half_heads = HEADS // 2
    repeat = chips // half_heads
    length = micro * chips * 2 * span
    rows_w = query_weight.shape[0]
    rows_f = down_weight.shape[0]
    rows_all = n_batch * rows_w
    blocks_all = micro * chips
    ff_here = rows_f * micro * 2 * n_batch
    row, chip, core = lax.axis_index("m"), lax.axis_index("q"), lax.axis_index("c")
    share = chip % repeat
    flag_row = row == 1
    pos = jnp.stack([row, chip, core, lax.axis_index("b")]).astype(jnp.int32)

    mine = run_kernel(
        pack_heads,
        "pack_heads",
        (pos, query_weight, key_weight, value_weight, outgate_weight, beta_weight.T)
        + (mixer_gain[None, :], swiglu_gain[None, :], conv_weight),
        [((rows_w, 9 * HEAD), BF16)] * chips,
        [((4, rows_w, width), BF16), ((HEAD, HEAD), F32)],
        1,
        (0,),
        (1, 2, 3, 4),
    )
    head_s = [swap(mine[d], "q", d) for d in range(1, chips)]

    def own_slab(value):
        return jnp.where(flag_row, value[1], value[0])

    def away_slab(value):
        return jnp.where(flag_row, value[0], value[1])

    x_s = swap(away_slab(inputs[:, 0]), "m", 1)
    head_s, x_s = together(head_s, x_s)
    head_q = jnp.stack([mine[0]] + head_s, axis=0)
    x_own = jnp.stack([own_slab(inputs[:, 0]), x_s], axis=0)
    head_m = jnp.stack([head_q, swap(head_q, "m", 1)], axis=0)
    x_half = jnp.stack(from_chips(x_own), axis=0)
    out_s = swap(tie(output_weight, x_s), "m", 1)
    ids = own_slab(document_ids[:, 0])
    flags, id_rows, id_cols = token_flags(ids)
    gain_vec = head_gain.astype(F32)[None, :]
    pair = jnp.stack([gate_weight, up_weight], axis=1).reshape(
        rows_w, 2, micro, chips, 2 * n_batch * rows_f
    )
    pair = jnp.moveaxis(pair, 3, 0).reshape(chips, rows_w, 2 * ff_here)
    cot_away = away_slab(cotangent[:, 0])
    head_m, x_half, out_s, flags, id_rows, id_cols, gain_vec, pair, cot_away = together(
        head_m, x_half, out_s, flags, id_rows, id_cols, gain_vec, pair, cot_away
    )
    head_b = gather_batch(head_m.reshape(blocks_all, rows_w, 9 * HEAD), 1)
    x_sib = swap(x_half, "c", 1)
    cot_s = swap(cot_away, "m", 1)
    down_s = swap(tie(down_weight, x_half), "m", 1)
    out_b = gather_batch(jnp.stack([output_weight, out_s], axis=0), 1)
    pair_q = lax.all_to_all(pair, ("q",), 0, 0, tiled=True)
    head_b, x_sib, cot_s, down_s, out_b, pair_q = together(
        head_b, x_sib, cot_s, down_s, out_b, pair_q
    )
    send = lax.dynamic_slice_in_dim(head_b, (1 - core) * 4 * HEAD, 4 * HEAD, 2)
    head_sib = swap(jnp.concatenate([send, head_b[..., 8 * HEAD :]], axis=-1), "c", 1)
    pair_s = swap(pair_q, "m", 1)
    cot_own = jnp.stack([own_slab(cotangent[:, 0]), cot_s], axis=0)
    down_m, down_got = gather_batch_start(jnp.stack(ordered(row, down_weight, down_s), axis=0), 1)
    out_q = lax.all_to_all(
        jnp.broadcast_to(out_b, (chips,) + out_b.shape), ("q",), 0, 0, tiled=True
    )
    cot_got = [swap(cot_own, "q", d) for d in range(1, chips)]

    count = length // CHUNK
    run = partial(run_kernel, scale=max(1, length // 1024))

    def tall(n):
        return ((n, length, HEAD), F32)

    slabs = ((2, span, width), BF16)
    slabs_wide = ((2, span, width), F32)
    saved = [
        ((length, width), BF16),
        ((width, 5 * HEAD), BF16),
        ((length + 8, 3 * HEAD), F32),
        tall(7),
        tall(3),
        tall(3),
        tall(2),
    ]
    heads_here, taps, gains, normed, w_cat, p_pad, kept, slopes, found, shaped = run(
        mixer_forward,
        "mixer_forward",
        (pos, x_half, x_sib, head_b, head_sib, flags, id_cols, id_rows, gain_vec),
        [((chips, 2, length // 2, HEAD), BF16), ((16, HEAD), F32), ((8, width), F32)] + saved,
        [((HEAD, width), F32)] + saved + [tall(4)],
        25,
        (0,),
        (),
        tuple(range(3, 10)),
    )
    pair_s, down_got, out_q, cot_got = tie((pair_s, down_got, out_q, cot_got), heads_here)

    got_heads = lax.all_to_all(
        heads_here.reshape(chips * 2, length // 2, HEAD), ("q", "c"), 0, 0, tiled=True
    )
    pair_m = jnp.stack([pair_q, pair_s], axis=0).reshape(blocks_all, rows_w, 2 * ff_here)
    pair_b = gather_batch(pair_m, 1).reshape(micro, chips, rows_all, 2 * ff_here)
    cot_half = jnp.stack([cot_own] + cot_got, axis=0)
    down_b = gather_batch_end(down_m, down_got, 1)
    out_sib = swap(out_q, "c", 1)
    down_sib = swap(down_b, "c", 1)
    pair_sib = swap(pair_b, "c", 1)
    w_down = jnp.stack(ordered(core, down_b, down_sib), axis=1).reshape(ff_here, width)
    half = length // 2
    w_out, normed_two, pair_up, hidden, cot_rows, swiglu_part, res_own, norm_own, *norm_send = run(
        feed_forward,
        "feed_forward",
        (pos, got_heads, x_half, cot_half, out_q, out_sib, pair_b, pair_sib, w_down, gains),
        [
            ((width, width), BF16),
            ((half, width), BF16),
            ((half, 2 * ff_here), BF16),
            ((half, ff_here), BF16),
            ((half, width), BF16),
            ((8, width), F32),
            slabs_wide,
            slabs_wide,
        ]
        + [slabs] * (chips - 1),
        [
            ((width, 2 * ff_here), BF16),
            ((half, width), BF16),
            ((half, width), F32),
            ((half, width), F32),
            ((half, width), F32),
        ],
        12,
        (0,),
    )
    norm_got = [swap(v, "q", d + 1) for d, v in enumerate(norm_send)]
    pair_keep, pair_send, down_keep, down_send, out_part = run(
        feed_forward_grads,
        "feed_forward_grads",
        (pos, normed_two, pair_up, hidden, cot_rows, w_down),
        [
            ((blocks_all, rows_all, 2 * ff_here), BF16),
            ((blocks_all, rows_all, 2 * ff_here), BF16),
            ((micro, n_batch * rows_f, width), BF16),
            ((micro, n_batch * rows_f, width), BF16),
            ((chips, 2, span, width), BF16),
        ],
        [],
        6,
        (0,),
    )
    norm_got, norm_own, pair_send, down_send = together(norm_got, norm_own, pair_send, down_send)
    grad_resid, grad_branch, grad_heads = run(
        branch_gradient,
        "branch_gradient",
        (pos, norm_own, res_own, cot_own[None], gains, w_out, *norm_got),
        [slabs_wide, slabs, ((chips * 2, 2, span, HEAD), BF16)],
        [],
        2,
        (0,),
    )

    pair_got = swap(pair_send, "c", 1)
    down_got = swap(down_send, "c", 1)
    dheads = lax.all_to_all(grad_heads, ("q", "c"), 0, 0, tiled=True)
    grad_branch, pair_got, down_got = together(grad_branch, pair_got, down_got)
    pair_grad = (pair_keep.astype(F32) + pair_got.astype(F32)).astype(BF16)
    down_grad = (down_keep.astype(F32) + down_got.astype(F32)).astype(BF16)
    down_grad = down_grad.reshape(micro, n_batch, rows_f, width)
    dheads, pair_grad, down_grad, grad_branch, out_part = together(
        dheads, pair_grad, down_grad, grad_branch, out_part
    )
    out_got = lax.all_to_all(out_part, ("q",), 0, 0, tiled=True)
    branch_got = [swap(grad_branch, "q", d) for d in range(1, chips)]
    pair_grad = pair_grad.reshape(micro, chips, n_batch, rows_w, 2 * ff_here)
    pair_keep = lax.dynamic_index_in_dim(pair_grad, row, 0, keepdims=False)
    pair_got = swap(lax.dynamic_index_in_dim(pair_grad, 1 - row, 0, keepdims=False), "m", 1)
    down_grad = scatter_batch(down_grad, 1)

    def to_rows(value):
        keep = jnp.where(flag_row, value[1], value[0])
        send = jnp.where(flag_row, value[0], value[1])
        return jnp.stack(ordered(row, keep, swap(send, "m", 1)), axis=0)[:, None]

    blocks_out = ((blocks_all, span, width), BF16)
    weights_out = ((blocks_all, rows_all, 5 * HEAD), BF16)
    norm_keep, norm_send, w_keep, w_send = run(
        partial(mixer_backward, rows_w),
        "mixer_backward",
        (pos, dheads, flags, id_cols, id_rows, gain_vec, taps, swiglu_part)
        + (kept, shaped, found, slopes, p_pad, normed, w_cat),
        [blocks_out, blocks_out, weights_out, weights_out],
        [saved[i] for i in (3, 6, 5, 4, 2, 0, 1)]
        + [
            tall(3),
            ((length, HEAD), F32),
            ((length + 8, 3 * HEAD), F32),
            ((length, 5 * HEAD), BF16),
            ((16, HEAD), F32),
            ((8, HEAD), F32),
        ],
        25,
        (0,),
        tuple(range(8, 15)),
    )
    pair_got, down_grad, branch_got, out_got, w_send, norm_send = together(
        pair_got, down_grad, branch_got, out_got, w_send, norm_send
    )

    norm_got = swap(norm_send, "c", 1)
    w_got = swap(w_send, "c", 1)
    (out_rows,) = run(
        output_gradient,
        "output_gradient",
        (pos, got_heads, grad_branch, *branch_got),
        [((2, HEAD, width), BF16)],
        [((half, width), BF16), ((half, 2 * HEAD), BF16)],
        1,
        (0,),
    )
    w_got, out_rows = together(w_got, out_rows)
    piece = ((chips, rows_w, 9 * HEAD), BF16)
    if n_batch == 2:
        value = run(
            merge_heads, "merge_heads", (pos, w_keep, w_got), [piece] * 4, [], 1, (0,)
        )
    else:
        merged_all = ((blocks_all, rows_all, 9 * HEAD), BF16)
        (value,) = run(
            merge_heads, "merge_heads", (pos, w_keep, w_got), [merged_all], [], 1, (0,)
        )
        value = value.reshape(blocks_all, n_batch, rows_w, 9 * HEAD)
        value = scatter_batch(value, 1, 2).reshape(micro, chips, 2, rows_w, 9 * HEAD)
        batch = lax.axis_index("b") % 2
        value = [
            lax.dynamic_index_in_dim(
                lax.dynamic_index_in_dim(value, row ^ (i // 2), 0, keepdims=False),
                batch ^ (i % 2),
                1,
                keepdims=False,
            ).astype(BF16)
            for i in range(4)
        ]
    value, norm_got, out_rows, pair_got = together(value, norm_got, out_rows, pair_got)
    (norm_send,) = run(
        token_pieces,
        "token_pieces",
        (norm_keep, norm_got),
        [((chips, 2, span, width), BF16)],
        [],
        1,
    )
    step = repeat // 2
    while step >= 1:
        out_rows = out_rows.reshape(micro, 2, out_rows.shape[1] // 2, width)
        out_rows = scatter_bit(out_rows, 1, (share // step) % 2, "q", step)
        step //= 2
    out_rows = out_rows.reshape(micro, 2, n_batch, rows_w, width)
    norm_got = lax.all_to_all(norm_send, ("q",), 0, 0, tiled=True)
    value_got = [
        swap(value[1], "b", 1),
        swap(value[2], "m", 1),
        swap(value[3], ("m", "b"), n_batch + 1),
    ]
    pair_rows = (pair_keep.astype(F32) + pair_got.astype(F32)).astype(BF16)
    pair_rows = scatter_batch(pair_rows, 1)
    out_rows = scatter_bit(out_rows, 1, core, "c", 1)
    norm_got, pair_rows, out_rows = together(norm_got, pair_rows, out_rows)
    pair_got = lax.all_to_all(pair_rows.astype(BF16), ("q",), 0, 0, tiled=True)
    out_rows = scatter_batch(out_rows, 1)
    (grad_own,) = run(
        input_gradient,
        "input_gradient",
        (pos, grad_resid, x_own, gains, norm_got),
        [slabs],
        [],
        1,
        (0,),
    )
    grad_final = to_rows(grad_own)
    value_got, out_rows, down_grad, out_got = together(value_got, out_rows, down_grad, out_got)
    head_got = run(
        add_partners,
        "add_partners",
        (pos, value[0], *value_got),
        [((rows_w, 9 * HEAD), BF16)] * chips,
        [],
        1,
        (0,),
    )
    head_got = [head_got[0]] + [swap(head_got[d], "q", d) for d in range(1, chips)]
    outproj_grad = scatter_bit(out_rows, 0, row, "m", 1)
    down_grad = scatter_bit(down_grad, 0, row, "m", 1)
    out_all = (res_own + jnp.sum(out_got.astype(F32), axis=0)).astype(BF16)
    out_final = to_rows(out_all)
    gate_grad, up_grad = run(
        spread_pair,
        "spread_pair",
        (pair_got,),
        [(gate_weight.shape[:1] + (chips * ff_here,), F32)] * 2,
        [],
        2,
    )
    *merged, beta_sum, gain_sums, tap_sums, head_sum = run(
        spread_heads,
        "spread_heads",
        (pos, *head_got),
        [((rows_w, width), F32)] * 4
        + [((HEADS, rows_w), F32), ((8, rows_w), F32), ((3 * CONV, rows_w), F32), ((1, HEAD), F32)],
        [((HEAD, HEAD), F32)],
        1,
        (0,),
    )
    return (
        out_final,
        grad_final,
        merged[0],
        merged[1],
        merged[2],
        beta_sum.T,
        merged[3],
        outproj_grad,
        gate_grad,
        up_grad,
        down_grad,
        gain_sums[0],
        gain_sums[1],
        head_sum[0],
        tap_sums,
    )


def solution(mesh):
    n_seq, n_batch = mesh.shape["seq"], mesh.shape["batch"]

    def program(*arrays):
        micro = arrays[0].shape[0]
        shape = (micro, n_seq // (2 * micro), 2, n_batch)
        fine = Mesh(mesh.devices.reshape(shape), ("m", "q", "c", "b"))
        seq, every = ("m", "q", "c"), ("m", "q", "c", "b")
        tokens, rows, vector, taps = P(None, "b", seq, None), P(every, None), P(every), P(None, every)
        return jax.shard_map(
            on_device,
            mesh=fine,
            in_specs=(tokens, tokens, P(None, "b", None))
            + (rows,) * 9
            + (vector, vector, P(), taps),
            out_specs=(tokens, tokens) + (rows,) * 9 + (vector, vector, P(), taps),
            check_vma=False,
        )(*arrays)

    return program
```
